128 devices in a mesh: fsdp: 8 (over x, core), context: 4 (over z), tensor: 4 (over y).
Axes of the slice: x: 4, y: 4, z: 4, core: 2. Of those that a mesh axis runs over, the one named last changes fastest.
Arguments:
- tokens: bfloat16 [32, 1024, 1536], P('fsdp', 'context'), may hold values from -6 to 6
- output_cotangent: bfloat16 [32, 1024, 1536], P('fsdp', 'context'), may hold values from -6 to 6
- segments: int32 [32, 1024], P('fsdp', 'context'), may hold values from 0 to 3, never falling along the last dimension, each value on 1 to 512 neighbouring positions
- sequence_adapter: int32 [32], P('fsdp'), may hold values from 0 to 7
- input_norm_gain: float32 [1536], replicated, may hold values from 0.1 to 1.9
- gate_x_projection_weight: bfloat16 [1536, 2, 3072], P(('fsdp', 'context'), None, 'tensor'), may hold values from -0.15625 to 0.15625
- bc_projection_weight: bfloat16 [1536, 256], P(('fsdp', 'context')), may hold values from -0.15625 to 0.15625
- step_projection_weight: bfloat16 [1536, 48], P(('fsdp', 'context'), 'tensor'), may hold values from -0.15625 to 0.15625
- x_convolution_taps: float32 [4, 3072], P(None, 'tensor'), may hold values from -3 to 3
- x_convolution_bias: float32 [3072], P('tensor'), may hold values from -3 to 3
- bc_convolution_taps: float32 [4, 256], replicated, may hold values from -3 to 3
- bc_convolution_bias: float32 [256], replicated, may hold values from -3 to 3
- step_size_bias: float32 [48], P('tensor'), may hold values from -4.6 to -2.2
- log_decay_rate: float32 [48], P('tensor'), may hold values from -3 to 0.7
- head_skip_gain: float32 [48], P('tensor'), may hold values from 0.5 to 1.5
- gated_norm_gain: float32 [3072], P('tensor'), may hold values from 0.1 to 1.9
- output_projection_weight: bfloat16 [3072, 1536], P('tensor', ('fsdp', 'context')), may hold values from -0.109375 to 0.109375
- in_adapter_down: bfloat16 [8, 1536, 16], replicated, may hold values from -0.15625 to 0.15625
- in_adapter_up: bfloat16 [8, 16, 2, 3072], P(None, None, None, 'tensor'), may hold values from -0.75 to 0.75
- out_adapter_down: bfloat16 [8, 3072, 16], P(None, 'tensor'), may hold values from -0.109375 to 0.109375
- out_adapter_up: bfloat16 [8, 16, 1536], replicated, may hold values from -0.75 to 0.75
Outputs:
- layer_out: bfloat16 [32, 1024, 1536], P('fsdp', 'context')
- grad_tokens: float32 [32, 1024, 1536], P('fsdp', 'context')
- grad_lora_in_a: float32 [8, 1536, 16], replicated
- grad_lora_in_b: float32 [8, 16, 2, 3072], P(None, None, None, 'tensor')
- grad_lora_out_a: float32 [8, 3072, 16], P(None, 'tensor')
- grad_lora_out_b: float32 [8, 16, 1536], replicated
The draws below stay inside these ranges and needn't reach their ends.
Inputs may be any that keep to these rules, and one draw needn't show every extreme that they name: `segments`: segment numbers never fall along a sequence, every one of 0 .. 3 occurs in each sequence, and one document has exactly 512 tokens.
All inputs are finite; a program needn't handle non-finite values.
Results may differ from the reference program's by a relative error of at most 0.0089.
Values may be sent and summed in bfloat16 or wider, within the bound.
No kernel may reach another device: no remote copies, remote signals or barrier semaphores. Data moves between devices by JAX's collectives and lax.ppermute only.
A program may use at most 192 MiB of HBM per device.

```python
import math
import jax
import jax.numpy as jnp
import numpy as np
from jax import lax

MODEL_WIDTH = 1536
INNER_CHANNELS = 3072
HEAD_DIM = 64
STATE = 128
CONV = 4
ADAPTER_RANK = 16
ADAPTER_COUNT = 8
SEGS = 4
BLOCK = 256
HEADS = 48
LEN = 1024
SEQS = 32


def touch_ends(values, rng, low, largest):
    place = [jax.random.randint(jax.random.fold_in(rng, axis), (), 0, length) for axis, length in enumerate(values.shape)]
    longest = values.shape.index(max(values.shape))
    neighbour = place[:longest] + [(place[longest] + 1) % values.shape[longest]] + place[longest + 1:]
    return values.at[tuple(place)].set(low).at[tuple(neighbour)].set(largest)


def block_levels(key, dims, split, least, high):
    loudness, own = 1.0, jax.random.fold_in(key, 6)
    for position, shards_of in split:
        steps = jnp.exp(jax.random.uniform(jax.random.fold_in(own, position), (shards_of,), jnp.float32, least / len(split), high / len(split)))
        loudness = loudness * jnp.repeat(steps, dims[position] // shards_of).reshape([-1 if axis == position else 1 for axis in range(len(dims))])
    return loudness


def profile(count, total, bound, slope):
    weights = [(1 << 20) // math.isqrt(grade ** slope) + 1 for grade in range(2, count + 1)]
    rest, holding = total - bound - (count - 1), [1] * (count - 1)
    while rest > 0:
        candidates = [i for i in range(count - 1) if holding[i] < bound]
        mass, budget = sum([weights[i] for i in candidates]), rest
        for i in candidates:
            addition = min(bound - holding[i], max(1, budget * weights[i] // mass), rest)
            holding[i] = holding[i] + addition
            rest = rest - addition
    return np.array([bound] + holding)


def uneven_parts(rng, number_of, total, bound, skew):
    if number_of == 2:
        one = jax.random.randint(rng, (), max(1, total - bound), min(bound, total - 1) + 1)
        return jnp.stack([one, total - one])
    sizes = jnp.asarray(profile(number_of, total, bound, skew), jnp.int32)
    twos = (number_of - 1) // 2
    donor, taker = sizes[1:1 + 2 * twos:2], sizes[2:2 + 2 * twos:2]
    margin = jnp.minimum(donor - 1, bound - taker)
    moved = jax.random.randint(jax.random.fold_in(rng, 1), (twos,), 0, 1 << 20) % (margin + 1)
    sizes = sizes.at[1:1 + 2 * twos:2].set(donor - moved).at[2:2 + 2 * twos:2].set(taker + moved)
    return sizes[jax.random.permutation(jax.random.fold_in(rng, 2), number_of)]


def bell_draw(stream_key, shape, scale, bound, shards=(), kind=jnp.bfloat16):
    gain = block_levels(stream_key, shape, shards, -0.22, 0.18) if shards else 1.0
    values = jax.random.normal(stream_key, shape, jnp.float32) * scale * gain
    return jnp.minimum(jnp.maximum(values, -bound), bound).astype(kind)


def setup_inputs(seed: int = 0) -> dict:
    key_of = jax.random.split(jax.random.key(seed), 22)
    return {
        "tokens": bell_draw(key_of[0], (SEQS, LEN, MODEL_WIDTH), 1.0, 6.0, ((0, 8), (1, 4))),
        "output_cotangent": bell_draw(key_of[1], (SEQS, LEN, MODEL_WIDTH), 1.0, 6.0, ((0, 8), (1, 4))),
        "segments": jax.vmap(lambda own: jnp.searchsorted(jnp.cumsum(uneven_parts(own, SEGS, LEN, LEN // 2, 0)), jnp.arange(LEN), side="right"))(jax.random.split(key_of[2], SEQS)).reshape((SEQS, LEN)).astype(jnp.int32),
        "sequence_adapter": touch_ends(jax.random.randint(key_of[3], (SEQS,), 0, ADAPTER_COUNT), jax.random.fold_in(key_of[3], 1), 0, ADAPTER_COUNT - 1).astype(jnp.int32),
        "input_norm_gain": jnp.clip(1.0 + 0.18 * jax.random.normal(key_of[4], (MODEL_WIDTH,), jnp.float32), 0.1, 1.9),
        "gate_x_projection_weight": bell_draw(key_of[5], (MODEL_WIDTH, 2, INNER_CHANNELS), MODEL_WIDTH ** -0.5, 0.15625, ((0, 32), (2, 4))),
        "bc_projection_weight": bell_draw(key_of[6], (MODEL_WIDTH, 2 * STATE), MODEL_WIDTH ** -0.5, 0.15625, ((0, 32),)),
        "step_projection_weight": bell_draw(key_of[7], (MODEL_WIDTH, HEADS), MODEL_WIDTH ** -0.5, 0.15625, ((0, 32), (1, 4))),
        "x_convolution_taps": bell_draw(key_of[8], (CONV, INNER_CHANNELS), CONV ** -0.5, 3.0, ((1, 4),), jnp.float32),
        "x_convolution_bias": bell_draw(key_of[9], (INNER_CHANNELS,), 0.5, 3.0, ((0, 4),), jnp.float32),
        "bc_convolution_taps": bell_draw(key_of[10], (CONV, 2 * STATE), CONV ** -0.5, 3.0, (), jnp.float32),
        "bc_convolution_bias": bell_draw(key_of[11], (2 * STATE,), 0.5, 3.0, (), jnp.float32),
        "step_size_bias": jnp.clip(-4.6 + 2.3999999 * jax.random.uniform(key_of[12], (HEADS,), jnp.float32) ** block_levels(key_of[12], (HEADS,), ((0, 4),), -0.2, 0.2), -4.6, -2.2),
        "log_decay_rate": jnp.clip(-3.0 + 3.7 * jax.random.uniform(key_of[13], (HEADS,), jnp.float32) ** block_levels(key_of[13], (HEADS,), ((0, 4),), -0.2, 0.2), -3.0, 0.7),
        "head_skip_gain": jnp.clip(0.5 + 1.0 * jax.random.uniform(key_of[14], (HEADS,), jnp.float32) ** block_levels(key_of[14], (HEADS,), ((0, 4),), -0.2, 0.2), 0.5, 1.5),
        "gated_norm_gain": jnp.clip(1.0 + 0.18 * jax.random.normal(key_of[15], (INNER_CHANNELS,), jnp.float32), 0.1, 1.9),
        "output_projection_weight": bell_draw(key_of[16], (INNER_CHANNELS, MODEL_WIDTH), INNER_CHANNELS ** -0.5, 0.109375, ((0, 4), (1, 32))),
        "in_adapter_down": bell_draw(key_of[17], (ADAPTER_COUNT, MODEL_WIDTH, ADAPTER_RANK), MODEL_WIDTH ** -0.5, 0.15625),
        "in_adapter_up": bell_draw(key_of[18], (ADAPTER_COUNT, ADAPTER_RANK, 2, INNER_CHANNELS), (4 * ADAPTER_RANK) ** -0.5, 0.75, ((3, 4),)),
        "out_adapter_down": bell_draw(key_of[19], (ADAPTER_COUNT, INNER_CHANNELS, ADAPTER_RANK), INNER_CHANNELS ** -0.5, 0.109375, ((1, 4),)),
        "out_adapter_up": bell_draw(key_of[20], (ADAPTER_COUNT, ADAPTER_RANK, MODEL_WIDTH), (4 * ADAPTER_RANK) ** -0.5, 0.75),
    }


EPS_NORM = 1e-05

@jax.custom_vjp
def low(v):
    return lax.optimization_barrier(v.astype(jnp.bfloat16)).astype(jnp.float32)

@jax.custom_vjp
def low_back(v):
    return v

def low_keep(v):
    return (low(v), None)

def low_pass(kept, grad):
    return (grad,)

def back_keep(v):
    return (v, None)

def back_low(kept, grad):
    return (low(grad),)
low.defvjp(low_keep, low_pass)
low_back.defvjp(back_keep, back_low)

def conv_silu(padded, padded_seg, seg_ids, tap_weight, tap_bias):
    length = seg_ids.shape[-1]
    running_sum = tap_bias
    for offset in range(tap_weight.shape[0]):
        agrees = (padded_seg[..., offset:offset + length] == seg_ids).astype(jnp.float32)
        running_sum = running_sum + tap_weight[offset] * padded[..., offset:offset + length, :] * agrees[..., None]
    return jax.nn.silu(running_sum)

def ssd_parts(x_heads, b_values, c_values, raw_dt, step_size_bias, decay_rates, skip_gain, seg_ids, seg_before):
    highest = lax.Precision.HIGHEST
    step_dt = jax.nn.softplus(raw_dt + step_size_bias)
    running = jnp.cumsum(step_dt * decay_rates, axis=1)
    run_heads = jnp.swapaxes(running, 1, 2)
    length = seg_ids.shape[1]
    causal = jnp.arange(length)[:, None] >= jnp.arange(length)[None, :]
    allowed = (causal[None] & (seg_ids[:, :, None] == seg_ids[:, None, :]))[:, None]
    spread = run_heads[:, :, :, None] - run_heads[:, :, None, :]
    decay_mask = jnp.where(allowed, jnp.exp(jnp.where(allowed, spread, 0.0)), 0.0)
    intersection = jnp.einsum('stn,sun->stu', c_values, b_values, precision=highest)
    weights = decay_mask * intersection[:, None] * jnp.swapaxes(step_dt, 1, 2)[:, :, None, :]
    outputs = jnp.einsum('shtu,suhp->sthp', weights, x_heads, precision=highest)
    outputs = outputs + skip_gain[:, None] * x_heads
    linked = (seg_ids == seg_before[:, None]).astype(jnp.float32)
    reach_in = jnp.exp(running) * linked[:, :, None]
    final_log = running[:, -1, :]
    ending = (seg_ids == seg_ids[:, -1:]).astype(jnp.float32)
    toward = jnp.exp(final_log[:, None, :] - running) * ending[:, :, None] * step_dt
    local_state = jnp.einsum('sth,stn,sthp->shpn', toward, b_values, x_heads, precision=highest)
    passing = jnp.exp(final_log) * (seg_ids[:, -1] == seg_before).astype(jnp.float32)[:, None]
    return (outputs, local_state, passing, reach_in)

def carried_term(reach_in, c_values, carried):
    return reach_in[..., None] * jnp.einsum('stn,shpn->sthp', c_values, carried, precision=lax.Precision.HIGHEST)

def layer_one(seq_tokens, seq_ids, one_pick, in_down, in_up, out_down, out_up, frozen):
    input_norm_gain, gate_x_projection_weight, bc_projection_weight, step_projection_weight, tap_weight, tap_bias, step_size_bias, log_decay_rate, head_skip_gain, gated_norm_gain, output_projection_weight = frozen
    highest = lax.Precision.HIGHEST
    scale_in = lax.rsqrt(lax.optimization_barrier(jnp.mean(seq_tokens * seq_tokens, -1, keepdims=True)) + EPS_NORM)
    normed = low(seq_tokens * scale_in * input_norm_gain)
    down_in = jnp.einsum('a,adr->dr', one_pick, in_down, precision=highest)
    up_in = jnp.einsum('a,arkc->rkc', one_pick, in_up, precision=highest)
    down_out = jnp.einsum('a,acr->cr', one_pick, out_down, precision=highest)
    up_out = jnp.einsum('a,ard->rd', one_pick, out_up, precision=highest)
    low_rank = low(low_back(jnp.dot(normed, down_in, precision=highest)))
    gate_x = low(low_back(jnp.einsum('td,dkc->tkc', normed, gate_x_projection_weight, precision=highest) + jnp.einsum('tr,rkc->tkc', low_rank, up_in, precision=highest)))
    bc_proj = low(low_back(jnp.dot(normed, bc_projection_weight, precision=highest)))
    raw_dt = low(low_back(jnp.dot(normed, step_projection_weight, precision=highest)))
    conv_in = jnp.concatenate([gate_x[:, 1], bc_proj], -1)
    tap_count = tap_weight.shape[0]
    padded = jnp.concatenate([jnp.zeros((tap_count - 1, conv_in.shape[1]), jnp.float32), conv_in], 0)
    padded_seg = jnp.concatenate([jnp.full((tap_count - 1,), -1, jnp.int32), seq_ids], 0)
    conv_out = conv_silu(padded, padded_seg, seq_ids, tap_weight, tap_bias)
    x_conv = low(conv_out[:, :INNER_CHANNELS])
    b_conv = low(conv_out[:, INNER_CHANNELS:INNER_CHANNELS + STATE])
    c_conv = low(conv_out[:, INNER_CHANNELS + STATE:])
    blocks = LEN // BLOCK
    decay_rates = -jnp.exp(log_decay_rate)

    def advance(carry, block_piece):
        carried, seg_before = carry
        x_blk, b_blk, c_blk, dt_blk, seg_blk = block_piece
        outputs, local_state, passing, reach_in = ssd_parts(x_blk[None], b_blk[None], c_blk[None], dt_blk[None], step_size_bias, decay_rates, head_skip_gain, seg_blk[None], seg_before[None])
        outputs = outputs + carried_term(reach_in, c_blk[None], carried[None])
        carried = passing[0][:, None, None] * carried + local_state[0]
        return ((carried, seg_blk[-1]), outputs[0])
    start_carry = (jnp.zeros((HEADS, HEAD_DIM, STATE), jnp.float32), jnp.array(-1, jnp.int32))
    pieces = (x_conv.reshape(blocks, BLOCK, HEADS, HEAD_DIM), b_conv.reshape(blocks, BLOCK, STATE), c_conv.reshape(blocks, BLOCK, STATE), raw_dt.reshape(blocks, BLOCK, HEADS), seq_ids.reshape(blocks, BLOCK))
    unused, ssd_out = lax.scan(jax.checkpoint(advance), start_carry, pieces)
    ssd_out = ssd_out.reshape(LEN, INNER_CHANNELS)
    gated_mix = ssd_out * jax.nn.silu(gate_x[:, 0])
    scale_gate = lax.rsqrt(lax.optimization_barrier(jnp.mean(gated_mix * gated_mix, -1, keepdims=True)) + EPS_NORM)
    gate_normed = low(gated_mix * scale_gate * gated_norm_gain)
    low_out = low(low_back(jnp.dot(gate_normed, down_out, precision=highest)))
    branch = jnp.dot(gate_normed, output_projection_weight, precision=highest) + jnp.dot(low_out, up_out, precision=highest)
    return seq_tokens + branch

def reference(tokens, output_cotangent, segments, sequence_adapter, input_norm_gain, gate_x_projection_weight, bc_projection_weight, step_projection_weight, x_convolution_taps, x_convolution_bias, bc_convolution_taps, bc_convolution_bias, step_size_bias, log_decay_rate, head_skip_gain, gated_norm_gain, output_projection_weight, in_adapter_down, in_adapter_up, out_adapter_down, out_adapter_up):
    frozen = (input_norm_gain, gate_x_projection_weight.astype(jnp.float32), bc_projection_weight.astype(jnp.float32), step_projection_weight.astype(jnp.float32), jnp.concatenate([x_convolution_taps, bc_convolution_taps], 1), jnp.concatenate([x_convolution_bias, bc_convolution_bias], 0), step_size_bias, log_decay_rate, head_skip_gain, gated_norm_gain, output_projection_weight.astype(jnp.float32))
    adapter_tables = (in_adapter_down.astype(jnp.float32), in_adapter_up.astype(jnp.float32), out_adapter_down.astype(jnp.float32), out_adapter_up.astype(jnp.float32))
    group_size = math.gcd(SEQS, max(1, 4096 // LEN))
    count_groups = SEQS // group_size
    adapter_select = (sequence_adapter[:, None] == jnp.arange(ADAPTER_COUNT, dtype=jnp.int32)[None, :]).astype(jnp.float32)

    def per_group(totals, group_piece):
        group_tokens, group_cot, group_ids, group_pick = group_piece

        def forward(tok_in, in_down, in_up, out_down, out_up):
            return jax.vmap(lambda one_tokens, one_ids, one_pick: layer_one(one_tokens, one_ids, one_pick, in_down, in_up, out_down, out_up, frozen))(tok_in, group_ids, group_pick)
        result, pullback = jax.vjp(forward, group_tokens, *adapter_tables)
        grad_list = pullback(group_cot)
        totals = tuple((earlier_sum + new_grad for earlier_sum, new_grad in zip(totals, grad_list[1:])))
        return (totals, (result.astype(jnp.bfloat16), grad_list[0]))
    pieces = (tokens.astype(jnp.float32).reshape(count_groups, group_size, LEN, MODEL_WIDTH), output_cotangent.astype(jnp.float32).reshape(count_groups, group_size, LEN, MODEL_WIDTH), segments.reshape(count_groups, group_size, LEN), adapter_select.reshape(count_groups, group_size, ADAPTER_COUNT))
    start_totals = tuple((jnp.zeros_like(table) for table in adapter_tables))
    totals, (outputs, grads_in) = lax.scan(per_group, start_totals, pieces)
    return (outputs.reshape(SEQS, LEN, MODEL_WIDTH), grads_in.reshape(SEQS, LEN, MODEL_WIDTH), totals[0], totals[1], totals[2], totals[3])
```

```python
import functools

import jax
import jax.numpy as jnp
from jax import lax
from jax.experimental import pallas as pl
from jax.experimental.pallas import tpu as pltpu
from jax.sharding import PartitionSpec as P

INNER_CHANNELS = 3072
EPS_NORM = 1e-05
SUB = 128
NEG = -1e30
BF = jnp.bfloat16
F32 = jnp.float32
HIGHEST = lax.Precision.HIGHEST


def dot_nn(a, b):
    return lax.dot_general(a, b, (((1,), (0,)), ((), ())), preferred_element_type=F32)


def dot_nt(a, b):
    return lax.dot_general(a, b, (((1,), (1,)), ((), ())), preferred_element_type=F32)


def dot_tn(a, b):
    return lax.dot_general(a, b, (((0,), (0,)), ((), ())), preferred_element_type=F32)


def softplus(v):
    return jnp.maximum(v, 0.0) + jnp.log1p(jnp.exp(-jnp.abs(v)))


def lane(shape, dim):
    return lax.broadcasted_iota(jnp.int32, shape, dim)


def wide(column):
    return jnp.broadcast_to(column, (SUB, SUB))


def decays(raw, par_ref):
    rate = par_ref[1:2, :]
    shifted = raw + par_ref[0:1, :]
    dt = softplus(shifted)
    lower = (lane((SUB, SUB), 0) >= lane((SUB, SUB), 1)).astype(F32)
    run = jnp.dot(lower, dt * rate, precision=HIGHEST, preferred_element_type=F32)
    return shifted, dt, rate, run


def scan_forward(
    z_ref, x_ref, bcdt_ref, marks_ref, taps_ref, bias_ref, par_ref, skip_ref, gain_ref,
    y_ref, xc_ref, bc_ref, slope_ref, g2_ref, states_ref, square_ref,
    state, ext,
):
    step = pl.program_id(0)
    inner = z_ref.shape[1]
    chans = ext.shape[1]

    @pl.when(step == 0)
    def _():
        state[...] = jnp.zeros_like(state)
        ext[0:8, :] = jnp.zeros((8, chans), F32)

    @pl.when(step > 0)
    def _():
        ext[0:8, :] = ext[SUB : SUB + 8, :]

    ext[8 : SUB + 8, 0:inner] = x_ref[...].astype(F32)
    ext[8 : SUB + 8, inner:chans] = bcdt_ref[:, 0 : 2 * SUB].astype(F32)
    near = [wide(marks_ref[:, k : k + 1]) for k in range(3)]
    linked = wide(marks_ref[:, 3:4])
    ending = wide(marks_ref[:, 4:5])
    ids = wide(marks_ref[:, 5:6])
    passing = marks_ref[0:1, 6:7]
    left = lane((SUB, SUB), 1) < 64

    def conv(sl):
        pre = bias_ref[:, sl] + taps_ref[3:4, sl] * ext[8 : SUB + 8, sl]
        for k in range(1, 4):
            pre = pre + taps_ref[3 - k : 4 - k, sl] * (ext[8 - k : SUB + 8 - k, sl] * near[k - 1])
        sig = jax.nn.sigmoid(pre)
        out = (pre * sig).astype(BF)
        slope_ref[:, sl] = (sig * (1.0 + pre * (1.0 - sig))).astype(BF)
        return out

    b_low = conv(slice(inner, inner + SUB))
    c_low = conv(slice(inner + SUB, inner + 2 * SUB))
    bc_ref[:, 0:SUB] = b_low
    bc_ref[:, SUB : 2 * SUB] = c_low
    b_turned = b_low.astype(F32).T.astype(BF)
    _, dt, _, run = decays(bcdt_ref[:, 2 * SUB : 3 * SUB].astype(F32), par_ref)
    run_rows = run.T
    allowed = (ids == ids.T) & (lane((SUB, SUB), 0) >= lane((SUB, SUB), 1))
    mask = jnp.where(allowed, 0.0, NEG)
    cross = dot_nt(c_low, b_low)
    square = jnp.zeros((SUB, SUB), F32)
    for p in range(inner // SUB):
        sl = slice(p * SUB, (p + 1) * SUB)
        x_low = conv(sl)
        xc_ref[:, sl] = x_low
        x = x_low.astype(F32)
        run0, run1 = wide(run[:, 2 * p : 2 * p + 1]), wide(run[:, 2 * p + 1 : 2 * p + 2])
        run_p = jnp.where(left, run0, run1)
        dt_p = jnp.where(left, wide(dt[:, 2 * p : 2 * p + 1]), wide(dt[:, 2 * p + 1 : 2 * p + 2]))
        m0 = (jnp.exp(run0 - run_rows[2 * p : 2 * p + 1, :] + mask) * cross).astype(BF)
        m1 = (jnp.exp(run1 - run_rows[2 * p + 1 : 2 * p + 2, :] + mask) * cross).astype(BF)
        xdt = x * dt_p
        split = jnp.concatenate([jnp.where(left, xdt, 0.0), jnp.where(left, 0.0, xdt)], 0).astype(BF)
        before = state[:, sl]
        before_low = before.astype(BF)
        states_ref[0, :, sl] = before_low
        y = dot_nn(jnp.concatenate([m0, m1], 1), split)
        y = y + jnp.exp(run_p) * linked * dot_nn(c_low, before_low) + skip_ref[:, sl] * x
        last = run_p[SUB - 1 : SUB, :]
        toward = (xdt * (jnp.exp(last - run_p) * ending)).astype(BF)
        state[:, sl] = (jnp.exp(last) * passing) * before + dot_nn(b_turned, toward)
        z = z_ref[:, sl].astype(F32)
        gated = y * (z * jax.nn.sigmoid(z))
        y_ref[:, sl] = y.astype(BF)
        g2_ref[:, sl] = (gated * gain_ref[:, sl]).astype(BF)
        square = square + gated * gated
    square_ref[...] = square


def scan_backward(
    z_ref, dt_ref, xc_ref, bc_ref, slope_ref, y_ref, dn_ref, states_ref, scale_ref, marks_ref,
    taps_ref, par_ref, skip_ref, gain_ref, pick_ref,
    da_ref,
    lam, ext, to_dt, to_run, to_end,
):
    step = pl.program_id(0)
    inner = z_ref.shape[1]
    chans = ext.shape[1]

    @pl.when(step == 0)
    def _():
        lam[...] = jnp.zeros_like(lam)
        ext[SUB : SUB + 8, :] = jnp.zeros((8, chans), F32)

    @pl.when(step > 0)
    def _():
        ext[SUB : SUB + 8, :] = ext[0:8, :]

    linked = wide(marks_ref[:, 3:4])
    ending = wide(marks_ref[:, 4:5])
    ids = wide(marks_ref[:, 5:6])
    passing = marks_ref[0:1, 6:7]
    later = [wide(marks_ref[:, 7 + k : 8 + k]) for k in range(3)]
    left = lane((SUB, SUB), 1) < 64
    rn = jnp.broadcast_to(scale_ref[0:1, :], (SUB, SUB)).T
    kappa = jnp.broadcast_to(scale_ref[1:2, :], (SUB, SUB)).T
    shifted, dt, rate, run = decays(dt_ref[...].astype(F32), par_ref)
    run_rows = run.T
    b_low, c_low = bc_ref[:, 0:SUB], bc_ref[:, SUB : 2 * SUB]
    c_turned = c_low.astype(F32).T.astype(BF)
    allowed = (ids == ids.T) & (lane((SUB, SUB), 0) <= lane((SUB, SUB), 1))
    mask = jnp.where(allowed, 0.0, NEG)
    cross = dot_nt(b_low, c_low)
    d_cross = jnp.zeros((SUB, SUB), F32)
    d_b = jnp.zeros((SUB, SUB), F32)
    d_c = jnp.zeros((SUB, SUB), F32)
    for p in range(inner // SUB):
        sl = slice(p * SUB, (p + 1) * SUB)
        z = z_ref[:, sl].astype(F32)
        sig = jax.nn.sigmoid(z)
        silu = z * sig
        y = y_ref[:, sl].astype(F32)
        d_gated = rn * (dn_ref[:, sl].astype(F32) * gain_ref[:, sl]) - kappa * (y * silu)
        da_ref[:, sl] = (d_gated * y * sig * (1.0 + z * (1.0 - sig))).astype(BF)
        dy = d_gated * silu
        x = xc_ref[:, sl].astype(F32)
        run0, run1 = wide(run[:, 2 * p : 2 * p + 1]), wide(run[:, 2 * p + 1 : 2 * p + 2])
        run_p = jnp.where(left, run0, run1)
        dt_p = jnp.where(left, wide(dt[:, 2 * p : 2 * p + 1]), wide(dt[:, 2 * p + 1 : 2 * p + 2]))
        l0 = jnp.exp(run_rows[2 * p : 2 * p + 1, :] - run0 + mask)
        l1 = jnp.exp(run_rows[2 * p + 1 : 2 * p + 2, :] - run1 + mask)
        xdt = x * dt_p
        x_split = jnp.concatenate([jnp.where(left, xdt, 0.0), jnp.where(left, 0.0, xdt)], 0).astype(BF)
        dy_split = jnp.concatenate([jnp.where(left, dy, 0.0), jnp.where(left, 0.0, dy)], 0).astype(BF)
        d_m = dot_nt(x_split, dy.astype(BF))
        d_cross = d_cross + l0 * d_m[0:SUB] + l1 * d_m[SUB : 2 * SUB]
        m = jnp.concatenate([l0 * cross, l1 * cross], 1).astype(BF)
        lam_p = lam[:, sl]
        lam_low = lam_p.astype(BF)
        last = run_p[SUB - 1 : SUB, :]
        toward = jnp.exp(last - run_p) * ending
        carried = toward * dot_nn(b_low, lam_low)
        d_xt = dot_nn(m, dy_split) + carried
        skip = skip_ref[:, sl]
        ext[0:SUB, sl] = (dt_p * d_xt + skip * dy) * slope_ref[:, sl].astype(F32)
        x_dx = x * d_xt
        to_dt[:, sl] = x_dx
        to_run[:, sl] = dy * (y - skip * x) - dt_p * x_dx
        reached = (jnp.exp(run_p) * linked * dy).astype(BF)
        before_low = states_ref[0, :, sl]
        keep = jnp.exp(last) * passing
        to_end[0:1, sl] = jnp.sum(xdt * carried, 0, keepdims=True) + keep * jnp.sum(
            lam_p * before_low.astype(F32), 0, keepdims=True
        )
        d_b = d_b + dot_nt((xdt * toward).astype(BF), lam_low)
        d_c = d_c + dot_nt(reached, before_low)
        lam[:, sl] = keep * lam_p + dot_nn(c_turned, reached)
    d_cross_low = d_cross.astype(BF)
    d_b = d_b + dot_nn(d_cross_low, c_low)
    d_c = d_c + dot_nn(d_cross.T.astype(BF), b_low)
    ext[0:SUB, inner : inner + SUB] = d_b * slope_ref[:, inner : inner + SUB].astype(F32)
    ext[0:SUB, inner + SUB : chans] = d_c * slope_ref[:, inner + SUB : chans].astype(F32)

    def by_head(v):
        high = v.astype(BF)
        return dot_nn(high, pick_ref[...]) + dot_nn((v - high.astype(F32)).astype(BF), pick_ref[...])

    d_run = by_head(to_run[...])
    d_end = by_head(to_end[...])[0:1, :]
    d_run = d_run + jnp.where(lane((SUB, SUB), 0) == SUB - 1, d_end, 0.0)
    upper = (lane((SUB, SUB), 0) <= lane((SUB, SUB), 1)).astype(F32)
    d_log = jnp.dot(upper, d_run, precision=HIGHEST, preferred_element_type=F32)
    d_dt = by_head(to_dt[...]) + rate * d_log
    da_ref[:, inner + chans : inner + chans + SUB] = (d_dt * jax.nn.sigmoid(shifted)).astype(BF)
    for s in range(chans // SUB):
        sl = slice(s * SUB, (s + 1) * SUB)
        acc = taps_ref[3:4, sl] * ext[0:SUB, sl]
        for k in range(1, 4):
            acc = acc + taps_ref[3 - k : 4 - k, sl] * (ext[k : SUB + k, sl] * later[k - 1])
        da_ref[:, inner + s * SUB : inner + (s + 1) * SUB] = acc.astype(BF)


def run_forward(gx, marks, taps, bias, par, skip, gain):
    length = gx.shape[0]
    inner = skip.shape[1]
    chans = taps.shape[1]
    steps = length // SUB
    row = lambda cols, at=0: pl.BlockSpec((SUB, cols), lambda i, at=at: (i, at))
    whole = lambda a: pl.BlockSpec(a.shape, lambda i: (0,) * a.ndim)
    return pl.pallas_call(
        scan_forward,
        grid=(steps,),
        in_specs=[
            row(inner, 0), row(inner, 1), row(3 * SUB, 2 * inner // (3 * SUB)), row(marks.shape[1]),
            whole(taps), whole(bias), whole(par), whole(skip), whole(gain),
        ],
        out_specs=[
            row(inner), row(inner), row(2 * SUB), row(chans), row(inner),
            pl.BlockSpec((1, SUB, inner), lambda i: (i, 0, 0)), row(SUB),
        ],
        out_shape=[
            jax.ShapeDtypeStruct((length, inner), BF),
            jax.ShapeDtypeStruct((length, inner), BF),
            jax.ShapeDtypeStruct((length, 2 * SUB), BF),
            jax.ShapeDtypeStruct((length, chans), BF),
            jax.ShapeDtypeStruct((length, inner), BF),
            jax.ShapeDtypeStruct((steps, SUB, inner), BF),
            jax.ShapeDtypeStruct((length, SUB), F32),
        ],
        scratch_shapes=[pltpu.VMEM((SUB, inner), F32), pltpu.VMEM((SUB + 8, chans), F32)],
        compiler_params=pltpu.CompilerParams(vmem_limit_bytes=40 << 20),
        cost_estimate=pl.CostEstimate(flops=2 << 30, bytes_accessed=14 << 20, transcendentals=6 << 20),
        name="scan_forward",
    )(gx, gx, gx, marks, taps, bias, par, skip, gain)


def run_backward(gx, xc, bc, slope, y, dn, states, scale, marks, taps, par, skip, gain, pick):
    length = gx.shape[0]
    inner = skip.shape[1]
    chans = taps.shape[1]
    steps = length // SUB
    row = lambda cols, at=0: pl.BlockSpec((SUB, cols), lambda i, at=at: (steps - 1 - i, at))
    whole = lambda a: pl.BlockSpec(a.shape, lambda i: (0,) * a.ndim)
    total = inner + chans + SUB
    return pl.pallas_call(
        scan_backward,
        grid=(steps,),
        in_specs=[
            row(inner), row(SUB, (inner + chans) // SUB), row(inner), row(2 * SUB), row(chans), row(inner), row(inner),
            pl.BlockSpec((1, SUB, inner), lambda i: (steps - 1 - i, 0, 0)),
            pl.BlockSpec((8, SUB), lambda i: (0, steps - 1 - i)),
            row(marks.shape[1]), whole(taps), whole(par), whole(skip), whole(gain), whole(pick),
        ],
        out_specs=row(total),
        out_shape=jax.ShapeDtypeStruct((length, total), BF),
        scratch_shapes=[
            pltpu.VMEM((SUB, inner), F32),
            pltpu.VMEM((SUB + 8, chans), F32),
            pltpu.VMEM((SUB, inner), F32),
            pltpu.VMEM((SUB, inner), F32),
            pltpu.VMEM((8, inner), F32),
        ],
        compiler_params=pltpu.CompilerParams(vmem_limit_bytes=40 << 20),
        cost_estimate=pl.CostEstimate(flops=4 << 30, bytes_accessed=16 << 20, transcendentals=6 << 20),
        name="scan_backward",
    )(gx, gx, xc, bc, slope, y, dn, states, scale, marks, taps, par, skip, gain, pick)


def shifted_by(value, axis, distance):
    size = lax.axis_size(axis)
    return lax.ppermute(value, axis, [(i, (i + distance) % size) for i in range(size)])


def spread(value, axis):
    size, me = lax.axis_size(axis), lax.axis_index(axis)
    out = jnp.zeros((size, *value.shape), value.dtype)
    out = lax.dynamic_update_index_in_dim(out, value, me, 0)
    for d in range(1, size):
        got = shifted_by(value, axis, d)
        out = lax.dynamic_update_index_in_dim(out, got, (me - d) % size, 0)
    return out


def collect(blocks, axis):
    size, me = lax.axis_size(axis), lax.axis_index(axis)
    total = lax.dynamic_index_in_dim(blocks, me, 0, False).astype(F32)
    for d in range(1, size):
        piece = lax.dynamic_index_in_dim(blocks, (me + d) % size, 0, False)
        total = total + shifted_by(piece, axis, d).astype(F32)
    return total


def summed(value, axis):
    total = value
    for d in range(1, lax.axis_size(axis)):
        total = total + shifted_by(value, axis, d)
    return total


def swapped(value, axis):
    return lax.all_to_all(value, axis, 0, 0, tiled=True)


def per_device(
    tokens, output_cotangent, segments, sequence_adapter, input_norm_gain,
    gate_x_projection_weight, bc_projection_weight, step_projection_weight,
    x_convolution_taps, x_convolution_bias, bc_convolution_taps, bc_convolution_bias,
    step_size_bias, log_decay_rate, head_skip_gain, gated_norm_gain, output_projection_weight,
    in_adapter_down, in_adapter_up, out_adapter_down, out_adapter_up,
):
    seqs, block, width = tokens.shape
    inner = gate_x_projection_weight.shape[2]
    heads = step_projection_weight.shape[1]
    rank = in_adapter_down.shape[2]
    ny, nz = lax.axis_size("tensor"), lax.axis_size("context")
    my, mz = lax.axis_index("tensor"), lax.axis_index("context")
    length = block * nz
    share = block // ny

    rows = gate_x_projection_weight.shape[0]
    packed = jnp.concatenate(
        [
            output_projection_weight.T,
            gate_x_projection_weight.reshape(rows, 2 * inner),
            bc_projection_weight,
            step_projection_weight,
            jnp.zeros((rows, SUB - heads), BF),
        ],
        1,
    )
    full = lax.all_gather(packed, ("fsdp", "context"), axis=0, tiled=True)
    w_out, w_in = full[:, :inner], full[:, inner:]

    seg = swapped(segments, "context").reshape(length)
    every_adapter = lax.all_gather(sequence_adapter, "fsdp", axis=0, tiled=True)
    mine = lax.dynamic_index_in_dim(sequence_adapter, mz, 0, False)
    down_in = lax.dynamic_index_in_dim(in_adapter_down.transpose(0, 2, 1), mine, 0, False)
    up_in = lax.dynamic_index_in_dim(in_adapter_up, mine, 0, False).reshape(rank, 2 * inner)
    down_out = lax.dynamic_index_in_dim(out_adapter_down.transpose(0, 2, 1), mine, 0, False)
    up_out = lax.dynamic_index_in_dim(out_adapter_up, mine, 0, False)

    tokens_q = lax.dynamic_slice_in_dim(tokens, my * share, share, 1).astype(F32)
    cot_q = lax.dynamic_slice_in_dim(output_cotangent, my * share, share, 1)
    rms = lax.rsqrt(jnp.mean(tokens_q * tokens_q, -1, keepdims=True) + EPS_NORM)
    normed_q = (tokens_q * rms * input_norm_gain).astype(BF)

    def own_sequence(quarter):
        return spread(swapped(quarter, "context"), "tensor").transpose(1, 0, 2, 3).reshape(length, width)

    normed = own_sequence(normed_q)
    cot = own_sequence(cot_q)

    pos = jnp.arange(length)
    by_sub = seg.reshape(-1, SUB)
    last = by_sub[:, -1]
    before = jnp.concatenate([jnp.full((1,), -1, seg.dtype), last[:-1]])
    back = [jnp.where(pos >= k, jnp.roll(seg, k) == seg, False) for k in (1, 2, 3)]
    forth = [jnp.where(pos < length - k, jnp.roll(seg, -k) == seg, False) for k in (1, 2, 3)]
    same = lambda v: jnp.broadcast_to(v[:, None], by_sub.shape)
    columns = [
        *back,
        (by_sub == same(before)).reshape(-1),
        (by_sub == same(last)).reshape(-1),
        seg,
        same(last == before).reshape(-1),
        *forth,
    ]
    marks = jnp.stack([c.astype(F32) for c in columns] + [jnp.zeros((length,), F32)] * 6, -1)

    taps = jnp.concatenate([x_convolution_taps, bc_convolution_taps], 1)
    conv_bias = jnp.concatenate([x_convolution_bias, bc_convolution_bias], 0)[None]
    par = jnp.zeros((8, SUB), F32)
    par = par.at[0, :heads].set(step_size_bias).at[1, :heads].set(-jnp.exp(log_decay_rate))
    skip = jnp.repeat(head_skip_gain, inner // heads)[None]
    gain = gated_norm_gain[None]
    pick = (jnp.arange(inner)[:, None] // (inner // heads) == jnp.arange(SUB)[None, :]).astype(BF)

    low_rank = dot_nt(normed, down_in).astype(BF)
    up_wide = jnp.pad(up_in, ((0, 0), (0, w_in.shape[1] - 2 * inner)))
    gx = (dot_nn(normed, w_in) + dot_nn(low_rank, up_wide)).astype(BF)
    y, xc, bc, slope, g2, states, square = run_forward(gx, marks, taps, conv_bias, par, skip, gain)
    d_low = dot_nt(cot, up_out).astype(BF)
    dn = (dot_nn(cot, w_out) + dot_nn(d_low, down_out)).astype(BF)
    norm_dot = jnp.sum(dn.astype(F32) * g2.astype(F32), -1)
    low_part = dot_nt(down_out, g2)
    stats = jnp.concatenate(
        [jnp.sum(square, -1)[None], norm_dot[None], jnp.zeros((6, length), F32), low_part], 0
    )
    stats = summed(stats, "tensor")
    rn = lax.rsqrt(stats[0:1] / INNER_CHANNELS + EPS_NORM)
    kappa = rn * rn * rn * stats[1:2] / INNER_CHANNELS
    scale = jnp.concatenate([rn, kappa, jnp.zeros((6, length), F32)], 0)
    low_out = (stats[8:] * rn).astype(BF)

    def by_owner(value):
        return value.reshape(nz, ny, share, width).transpose(1, 0, 2, 3)

    branch = collect(by_owner(dot_nt(g2, w_out).astype(BF)), "tensor").reshape(nz * share, width)
    my_rows = lambda v: lax.dynamic_index_in_dim(v.reshape(-1, nz, ny, share), my, 2, False).reshape(-1, nz * share)
    branch = branch * my_rows(rn)[0][:, None] + dot_tn(my_rows(low_out), up_out)
    branch = swapped(branch.astype(BF).reshape(nz, share, width), "context")
    out_q = (tokens_q + branch.astype(F32)).astype(BF)
    layer_out = spread(out_q, "tensor").transpose(1, 0, 2, 3).reshape(seqs, block, width)

    grad_out_b = dot_nn(low_out, cot)
    grad_out_a = dot_tn((d_low.astype(F32) * rn[0][:, None]).astype(BF), g2)

    d_all = run_backward(gx, xc, bc, slope, y, dn, states, scale, marks, taps, par, skip, gain, pick)
    d_gate = d_all[:, : 2 * inner]
    rank_part = dot_nt(d_gate, up_in).astype(BF)
    d_in = (dot_nt(d_all, w_in) + dot_nn(rank_part, down_in)).astype(BF)
    d_rank = summed(rank_part.astype(F32), "tensor").astype(BF)
    grad_in_b = dot_tn(low_rank, d_gate)
    grad_in_a = dot_tn(d_rank, normed)

    d_in_q = swapped(collect(by_owner(d_in), "tensor").astype(BF), "context").astype(F32)
    pulled = d_in_q * input_norm_gain
    grad_q = rms * pulled - tokens_q * (rms**3 * jnp.mean(pulled * tokens_q, -1, keepdims=True))
    grad_all = spread(grad_q.astype(BF), "tensor").transpose(1, 0, 2, 3).reshape(seqs, block, width)
    grad_tokens = grad_all.astype(F32) + output_cotangent.astype(F32)

    both = ("fsdp", "context")
    parts = lax.axis_size(both)
    mine_all = jnp.concatenate([grad_in_a, grad_in_b, grad_out_a, grad_out_b], 1).astype(BF)
    columns_all = mine_all.shape[1]
    slices = lax.all_to_all(mine_all.reshape(parts, -1), both, 0, 0, tiled=True)
    table = in_adapter_down.shape[0]
    chosen = (jnp.arange(table, dtype=jnp.int32)[:, None] == every_adapter[None, :]).astype(BF)
    mixed = dot_nn(chosen, slices).astype(BF)
    everything = lax.all_gather(mixed, both, axis=0)
    everything = everything.transpose(1, 0, 2).reshape(table, rank, columns_all).astype(F32)
    cut = jnp.split(everything, [width, width + 2 * inner, width + 3 * inner], 2)
    return (
        layer_out,
        grad_tokens,
        cut[0].transpose(0, 2, 1),
        cut[1].reshape(table, rank, 2, inner),
        cut[2].transpose(0, 2, 1),
        cut[3],
    )


def solution(mesh):
    placed = (
        P("fsdp", "context", None),
        P("fsdp", "context", None),
        P("fsdp", "context"),
        P("fsdp"),
        P(),
        P(("fsdp", "context"), None, "tensor"),
        P(("fsdp", "context"), None),
        P(("fsdp", "context"), "tensor"),
        P(None, "tensor"),
        P("tensor"),
        P(),
        P(),
        P("tensor"),
        P("tensor"),
        P("tensor"),
        P("tensor"),
        P("tensor", ("fsdp", "context")),
        P(),
        P(None, None, None, "tensor"),
        P(None, "tensor", None),
        P(),
    )
    return jax.shard_map(
        per_device,
        mesh=mesh,
        in_specs=placed,
        out_specs=(
            P("fsdp", "context", None),
            P("fsdp", "context", None),
            P(),
            P(None, None, None, "tensor"),
            P(None, "tensor", None),
            P(),
        ),
        check_vma=False,
    )
```

```python
import functools

import jax
import jax.numpy as jnp
from jax import lax
from jax.experimental import pallas as pl
from jax.experimental.pallas import tpu as pltpu
from jax.sharding import PartitionSpec as P

INNER_CHANNELS = 3072
EPS_NORM = 1e-05
SUB = 128
NEG = -1e30
BF = jnp.bfloat16
F32 = jnp.float32
HIGHEST = lax.Precision.HIGHEST


def dot_nn(a, b):
    return lax.dot_general(a, b, (((1,), (0,)), ((), ())), preferred_element_type=F32)


def dot_nt(a, b):
    return lax.dot_general(a, b, (((1,), (1,)), ((), ())), preferred_element_type=F32)


def dot_tn(a, b):
    return lax.dot_general(a, b, (((0,), (0,)), ((), ())), preferred_element_type=F32)


def softplus(v):
    return jnp.maximum(v, 0.0) + jnp.log1p(jnp.exp(-jnp.abs(v)))


def lane(shape, dim):
    return lax.broadcasted_iota(jnp.int32, shape, dim)


def wide(column):
    return jnp.broadcast_to(column, (SUB, SUB))


def decays(raw, par_ref):
    rate = par_ref[1:2, :]
    shifted = raw + par_ref[0:1, :]
    dt = softplus(shifted)
    lower = (lane((SUB, SUB), 0) >= lane((SUB, SUB), 1)).astype(F32)
    run = jnp.dot(lower, dt * rate, precision=HIGHEST, preferred_element_type=F32)
    return shifted, dt, rate, run


def scan_forward(
    z_ref, x_ref, bcdt_ref, marks_ref, taps_ref, bias_ref, par_ref, skip_ref, gain_ref,
    y_ref, xc_ref, bc_ref, slope_ref, g2_ref, states_ref, square_ref,
    state, ext,
):
    step = pl.program_id(0)
    inner = z_ref.shape[1]
    chans = ext.shape[1]

    @pl.when(step == 0)
    def _():
        state[...] = jnp.zeros_like(state)
        ext[0:8, :] = jnp.zeros((8, chans), F32)

    @pl.when(step > 0)
    def _():
        ext[0:8, :] = ext[SUB : SUB + 8, :]

    ext[8 : SUB + 8, 0:inner] = x_ref[...].astype(F32)
    ext[8 : SUB + 8, inner:chans] = bcdt_ref[:, 0 : 2 * SUB].astype(F32)
    near = [wide(marks_ref[:, k : k + 1]) for k in range(3)]
    linked = wide(marks_ref[:, 3:4])
    ending = wide(marks_ref[:, 4:5])
    ids = wide(marks_ref[:, 5:6])
    passing = marks_ref[0:1, 6:7]
    left = lane((SUB, SUB), 1) < 64

    def conv(sl):
        pre = bias_ref[:, sl] + taps_ref[3:4, sl] * ext[8 : SUB + 8, sl]
        for k in range(1, 4):
            pre = pre + taps_ref[3 - k : 4 - k, sl] * (ext[8 - k : SUB + 8 - k, sl] * near[k - 1])
        sig = jax.nn.sigmoid(pre)
        out = (pre * sig).astype(BF)
        slope_ref[:, sl] = (sig * (1.0 + pre * (1.0 - sig))).astype(BF)
        return out

    b_low = conv(slice(inner, inner + SUB))
    c_low = conv(slice(inner + SUB, inner + 2 * SUB))
    bc_ref[:, 0:SUB] = b_low
    bc_ref[:, SUB : 2 * SUB] = c_low
    b_turned = b_low.astype(F32).T.astype(BF)
    _, dt, _, run = decays(bcdt_ref[:, 2 * SUB : 3 * SUB].astype(F32), par_ref)
    run_rows = run.T
    allowed = (ids == ids.T) & (lane((SUB, SUB), 0) >= lane((SUB, SUB), 1))
    mask = jnp.where(allowed, 0.0, NEG)
    cross = dot_nt(c_low, b_low)
    square = jnp.zeros((SUB, SUB), F32)
    for p in range(inner // SUB):
        sl = slice(p * SUB, (p + 1) * SUB)
        x_low = conv(sl)
        xc_ref[:, sl] = x_low
        x = x_low.astype(F32)
        run0, run1 = wide(run[:, 2 * p : 2 * p + 1]), wide(run[:, 2 * p + 1 : 2 * p + 2])
        run_p = jnp.where(left, run0, run1)
        dt_p = jnp.where(left, wide(dt[:, 2 * p : 2 * p + 1]), wide(dt[:, 2 * p + 1 : 2 * p + 2]))
        m0 = (jnp.exp(run0 - run_rows[2 * p : 2 * p + 1, :] + mask) * cross).astype(BF)
        m1 = (jnp.exp(run1 - run_rows[2 * p + 1 : 2 * p + 2, :] + mask) * cross).astype(BF)
        xdt = x * dt_p
        split = jnp.concatenate([jnp.where(left, xdt, 0.0), jnp.where(left, 0.0, xdt)], 0).astype(BF)
        before = state[:, sl]
        before_low = before.astype(BF)
        states_ref[0, :, sl] = before_low
        y = dot_nn(jnp.concatenate([m0, m1], 1), split)
        y = y + jnp.exp(run_p) * linked * dot_nn(c_low, before_low) + skip_ref[:, sl] * x
        last = run_p[SUB - 1 : SUB, :]
        toward = (xdt * (jnp.exp(last - run_p) * ending)).astype(BF)
        state[:, sl] = (jnp.exp(last) * passing) * before + dot_nn(b_turned, toward)
        z = z_ref[:, sl].astype(F32)
        gated = y * (z * jax.nn.sigmoid(z))
        y_ref[:, sl] = y.astype(BF)
        g2_ref[:, sl] = (gated * gain_ref[:, sl]).astype(BF)
        square = square + gated * gated
    square_ref[...] = square


def scan_backward(
    z_ref, dt_ref, xc_ref, bc_ref, slope_ref, y_ref, dn_ref, states_ref, s0_ref, s1_ref, s2_ref, s3_ref, marks_ref,
    taps_ref, par_ref, skip_ref, gain_ref, pick_ref, lam_in_ref, edge_in_ref,
    cot_ref, g2_ref, low_t_ref, chosen_ref, grads_in_ref,
    da_ref, lam, edge_ref, grads_ref, sent_ref,
    ext, to_dt, to_run, to_end,
):
    step = pl.program_id(0)
    inner = z_ref.shape[1]
    chans = ext.shape[1]

    @pl.when(step == 0)
    def _():
        lam[...] = lam_in_ref[...]
        ext[SUB : SUB + 8, :] = edge_in_ref[...]
        grads_ref[...] = grads_in_ref[...]

    @pl.when(step > 0)
    def _():
        ext[SUB : SUB + 8, :] = ext[0:8, :]

    linked = wide(marks_ref[:, 3:4])
    ending = wide(marks_ref[:, 4:5])
    ids = wide(marks_ref[:, 5:6])
    passing = marks_ref[0:1, 6:7]
    later = [wide(marks_ref[:, 7 + k : 8 + k]) for k in range(3)]
    left = lane((SUB, SUB), 1) < 64
    stats = s0_ref[...] + s1_ref[...] + s2_ref[...] + s3_ref[...]
    rn_row = lax.rsqrt(stats[0:1, :] / INNER_CHANNELS + EPS_NORM)
    grads_ref[:, 0:inner] += dot_nn((low_t_ref[...].astype(F32) * rn_row).astype(BF), g2_ref[...])
    grads_ref[:, inner:] += dot_nn((stats[8:, :] * rn_row).astype(BF), cot_ref[...])
    rn = jnp.broadcast_to(rn_row, (SUB, SUB)).T
    kappa = jnp.broadcast_to(rn_row * rn_row * rn_row * stats[1:2, :] / INNER_CHANNELS, (SUB, SUB)).T
    shifted, dt, rate, run = decays(dt_ref[...].astype(F32), par_ref)
    run_rows = run.T
    b_low, c_low = bc_ref[:, 0:SUB], bc_ref[:, SUB : 2 * SUB]
    c_turned = c_low.astype(F32).T.astype(BF)
    allowed = (ids == ids.T) & (lane((SUB, SUB), 0) <= lane((SUB, SUB), 1))
    mask = jnp.where(allowed, 0.0, NEG)
    cross = dot_nt(b_low, c_low)
    d_cross = jnp.zeros((SUB, SUB), F32)
    d_b = jnp.zeros((SUB, SUB), F32)
    d_c = jnp.zeros((SUB, SUB), F32)
    for p in range(inner // SUB):
        sl = slice(p * SUB, (p + 1) * SUB)
        z = z_ref[:, sl].astype(F32)
        sig = jax.nn.sigmoid(z)
        silu = z * sig
        y = y_ref[:, sl].astype(F32)
        d_gated = rn * (dn_ref[:, sl].astype(F32) * gain_ref[:, sl]) - kappa * (y * silu)
        da_ref[:, sl] = (d_gated * y * sig * (1.0 + z * (1.0 - sig))).astype(BF)
        dy = d_gated * silu
        x = xc_ref[:, sl].astype(F32)
        run0, run1 = wide(run[:, 2 * p : 2 * p + 1]), wide(run[:, 2 * p + 1 : 2 * p + 2])
        run_p = jnp.where(left, run0, run1)
        dt_p = jnp.where(left, wide(dt[:, 2 * p : 2 * p + 1]), wide(dt[:, 2 * p + 1 : 2 * p + 2]))
        l0 = jnp.exp(run_rows[2 * p : 2 * p + 1, :] - run0 + mask)
        l1 = jnp.exp(run_rows[2 * p + 1 : 2 * p + 2, :] - run1 + mask)
        xdt = x * dt_p
        x_split = jnp.concatenate([jnp.where(left, xdt, 0.0), jnp.where(left, 0.0, xdt)], 0).astype(BF)
        dy_split = jnp.concatenate([jnp.where(left, dy, 0.0), jnp.where(left, 0.0, dy)], 0).astype(BF)
        d_m = dot_nt(x_split, dy.astype(BF))
        d_cross = d_cross + l0 * d_m[0:SUB] + l1 * d_m[SUB : 2 * SUB]
        m = jnp.concatenate([l0 * cross, l1 * cross], 1).astype(BF)
        lam_p = lam[:, sl]
        lam_low = lam_p.astype(BF)
        last = run_p[SUB - 1 : SUB, :]
        toward = jnp.exp(last - run_p) * ending
        carried = toward * dot_nn(b_low, lam_low)
        d_xt = dot_nn(m, dy_split) + carried
        skip = skip_ref[:, sl]
        ext[0:SUB, sl] = (dt_p * d_xt + skip * dy) * slope_ref[:, sl].astype(F32)
        x_dx = x * d_xt
        to_dt[:, sl] = x_dx
        to_run[:, sl] = dy * (y - skip * x) - dt_p * x_dx
        reached = (jnp.exp(run_p) * linked * dy).astype(BF)
        before_low = states_ref[0, :, sl]
        keep = jnp.exp(last) * passing
        to_end[0:1, sl] = jnp.sum(xdt * carried, 0, keepdims=True) + keep * jnp.sum(
            lam_p * before_low.astype(F32), 0, keepdims=True
        )
        d_b = d_b + dot_nt((xdt * toward).astype(BF), lam_low)
        d_c = d_c + dot_nt(reached, before_low)
        lam[:, sl] = keep * lam_p + dot_nn(c_turned, reached)
    d_cross_low = d_cross.astype(BF)
    d_b = d_b + dot_nn(d_cross_low, c_low)
    d_c = d_c + dot_nn(d_cross.T.astype(BF), b_low)
    ext[0:SUB, inner : inner + SUB] = d_b * slope_ref[:, inner : inner + SUB].astype(F32)
    ext[0:SUB, inner + SUB : chans] = d_c * slope_ref[:, inner + SUB : chans].astype(F32)

    def by_head(v):
        high = v.astype(BF)
        return dot_nn(high, pick_ref[...]) + dot_nn((v - high.astype(F32)).astype(BF), pick_ref[...])

    d_run = by_head(to_run[...])
    d_end = by_head(to_end[...])[0:1, :]
    d_run = d_run + jnp.where(lane((SUB, SUB), 0) == SUB - 1, d_end, 0.0)
    upper = (lane((SUB, SUB), 0) <= lane((SUB, SUB), 1)).astype(F32)
    d_log = jnp.dot(upper, d_run, precision=HIGHEST, preferred_element_type=F32)
    d_dt = by_head(to_dt[...]) + rate * d_log
    da_ref[:, inner + chans : inner + chans + SUB] = (d_dt * jax.nn.sigmoid(shifted)).astype(BF)
    for s in range(chans // SUB):
        sl = slice(s * SUB, (s + 1) * SUB)
        acc = taps_ref[3:4, sl] * ext[0:SUB, sl]
        for k in range(1, 4):
            acc = acc + taps_ref[3 - k : 4 - k, sl] * (ext[k : SUB + k, sl] * later[k - 1])
        da_ref[:, inner + s * SUB : inner + (s + 1) * SUB] = acc.astype(BF)

    @pl.when(step == pl.num_programs(0) - 1)
    def _():
        edge_ref[...] = ext[0:8, :]
        sent_ref[:, 0 : grads_ref.shape[1]] = grads_ref[...].astype(BF)
        sent_ref[:, grads_ref.shape[1] :] = jnp.broadcast_to(chosen_ref[...], (grads_ref.shape[0], SUB)).astype(BF)


def whole(a):
    return pl.BlockSpec(a.shape, lambda i, *_: (0,) * a.ndim)


def params(mib=60):
    return pltpu.CompilerParams(vmem_limit_bytes=mib << 20)


def takes(us):
    return pl.CostEstimate(flops=us * 100_000_000, bytes_accessed=us * 300_000, transcendentals=0)


def run_forward(gx, marks, taps, bias, par, skip, gain):
    length = gx.shape[0]
    inner = skip.shape[1]
    chans = taps.shape[1]
    steps = length // SUB
    row = lambda cols, at=0: pl.BlockSpec((SUB, cols), lambda i, at=at: (i, at))
    return pl.pallas_call(
        scan_forward,
        grid=(steps,),
        in_specs=[
            row(inner, 0), row(inner, 1), row(3 * SUB, 2 * inner // (3 * SUB)), row(marks.shape[1]),
            whole(taps), whole(bias), whole(par), whole(skip), whole(gain),
        ],
        out_specs=[
            row(inner), row(inner), row(2 * SUB), row(chans), row(inner),
            pl.BlockSpec((1, SUB, inner), lambda i: (i, 0, 0)), row(SUB),
        ],
        out_shape=[
            jax.ShapeDtypeStruct((length, inner), BF),
            jax.ShapeDtypeStruct((length, inner), BF),
            jax.ShapeDtypeStruct((length, 2 * SUB), BF),
            jax.ShapeDtypeStruct((length, chans), BF),
            jax.ShapeDtypeStruct((length, inner), BF),
            jax.ShapeDtypeStruct((steps, SUB, inner), BF),
            jax.ShapeDtypeStruct((length, SUB), F32),
        ],
        scratch_shapes=[pltpu.VMEM((SUB, inner), F32), pltpu.VMEM((SUB + 8, chans), F32)],
        compiler_params=params(),
        cost_estimate=takes(11),
        name="scan_forward",
    )(gx, gx, gx, marks, taps, bias, par, skip, gain)


def run_backward(
    half, gx, xc, bc, slope, y, dn, states, stats, marks, taps, par, skip, gain, pick, cot, g2, low_t, chosen, lam, edge, grads
):
    length = gx.shape[0] // 2
    inner = skip.shape[1]
    chans = taps.shape[1]
    steps = length // SUB
    top = (half + 1) * steps - 1
    row = lambda cols, at=0: pl.BlockSpec((SUB, cols), lambda i, at=at: (top - i, at))
    total = inner + chans + SUB
    return pl.pallas_call(
        scan_backward,
        grid=(steps,),
        in_specs=[
            row(inner), row(SUB, (inner + chans) // SUB), row(inner), row(2 * SUB), row(chans), row(inner), row(inner),
            pl.BlockSpec((1, SUB, inner), lambda i: (top - i, 0, 0)),
            *[pl.BlockSpec((stats[0].shape[0], SUB), lambda i: (0, top - i))] * 4,
            row(marks.shape[1]), whole(taps), whole(par), whole(skip), whole(gain), whole(pick), whole(lam), whole(edge),
            row(cot.shape[1]), row(inner), pl.BlockSpec((low_t.shape[0], SUB), lambda i: (0, top - i)),
            whole(chosen), whole(grads),
        ],
        out_specs=[
            pl.BlockSpec((SUB, total), lambda i: (steps - 1 - i, 0)), whole(lam), whole(edge), whole(grads),
            pl.BlockSpec((grads.shape[0], grads.shape[1] + SUB), lambda i: (0, 0)),
        ],
        out_shape=[
            jax.ShapeDtypeStruct((length, total), BF),
            jax.ShapeDtypeStruct(lam.shape, F32),
            jax.ShapeDtypeStruct(edge.shape, F32),
            jax.ShapeDtypeStruct(grads.shape, F32),
            jax.ShapeDtypeStruct((grads.shape[0], grads.shape[1] + SUB), BF),
        ],
        scratch_shapes=[
            pltpu.VMEM((SUB + 8, chans), F32),
            pltpu.VMEM((SUB, inner), F32),
            pltpu.VMEM((SUB, inner), F32),
            pltpu.VMEM((8, inner), F32),
        ],
        compiler_params=params(),
        cost_estimate=takes(12),
        name="scan_backward",
    )(gx, gx, xc, bc, slope, y, dn, states, *stats, marks, taps, par, skip, gain, pick, lam, edge, cot, g2, low_t, chosen, grads)


def assemble(me, pieces, out_ref, block):
    own, behind, ahead, far_low, far_high = pieces
    chunks, share = own.shape[0], own.shape[1]
    for c in range(chunks):
        far = far_low[c] if c < chunks // 2 else far_high[c - chunks // 2]
        for d, part in ((0, own[c]), (1, behind[c]), (2, far), (3, ahead[c])):
            at = pl.multiple_of(c * block + ((me + 4 - d) % 4) * share, share)
            out_ref[pl.ds(at, share), :] = part


def ordered(me_ref, pieces, down_ref, rows_ref, rank_ref, rank_t_ref, gain_ref=None):
    assemble(me_ref[0], pieces, rows_ref, 4 * pieces[0].shape[1])
    if gain_ref is not None:
        for k in range(rows_ref.shape[0] // 64):
            here = slice(k * 64, (k + 1) * 64)
            t = rows_ref[here, :].astype(F32)
            rms = lax.rsqrt(jnp.mean(t * t, -1, keepdims=True) + EPS_NORM)
            rows_ref[here, :] = (t * rms * gain_ref[...]).astype(BF)
    low = dot_nt(rows_ref[...], down_ref[...])
    rank = low.shape[1]
    rank_ref[...] = low.astype(BF)
    low = jnp.concatenate([low, jnp.zeros((low.shape[0], SUB - rank), F32)], 1)
    for k in range(low.shape[0] // SUB):
        here = slice(k * SUB, (k + 1) * SUB)
        rank_t_ref[:, here] = low[here, :].T[0:rank, :].astype(BF)


def in_order(me_ref, p0, p1, p2, p3, p4, down_ref, gain_ref, rows_ref, rank_ref, rank_t_ref):
    ordered(me_ref, (p0, p1, p2, p3, p4), down_ref, rows_ref, rank_ref, rank_t_ref, gain_ref)


def run_in_order(me, pieces, down, gain):
    chunks, share, width = pieces[0].shape
    length = chunks * 4 * share
    rank = down.shape[0]
    shapes = [(length, width), (length, rank), (rank, length)]
    return pl.pallas_call(
        in_order,
        grid_spec=pltpu.PrefetchScalarGridSpec(
            num_scalar_prefetch=1,
            grid=(1,),
            in_specs=[*[whole(p) for p in pieces], whole(down), whole(gain)],
            out_specs=[pl.BlockSpec(n, lambda i, me: (0, 0)) for n in shapes],
        ),
        out_shape=[jax.ShapeDtypeStruct(n, BF) for n in shapes],
        compiler_params=params(),
        cost_estimate=takes(5),
        name="in_order",
    )(me, *pieces, down, gain)


def project_in(normed_ref, w_ref, rank_ref, up_ref, gx_ref):
    gx_ref[...] = (dot_nn(normed_ref[...], w_ref[...]) + dot_nn(rank_ref[...], up_ref[...])).astype(BF)


def run_project_in(normed, weights, low_rank, up, tile):
    length, width = normed.shape
    rank, columns = up.shape
    return pl.pallas_call(
        project_in,
        grid=(columns // tile,),
        in_specs=[
            whole(normed),
            pl.BlockSpec((width, tile), lambda j: (0, j)),
            whole(low_rank),
            pl.BlockSpec((rank, tile), lambda j: (0, j)),
        ],
        out_specs=pl.BlockSpec((length, tile), lambda j: (0, j)),
        out_shape=jax.ShapeDtypeStruct((length, columns), BF),
        compiler_params=params(),
        cost_estimate=takes(11),
        name="project_in",
    )(normed, weights, low_rank, up)


def lane_rows(v):
    return lax.dot_general(
        jnp.ones((8, v.shape[1]), F32), v, (((1,), (1,)), ((), ())), precision=HIGHEST, preferred_element_type=F32
    )


def pull_back(
    me_ref, p0, p1, p2, p3, p4, up_ref, w_ref, g2_ref, square_ref, down_ref,
    dn_ref, stats_ref, cot_ref, low_t_ref,
    low, dots,
):
    step = pl.program_id(0)

    @pl.when(step == 0)
    def _():
        ordered(me_ref, (p0, p1, p2, p3, p4), up_ref, cot_ref, low, low_t_ref)
        dots[...] = jnp.zeros_like(dots)
        stats_ref[...] = jnp.zeros_like(stats_ref)

    dn = dot_nn(cot_ref[...], w_ref[...]) + dot_nn(low[...], down_ref[...])
    dn_ref[...] = dn.astype(BF)
    g2 = g2_ref[...]
    both = dn * g2.astype(F32)
    total = dots[...]
    for k in range(both.shape[1] // SUB):
        total = total + both[:, k * SUB : (k + 1) * SUB]
    dots[...] = total
    stats_ref[8:, :] += dot_nt(down_ref[...], g2)

    @pl.when(step == pl.num_programs(0) - 1)
    def _():
        first = lane((8, stats_ref.shape[1]), 0) == 0
        stats_ref[0:8, :] = jnp.where(first, lane_rows(square_ref[...]), lane_rows(dots[...]))


def run_pull_back(me, pieces, weights, up, g2, square, down, tile=384):
    width = pieces[0].shape[2]
    length, inner = g2.shape
    rank = down.shape[0]
    first = (weights.shape[1] - inner) // tile
    return pl.pallas_call(
        pull_back,
        grid_spec=pltpu.PrefetchScalarGridSpec(
            num_scalar_prefetch=1,
            grid=(inner // tile,),
            in_specs=[
                *[whole(p) for p in pieces],
                whole(up),
                pl.BlockSpec((width, tile), lambda j, me: (0, first + j)),
                pl.BlockSpec((length, tile), lambda j, me: (0, j)),
                whole(square),
                pl.BlockSpec((rank, tile), lambda j, me: (0, j)),
            ],
            out_specs=[
                pl.BlockSpec((length, tile), lambda j, me: (0, j)),
                pl.BlockSpec((8 + rank, length), lambda j, me: (0, 0)),
                pl.BlockSpec((length, width), lambda j, me: (0, 0)),
                pl.BlockSpec((rank, length), lambda j, me: (0, 0)),
            ],
            scratch_shapes=[pltpu.VMEM((length, rank), BF), pltpu.VMEM((length, SUB), F32)],
        ),
        out_shape=[
            jax.ShapeDtypeStruct((length, inner), BF),
            jax.ShapeDtypeStruct((8 + rank, length), F32),
            jax.ShapeDtypeStruct((length, width), BF),
            jax.ShapeDtypeStruct((rank, length), BF),
        ],
        compiler_params=params(),
        cost_estimate=takes(8),
        name="pull_back",
    )(me, *pieces, up, weights, g2, square, down)


def deal(me, held, outs, share):
    far_low, far_high, ahead, behind, own = outs
    chunks = held.shape[0] // (4 * share)

    def rows(c, d):
        return held[pl.ds(pl.multiple_of((c * 4 + (me + d) % 4) * share, share), share), :]

    for c in range(chunks):
        at = pl.ds(c * share, share)
        ahead[at, :] = rows(c, 1)
        behind[at, :] = rows(c, 3)
        own[at, :] = rows(c, 0)
        if c < chunks // 2:
            far_low[at, :] = rows(c, 2)
        else:
            far_high[pl.ds((c - chunks // 2) * share, share), :] = rows(c, 2)


def project_out(me_ref, g2_ref, w0_ref, w1_ref, o0, o1, o2, o3, o4, held):
    cut = w0_ref.shape[1]
    held[...] = (dot_nt(g2_ref[:, 0:cut], w0_ref[...]) + dot_nt(g2_ref[:, cut:], w1_ref[...])).astype(BF)
    deal(me_ref[0], held, (o0, o1, o2, o3, o4), 64)


def dealt(length, width, tile):
    own = length // 4
    sizes = (own // 2, own // 2, own, own, own)
    specs = [pl.BlockSpec((n, tile), lambda j, me: (0, j)) for n in sizes]
    return specs, [jax.ShapeDtypeStruct((n, width), BF) for n in sizes]


def run_project_out(me, g2, weights, tile=256):
    length, inner = g2.shape
    width = weights.shape[0]
    first = 2 * (weights.shape[1] - inner) // inner
    specs, shapes = dealt(length, width, tile)
    return pl.pallas_call(
        project_out,
        grid_spec=pltpu.PrefetchScalarGridSpec(
            num_scalar_prefetch=1,
            grid=(width // tile,),
            in_specs=[
                whole(g2),
                pl.BlockSpec((tile, inner // 2), lambda j, me: (j, first)),
                pl.BlockSpec((tile, inner // 2), lambda j, me: (j, first + 1)),
            ],
            out_specs=specs,
            scratch_shapes=[pltpu.VMEM((length, tile), BF)],
        ),
        out_shape=shapes,
        compiler_params=params(),
        cost_estimate=takes(5),
        name="project_out",
    )(me, g2, weights, weights)


def input_grad(me_ref, d_ref, w_ref, down_ref, up_ref, rank_t_ref, o0, o1, o2, o3, o4, pushed_ref, up_grad_ref, held, low):
    inner2 = up_ref.shape[1]

    @pl.when(pl.program_id(0) == 0)
    def _():
        gate = d_ref[:, 0:inner2]
        low[...] = dot_nt(gate, up_ref[...]).astype(BF)
        pushed_ref[...] = dot_nt(up_ref[...], gate)
        up_grad_ref[...] = dot_nn(rank_t_ref[...], gate)

    total = dot_nt(d_ref[...], w_ref[...]) + dot_nn(low[...], down_ref[...])
    held[...] = total.astype(BF)
    deal(me_ref[0], held, (o0, o1, o2, o3, o4), 64)


def run_input_grad(me, half, d_all, weights, down, up, rank_t, tile=256):
    length, columns = d_all.shape
    width = weights.shape[0]
    rank = down.shape[0]
    specs, shapes = dealt(length, width, tile)
    return pl.pallas_call(
        input_grad,
        grid_spec=pltpu.PrefetchScalarGridSpec(
            num_scalar_prefetch=1,
            grid=(width // tile,),
            in_specs=[
                whole(d_all),
                pl.BlockSpec((tile, columns), lambda j, me: (j, 0)),
                pl.BlockSpec((rank, tile), lambda j, me: (0, j)),
                whole(up),
                pl.BlockSpec((rank, length), lambda j, me: (0, half)),
            ],
            out_specs=[
                *specs,
                pl.BlockSpec((rank, length), lambda j, me: (0, 0)),
                pl.BlockSpec(up.shape, lambda j, me: (0, 0)),
            ],
            scratch_shapes=[pltpu.VMEM((length, tile), BF), pltpu.VMEM((length, rank), BF)],
        ),
        out_shape=[*shapes, jax.ShapeDtypeStruct((rank, length), F32), jax.ShapeDtypeStruct(up.shape, F32)],
        compiler_params=params(),
        cost_estimate=takes(7),
        name="input_grad",
    )(me, d_all, weights, down, up, rank_t)


def place(me, pieces, out, seq, half):
    own, behind, ahead, far_low, far_high = pieces
    share = own.shape[1]
    for d, part in ((0, own), (1, behind), (3, ahead)):
        out[pl.ds(pl.multiple_of(((me + 4 - d) % 4) * share, share), share), :] = part[0]
    far = pl.ds(pl.multiple_of(((me + 2) % 4) * share, share), share)

    @pl.when(seq < half)
    def _():
        out[far, :] = far_low[0]

    @pl.when(seq >= half)
    def _():
        out[far, :] = far_high[0]


def columns_of(stats_refs, cols):
    total = stats_refs[0][...] + stats_refs[1][...] + stats_refs[2][...] + stats_refs[3][...]
    rows, length = total.shape
    total = jnp.concatenate([total, jnp.zeros((SUB - rows, length), F32)], 0)
    for k in range(length // SUB):
        cols[k * SUB : (k + 1) * SUB, :] = total[:, k * SUB : (k + 1) * SUB].T
    return total


def finish_branch(me_ref, own_ref, a_ref, b_ref, s0, s1, s2, s3, up_ref, out_ref, cols):
    columns_of((s0, s1, s2, s3), cols)
    share = out_ref.shape[1]
    rank = up_ref.shape[0]
    for c in range(out_ref.shape[0]):
        at = pl.multiple_of((c * 4 + me_ref[0]) * share, share)
        mine = cols[pl.ds(at, share), :]
        rn = lax.rsqrt(mine[:, 0:1] / INNER_CHANNELS + EPS_NORM)
        here = slice(c * share, (c + 1) * share)
        total = own_ref[here, :].astype(F32) + a_ref[here, :].astype(F32) + b_ref[here, :].astype(F32)
        low = (mine[:, 8 : 8 + rank] * rn).astype(BF)
        out_ref[c] = (total * rn + dot_nn(low, up_ref[...])).astype(BF)


def run_finish_branch(me, parts, stats, up, chunks):
    rows, width = parts[0].shape
    length = stats[0].shape[1]
    args = (*parts, *stats, up)
    return pl.pallas_call(
        finish_branch,
        grid_spec=pltpu.PrefetchScalarGridSpec(
            num_scalar_prefetch=1,
            grid=(1,),
            in_specs=[whole(a) for a in args],
            out_specs=pl.BlockSpec((chunks, rows // chunks, width), lambda i, me: (0, 0, 0)),
            scratch_shapes=[pltpu.VMEM((length, SUB), F32)],
        ),
        out_shape=jax.ShapeDtypeStruct((chunks, rows // chunks, width), BF),
        compiler_params=params(),
        cost_estimate=takes(3),
        name="finish_branch",
    )(me, *args)


def adapter_lanes(mine_ref, rows):
    return (lane((rows, SUB), 1) == mine_ref[0]).astype(BF)


def in_grads(mine_ref, p0, p1, p2, p3, up0_ref, up1_ref, normed_ref, out_ref):
    rank = (p0[...] + p1[...] + p2[...] + p3[...]).astype(BF)
    width, inner2 = normed_ref.shape[1], up0_ref.shape[1]
    out_ref[:, 0:width] = dot_nn(rank, normed_ref[...]).astype(BF)
    out_ref[:, width : width + inner2] = (up0_ref[...] + up1_ref[...]).astype(BF)
    out_ref[:, width + inner2 :] = adapter_lanes(mine_ref, out_ref.shape[0])


def run_grads(kernel, mine, args, columns, name):
    rank = args[-3].shape[0]
    return pl.pallas_call(
        kernel,
        grid_spec=pltpu.PrefetchScalarGridSpec(
            num_scalar_prefetch=1,
            grid=(1,),
            in_specs=[whole(a) for a in args],
            out_specs=pl.BlockSpec((rank, columns + SUB), lambda i, mine: (0, 0)),
        ),
        out_shape=jax.ShapeDtypeStruct((rank, columns + SUB), BF),
        compiler_params=params(),
        cost_estimate=takes(3),
        name=name,
    )(mine, *args)


def finish_out(me_ref, p0, p1, p2, p3, p4, tokens_ref, out_ref, held):
    place(me_ref[0], (p0, p1, p2, p3, p4), held, pl.program_id(0), pl.num_programs(0) // 2)
    out_ref[0] = (tokens_ref[0].astype(F32) + held[...].astype(F32)).astype(BF)


def finish_grad(me_ref, p0, p1, p2, p3, p4, tokens_ref, cot_ref, gain_ref, out_ref, held):
    place(me_ref[0], (p0, p1, p2, p3, p4), held, pl.program_id(0), pl.num_programs(0) // 2)
    t = tokens_ref[0].astype(F32)
    rms = lax.rsqrt(jnp.mean(t * t, -1, keepdims=True) + EPS_NORM)
    pulled = held[...].astype(F32) * gain_ref[...]
    slope = rms * rms * rms * jnp.mean(pulled * t, -1, keepdims=True)
    out_ref[0] = rms * pulled - t * slope + cot_ref[0].astype(F32)


def piece_specs(pieces):
    share, width = pieces[0].shape[1:]
    half = pieces[0].shape[0] // 2
    full = pl.BlockSpec((1, share, width), lambda s, me: (s, 0, 0))
    return [
        full, full, full,
        pl.BlockSpec((1, share, width), lambda s, me: (jnp.minimum(s, half - 1), 0, 0)),
        pl.BlockSpec((1, share, width), lambda s, me: (jnp.maximum(s - half, 0), 0, 0)),
    ]


def run_finish(kernel, me, pieces, extra, dtype, name):
    seqs, block, width = extra[0].shape
    seq = pl.BlockSpec((1, block, width), lambda s, me: (s, 0, 0))
    specs = [seq if a.ndim == 3 else whole(a) for a in extra]
    return pl.pallas_call(
        kernel,
        grid_spec=pltpu.PrefetchScalarGridSpec(
            num_scalar_prefetch=1,
            grid=(seqs,),
            in_specs=[*piece_specs(pieces), *specs],
            out_specs=seq,
            scratch_shapes=[pltpu.VMEM((block, width), BF)],
        ),
        out_shape=jax.ShapeDtypeStruct((seqs, block, width), dtype),
        compiler_params=params(30),
        cost_estimate=takes(5),
        name=name,
    )(me, *pieces, *extra)


def fill_tables(all_ref, *outs):
    table, rank = outs[0].shape[0], outs[0].shape[1]
    rows, columns = all_ref.shape
    spread = (lane((SUB, table * rank), 0) == lane((SUB, table * rank), 1) // rank).astype(BF)
    place = dot_nn(all_ref[:, columns - SUB :], spread)
    same = lane((rows, table * rank), 0) % rank == lane((rows, table * rank), 1) % rank
    place = jnp.where(same, place, 0.0).T.astype(BF)
    at = 0
    for out in outs:
        here = dot_nn(place, all_ref[:, at : at + out.shape[2]])
        for a in range(table):
            out[a] = here[a * rank : (a + 1) * rank, :]
        at += out.shape[2]


def run_tables(everything, table, rank, widths):
    return pl.pallas_call(
        fill_tables,
        out_shape=[jax.ShapeDtypeStruct((table, rank, w), F32) for w in widths],
        compiler_params=params(),
        cost_estimate=takes(3),
        name="fill_tables",
    )(everything)


def shifted_by(value, axis, distance):
    size = lax.axis_size(axis)
    return lax.ppermute(value, axis, [(i, (i + distance) % size) for i in range(size)])


def tie(*values):
    return lax.optimization_barrier(values)


def ring_near(own, axis):
    return shifted_by(own, axis, 1), shifted_by(own, axis, -1)


def ring_far(near, axis):
    half = near[0].shape[0] // 2
    return shifted_by(near[0][:half], axis, 1), shifted_by(near[1][half:], axis, -1)


def ring_first(pieces, axis):
    return shifted_by(pieces[0], axis, 1), shifted_by(pieces[1], axis, -1)


def add_half(ahead_in, behind_in, low_ref, high_ref, ahead_ref, behind_ref):
    ahead_ref[...] = (ahead_in[...].astype(F32) + low_ref[...].astype(F32)).astype(BF)
    behind_ref[...] = (behind_in[...].astype(F32) + high_ref[...].astype(F32)).astype(BF)


def ring_middle(pieces, got):
    _, _, ahead, behind, _ = pieces
    half, width = got[0].shape
    first, second = (pl.BlockSpec((half, width), lambda i, k=k: (k, 0)) for k in (0, 1))
    return pl.pallas_call(
        add_half,
        grid=(1,),
        in_specs=[first, second, first, first],
        out_specs=[first, second],
        out_shape=[jax.ShapeDtypeStruct(ahead.shape, BF), jax.ShapeDtypeStruct(behind.shape, BF)],
        input_output_aliases={0: 0, 1: 1},
        compiler_params=params(),
        cost_estimate=takes(1),
        name="add_half",
    )(ahead, behind, *got)


def ring_last(near, axis):
    return shifted_by(near[0], axis, 1), shifted_by(near[1], axis, -1)


def ring_total(pieces, got):
    return pieces[4].astype(F32) + got[0].astype(F32) + got[1].astype(F32)


def shared(value, axis):
    return [value] + [shifted_by(value, axis, d) for d in range(1, lax.axis_size(axis))]


def swapped(value, axis):
    return lax.all_to_all(value, axis, 0, 0, tiled=True)


def per_device(
    tokens, output_cotangent, segments, sequence_adapter, input_norm_gain,
    gate_x_projection_weight, bc_projection_weight, step_projection_weight,
    x_convolution_taps, x_convolution_bias, bc_convolution_taps, bc_convolution_bias,
    step_size_bias, log_decay_rate, head_skip_gain, gated_norm_gain, output_projection_weight,
    in_adapter_down, in_adapter_up, out_adapter_down, out_adapter_up,
):
    seqs, block, width = tokens.shape
    inner = gate_x_projection_weight.shape[2]
    heads = step_projection_weight.shape[1]
    rank = in_adapter_down.shape[2]
    ny, nz = lax.axis_size("tensor"), lax.axis_size("context")
    my, mz = lax.axis_index("tensor"), lax.axis_index("context")
    me = my.astype(jnp.int32).reshape(1)
    length = block * nz
    share = block // ny

    rows = gate_x_projection_weight.shape[0]
    packed = jnp.concatenate(
        [
            gate_x_projection_weight.reshape(rows, 2 * inner),
            bc_projection_weight,
            step_projection_weight,
            jnp.zeros((rows, SUB - heads), BF),
            output_projection_weight.T,
        ],
        1,
    )
    full = lax.all_gather(packed, ("fsdp", "context"), axis=0, tiled=True)

    quarter = lambda a: lax.dynamic_slice_in_dim(a, my * share, share, 1)
    tokens_q = quarter(tokens)
    later = (
        segments, sequence_adapter, x_convolution_taps, x_convolution_bias, bc_convolution_taps, bc_convolution_bias,
        step_size_bias, log_decay_rate, head_skip_gain, gated_norm_gain,
        in_adapter_down, in_adapter_up, out_adapter_down, out_adapter_up,
    )
    tokens_s, output_cotangent, later = tie(swapped(tokens_q, "context"), output_cotangent, later)
    cot_q = quarter(output_cotangent)
    (
        segments, sequence_adapter, x_convolution_taps, x_convolution_bias, bc_convolution_taps, bc_convolution_bias,
        step_size_bias, log_decay_rate, head_skip_gain, gated_norm_gain,
        in_adapter_down, in_adapter_up, out_adapter_down, out_adapter_up,
    ) = later
    tokens_near = ring_near(tokens_s, "tensor")

    seg = swapped(segments, "context").reshape(length)
    mine = lax.dynamic_index_in_dim(sequence_adapter, mz, 0, False)
    down_in = lax.dynamic_index_in_dim(in_adapter_down.transpose(0, 2, 1), mine, 0, False)
    up_in = lax.dynamic_index_in_dim(in_adapter_up, mine, 0, False).reshape(rank, 2 * inner)
    down_out = lax.dynamic_index_in_dim(out_adapter_down.transpose(0, 2, 1), mine, 0, False)
    up_out = lax.dynamic_index_in_dim(out_adapter_up, mine, 0, False)

    pos = jnp.arange(length)
    by_sub = seg.reshape(-1, SUB)
    last = by_sub[:, -1]
    before = jnp.concatenate([jnp.full((1,), -1, seg.dtype), last[:-1]])
    back = [jnp.where(pos >= k, jnp.roll(seg, k) == seg, False) for k in (1, 2, 3)]
    forth = [jnp.where(pos < length - k, jnp.roll(seg, -k) == seg, False) for k in (1, 2, 3)]
    same = lambda v: jnp.broadcast_to(v[:, None], by_sub.shape)
    kinds = [
        *back,
        (by_sub == same(before)).reshape(-1),
        (by_sub == same(last)).reshape(-1),
        seg,
        same(last == before).reshape(-1),
        *forth,
    ]
    marks = jnp.stack([c.astype(F32) for c in kinds] + [jnp.zeros((length,), F32)] * 6, -1)

    taps = jnp.concatenate([x_convolution_taps, bc_convolution_taps], 1)
    conv_bias = jnp.concatenate([x_convolution_bias, bc_convolution_bias], 0)[None]
    par = jnp.zeros((8, SUB), F32)
    par = par.at[0, :heads].set(step_size_bias).at[1, :heads].set(-jnp.exp(log_decay_rate))
    skip = jnp.repeat(head_skip_gain, inner // heads)[None]
    gain = gated_norm_gain[None]
    pick = (jnp.arange(inner)[:, None] // (inner // heads) == jnp.arange(SUB)[None, :]).astype(BF)

    up_wide = jnp.pad(up_in, ((0, 0), (0, 512)))
    lam, edge = jnp.zeros((SUB, inner), F32), jnp.zeros((8, taps.shape[1]), F32)
    grads = jnp.zeros((rank, inner + width), F32)
    chosen = (jnp.arange(SUB) == mine).astype(F32)[None]
    mine = mine.reshape(1)
    fixed = (lam, edge, mine, grads, chosen)
    small = (marks, taps, conv_bias, par, skip, gain, pick, down_in, up_in, up_wide, down_out, up_out, fixed)
    tokens_near, cot_q, small = tie(tokens_near, cot_q, small)
    marks, taps, conv_bias, par, skip, gain, pick, down_in, up_in, up_wide, down_out, up_out, fixed = small
    lam, edge, mine, grads, chosen = fixed
    tokens_far = ring_far(tokens_near, "tensor")
    cot_s = swapped(cot_q, "context")
    tokens_far, cot_s = tie(tokens_far, cot_s)
    cot_near = ring_near(cot_s, "tensor")
    normed, low_rank, rank_t = run_in_order(me, (tokens_s, *tokens_near, *tokens_far), down_in, input_norm_gain[None])
    gx = run_project_in(normed, full, low_rank, up_wide, 512)
    gx, cot_near = tie(gx, cot_near)
    cot_far = ring_far(cot_near, "tensor")
    y, xc, bc, slope, g2, states, square = run_forward(gx, marks, taps, conv_bias, par, skip, gain)
    g2, cot_far = tie(g2, cot_far)
    dn, stats, cot, d_low_t = run_pull_back(me, (cot_s, *cot_near, *cot_far), full, up_out, g2, square, down_out)
    g2, stats = tie(g2, stats)
    stats_all = shared(stats, "tensor")
    out_pieces = run_project_out(me, g2, full)
    out_pieces, stats_all = tie(out_pieces, stats_all)
    out_far = ring_first(out_pieces, "tensor")

    backward = lambda half, *carried: run_backward(
        half, gx, xc, bc, slope, y, dn, states, stats_all, marks, taps, par, skip, gain, pick, cot, g2, d_low_t, chosen, *carried
    )
    d_late, lam, edge, grads, _ = backward(1, lam, edge, grads)
    lam, out_far = tie(lam, out_far)
    out_near = ring_middle(out_pieces, out_far)
    d_late, out_near = tie(d_late, out_near)
    out_last = ring_last(out_near, "tensor")
    *late_pieces, late_pushed, late_up = run_input_grad(me, 1, d_late, full, down_in, up_in, rank_t)
    lam, late_pieces = tie(lam, late_pieces)
    late_far = ring_first(late_pieces, "tensor")
    d_early, _, _, _, sent = backward(0, lam, edge, grads)
    both = ("fsdp", "context")
    d_early, late_far, out_last, sent = tie(d_early, late_far, out_last, sent)
    sent_out = lax.all_gather(sent, both, axis=0, tiled=True)
    late_near = ring_middle(late_pieces, late_far)
    branch = run_finish_branch(me, (out_pieces[4], *out_last), stats_all, up_out, nz)
    d_early, branch, late_near = tie(d_early, branch, late_near)
    late_last = ring_last(late_near, "tensor")
    branch_q = swapped(branch, "context")
    *early_pieces, early_pushed, early_up = run_input_grad(me, 0, d_early, full, down_in, up_in, rank_t)
    early_pieces, branch_q, late_last, early_pushed = tie(early_pieces, branch_q, late_last, early_pushed)
    early_far = ring_first(early_pieces, "tensor")
    early_far, early_pushed = tie(early_far, early_pushed)
    early_near = ring_middle(early_pieces, early_far)
    early_near, branch_q, early_pushed = tie(early_near, branch_q, early_pushed)
    early_last = ring_last(early_near, "tensor")
    pushed_all = shared(jnp.concatenate([early_pushed, late_pushed], 1), "tensor")
    d_in = jnp.concatenate([ring_total(early_pieces, early_last), ring_total(late_pieces, late_last)], 0).astype(BF)
    d_in, branch_q, pushed_all = tie(d_in.reshape(nz, share, width), branch_q, pushed_all)
    d_in_q = swapped(d_in, "context")
    out_near = ring_near(branch_q, "tensor")
    sent = run_grads(in_grads, mine, (*pushed_all, early_up, late_up, normed), width + 2 * inner, "in_grads")
    out_near, d_in_q, sent = tie(out_near, d_in_q, sent)
    sent_in = lax.all_gather(sent, both, axis=0, tiled=True)
    d_in_near = ring_near(d_in_q, "tensor")
    out_far2 = ring_far(out_near, "tensor")
    table = in_adapter_down.shape[0]
    out_tables = run_tables(sent_out, table, rank, (inner, width))
    d_in_near, out_far2, out_tables = tie(d_in_near, out_far2, out_tables)
    d_in_far = ring_far(d_in_near, "tensor")
    layer_out = run_finish(finish_out, me, (branch_q, *out_near, *out_far2), (tokens,), BF, "finish_out")
    in_tables = run_tables(sent_in, table, rank, (width, 2 * inner))
    in_tables, layer_out, d_in_far = tie(in_tables, layer_out, d_in_far)
    grad_tokens = run_finish(
        finish_grad, me, (d_in_q, *d_in_near, *d_in_far), (tokens, output_cotangent, input_norm_gain[None]), F32, "finish_grad"
    )
    return (
        layer_out,
        grad_tokens,
        in_tables[0].transpose(0, 2, 1),
        in_tables[1].reshape(table, rank, 2, inner),
        out_tables[0].transpose(0, 2, 1),
        out_tables[1],
    )


def solution(mesh):
    placed = (
        P("fsdp", "context", None),
        P("fsdp", "context", None),
        P("fsdp", "context"),
        P("fsdp"),
        P(),
        P(("fsdp", "context"), None, "tensor"),
        P(("fsdp", "context"), None),
        P(("fsdp", "context"), "tensor"),
        P(None, "tensor"),
        P("tensor"),
        P(),
        P(),
        P("tensor"),
        P("tensor"),
        P("tensor"),
        P("tensor"),
        P("tensor", ("fsdp", "context")),
        P(),
        P(None, None, None, "tensor"),
        P(None, "tensor", None),
        P(),
    )
    return jax.shard_map(
        per_device,
        mesh=mesh,
        in_specs=placed,
        out_specs=(
            P("fsdp", "context", None),
            P("fsdp", "context", None),
            P(),
            P(None, None, None, "tensor"),
            P(None, "tensor", None),
            P(),
        ),
        check_vma=False,
    )
```

```python
import functools

import jax
import jax.numpy as jnp
from jax import lax
from jax.experimental import pallas as pl
from jax.experimental.pallas import tpu as pltpu
from jax.sharding import PartitionSpec as P

INNER_CHANNELS = 3072
EPS_NORM = 1e-05
SUB = 128
NEG = -1e30
BF = jnp.bfloat16
F32 = jnp.float32
HIGHEST = lax.Precision.HIGHEST


def dot_nn(a, b):
    return lax.dot_general(a, b, (((1,), (0,)), ((), ())), preferred_element_type=F32)


def dot_nt(a, b):
    return lax.dot_general(a, b, (((1,), (1,)), ((), ())), preferred_element_type=F32)


def dot_tn(a, b):
    return lax.dot_general(a, b, (((0,), (0,)), ((), ())), preferred_element_type=F32)


def softplus(v):
    return jnp.maximum(v, 0.0) + jnp.log1p(jnp.exp(-jnp.abs(v)))


def lane(shape, dim):
    return lax.broadcasted_iota(jnp.int32, shape, dim)


def wide(column):
    return jnp.broadcast_to(column, (SUB, SUB))


def decays(raw, par_ref):
    rate = par_ref[1:2, :]
    shifted = raw + par_ref[0:1, :]
    dt = softplus(shifted)
    lower = (lane((SUB, SUB), 0) >= lane((SUB, SUB), 1)).astype(F32)
    run = jnp.dot(lower, dt * rate, precision=HIGHEST, preferred_element_type=F32)
    return shifted, dt, rate, run


def scan_forward(
    k, gx, marks_ref, taps_ref, bias_ref, par_ref, skip_ref, gain_ref, down_ref,
    y_ref, xc_ref, bc_ref, slope_ref, g2_ref, states_ref, stats_ref, state, ext,
):
    inner = skip_ref.shape[1]
    chans = ext.shape[1]
    rows = pl.ds(pl.multiple_of(k * SUB, SUB), SUB)

    def strip(ref, at):
        each = ref.shape[2] // SUB
        return ref[at // each, rows, (at % each) * SUB : (at % each + 1) * SUB].astype(F32)

    @pl.when(k == 0)
    def _():
        state[...] = jnp.zeros_like(state)
        ext[0:8, :] = jnp.zeros((8, chans), F32)

    @pl.when(k > 0)
    def _():
        ext[0:8, :] = ext[SUB : SUB + 8, :]

    for c in range(chans // SUB):
        ext[8 : SUB + 8, c * SUB : (c + 1) * SUB] = strip(gx, inner // SUB + c)
    near = [wide(marks_ref[:, k : k + 1]) for k in range(3)]
    linked = wide(marks_ref[:, 3:4])
    ending = wide(marks_ref[:, 4:5])
    ids = wide(marks_ref[:, 5:6])
    passing = marks_ref[0:1, 6:7]
    left = lane((SUB, SUB), 1) < 64

    def conv(sl):
        pre = bias_ref[:, sl] + taps_ref[3:4, sl] * ext[8 : SUB + 8, sl]
        for k in range(1, 4):
            pre = pre + taps_ref[3 - k : 4 - k, sl] * (ext[8 - k : SUB + 8 - k, sl] * near[k - 1])
        sig = jax.nn.sigmoid(pre)
        out = (pre * sig).astype(BF)
        slope_ref[:, sl] = (sig * (1.0 + pre * (1.0 - sig))).astype(BF)
        return out

    b_low = conv(slice(inner, inner + SUB))
    c_low = conv(slice(inner + SUB, inner + 2 * SUB))
    bc_ref[:, 0:SUB] = b_low
    bc_ref[:, SUB : 2 * SUB] = c_low
    b_turned = b_low.astype(F32).T.astype(BF)
    _, dt, _, run = decays(strip(gx, (inner + chans) // SUB), par_ref)
    run_rows = run.T
    allowed = (ids == ids.T) & (lane((SUB, SUB), 0) >= lane((SUB, SUB), 1))
    mask = jnp.where(allowed, 0.0, NEG)
    cross = dot_nt(c_low, b_low)
    square = jnp.zeros((SUB, SUB), F32)
    for p in range(inner // SUB):
        sl = slice(p * SUB, (p + 1) * SUB)
        x_low = conv(sl)
        xc_ref[:, sl] = x_low
        x = x_low.astype(F32)
        run0, run1 = wide(run[:, 2 * p : 2 * p + 1]), wide(run[:, 2 * p + 1 : 2 * p + 2])
        run_p = jnp.where(left, run0, run1)
        dt_p = jnp.where(left, wide(dt[:, 2 * p : 2 * p + 1]), wide(dt[:, 2 * p + 1 : 2 * p + 2]))
        m0 = (jnp.exp(run0 - run_rows[2 * p : 2 * p + 1, :] + mask) * cross).astype(BF)
        m1 = (jnp.exp(run1 - run_rows[2 * p + 1 : 2 * p + 2, :] + mask) * cross).astype(BF)
        xdt = x * dt_p
        split = jnp.concatenate([jnp.where(left, xdt, 0.0), jnp.where(left, 0.0, xdt)], 0).astype(BF)
        before = state[:, sl]
        before_low = before.astype(BF)
        states_ref[0, :, sl] = before_low
        y = dot_nn(jnp.concatenate([m0, m1], 1), split)
        y = y + jnp.exp(run_p) * linked * dot_nn(c_low, before_low) + skip_ref[:, sl] * x
        last = run_p[SUB - 1 : SUB, :]
        toward = (xdt * (jnp.exp(last - run_p) * ending)).astype(BF)
        state[:, sl] = (jnp.exp(last) * passing) * before + dot_nn(b_turned, toward)
        z = strip(gx, p)
        gated = y * (z * jax.nn.sigmoid(z))
        y_ref[:, sl] = y.astype(BF)
        g2_ref[:, sl] = (gated * gain_ref[:, sl]).astype(BF)
        square = square + gated * gated
    stats_ref[0:8, rows] = lane_rows(square)
    stats_ref[8:, rows] = dot_nt(down_ref[...], g2_ref[...])


def forward_all(
    me_ref, p0, p1, p2, p3, p4, norm_gain_ref, down_ref, up_ref, w_ref, w0_ref, w1_ref, out_down_ref,
    marks_ref, taps_ref, bias_ref, par_ref, skip_ref, gain_ref,
    normed_hbm, gx_hbm, rank_t_ref, stats_ref, y_ref, xc_ref, bc_ref, slope_ref, g2_ref, states_ref, out_ref,
    normed, gx, rank, state, ext, g2_all, held, sems,
):
    step = pl.program_id(0)
    tiles, length, tile = gx.shape
    copy_normed = pltpu.make_async_copy(normed, normed_hbm, sems.at[0])

    def copy_gx(j):
        return pltpu.make_async_copy(gx.at[j], gx_hbm.at[:, pl.ds(j * tile, tile)], sems.at[1 + j])

    @pl.when(step == 0)
    def _():
        ordered(me_ref, (p0, p1, p2, p3, p4), down_ref, normed, rank, rank_t_ref, norm_gain_ref)
        copy_normed.start()

    for j in range(tiles):

        @pl.when(step == j)
        def _():
            gx[j] = (dot_nn(normed[...], w_ref[...]) + dot_nn(rank[...], up_ref[...])).astype(BF)
            copy_gx(j).start()

    done = tiles + length // SUB

    @pl.when((step >= tiles) & (step < done))
    def _():
        scan_forward(
            step - tiles, gx, marks_ref, taps_ref, bias_ref, par_ref, skip_ref, gain_ref, out_down_ref,
            y_ref, xc_ref, bc_ref, slope_ref, g2_ref, states_ref, stats_ref, state, ext,
        )
        g2_all[pl.ds(pl.multiple_of((step - tiles) * SUB, SUB), SUB), :] = g2_ref[...]

    @pl.when(step >= done)
    def _():
        cut = w0_ref.shape[1]
        held[...] = (dot_nt(g2_all[:, 0:cut], w0_ref[...]) + dot_nt(g2_all[:, cut:], w1_ref[...])).astype(BF)
        owners, rows, _ = out_ref.shape
        share = 64
        for c in range(rows // share):
            for y in range(owners):
                at = (c * owners + y) * share
                out_ref[y, c * share : (c + 1) * share, :] = held[at : at + share, :]

    @pl.when(step == pl.num_programs(0) - 1)
    def _():
        copy_normed.wait()
        for j in range(tiles):
            copy_gx(j).wait()


def backward_half(
    me_ref, z_ref, dt_ref, xc_ref, bc_ref, slope_ref, y_ref, dn_ref, states_ref, s0_ref, s1_ref, s2_ref, s3_ref, marks_ref,
    taps_ref, par_ref, skip_ref, gain_ref, pick_ref, lam_in_ref, edge_in_ref,
    w_ref, down_ref, up_ref, rank_t_ref, *rest, with_grads,
):
    if with_grads:
        (cot0_ref, g20_ref, low0_ref, cot1_ref, g21_ref, low1_ref, q0_ref, q1_ref, q2_ref, q3_ref), rest = rest[:10], rest[10:]
        o0, o1, o2, o3, lam, edge_ref, up_grad_ref, grads_ref, *scratch = rest
        grads, *scratch = scratch
    else:
        o0, o1, o2, o3, lam, edge_ref, up_grad_ref, *scratch = rest
    d_all, low, pushed, held, ext, to_dt, to_run, to_end = scratch
    step = pl.program_id(0)
    steps = d_all.shape[0] // SUB
    if with_grads:

        @pl.when(step == 0)
        def _():
            grads[...] = jnp.zeros_like(grads)

        @pl.when(step < steps)
        def _():
            cut = g20_ref.shape[1]
            for stats, low_t_ref, cot_ref, g2_ref in (
                (s0_ref[...] + s1_ref[...] + s2_ref[...] + s3_ref[...], low0_ref, cot0_ref, g20_ref),
                (q0_ref[...] + q1_ref[...] + q2_ref[...] + q3_ref[...], low1_ref, cot1_ref, g21_ref),
            ):
                rn_row = lax.rsqrt(stats[0:1, :] / INNER_CHANNELS + EPS_NORM)
                grads[:, 0:cut] += dot_nn((low_t_ref[...].astype(F32) * rn_row).astype(BF), g2_ref[...])
                grads[:, cut:] += dot_nn((stats[8:, :] * rn_row).astype(BF), cot_ref[...])

        @pl.when(step == steps)
        def _():
            grads_ref[...] = grads[...].astype(BF)

    @pl.when(step < steps)
    def _():
        at = pl.multiple_of((steps - 1 - step) * SUB, SUB)
        scan_backward(
            step, d_all.at[pl.ds(at, SUB), :], z_ref, dt_ref, xc_ref, bc_ref, slope_ref, y_ref, dn_ref, states_ref,
            (s0_ref, s1_ref, s2_ref, s3_ref), marks_ref, taps_ref, par_ref, skip_ref, gain_ref, pick_ref, lam_in_ref, edge_in_ref,
            lam, ext, to_dt, to_run, to_end,
        )
        gate = d_all[pl.ds(at, SUB), 0 : up_ref.shape[1]]
        part = dot_nt(gate, up_ref[...])
        rank = part.shape[1]
        low[pl.ds(at, SUB), :] = part.astype(BF)
        part = jnp.concatenate([part, jnp.zeros((SUB, SUB - rank), F32)], 1)
        pushed[:, pl.ds(at, SUB)] = part.T[0:rank, :].astype(BF)
        up_grad = dot_nn(rank_t_ref[...], gate)

        @pl.when(step == 0)
        def _():
            up_grad_ref[...] = up_grad

        @pl.when(step > 0)
        def _():
            up_grad_ref[...] += up_grad

    @pl.when(step == steps - 1)
    def _():
        edge_ref[...] = ext[0:8, :]

    @pl.when(step >= steps)
    def _():
        held[...] = (dot_nt(d_all[...], w_ref[...]) + dot_nn(low[...], down_ref[...])).astype(BF)
        deal(me_ref[0], held, (o0, o1, o2, o3))

    for out in (o0, o1, o2, o3):

        @pl.when(step == steps)
        def _():
            out[out.shape[0] - pushed.shape[0] :, :] = pushed[...]

        @pl.when(step > steps)
        def _():
            out[out.shape[0] - pushed.shape[0] :, :] = jnp.zeros_like(pushed)


def scan_backward(
    step, da_ref, z_ref, dt_ref, xc_ref, bc_ref, slope_ref, y_ref, dn_ref, states_ref, stats_refs, marks_ref,
    taps_ref, par_ref, skip_ref, gain_ref, pick_ref, lam_in_ref, edge_in_ref,
    lam, ext, to_dt, to_run, to_end,
):
    inner = z_ref.shape[1]
    chans = ext.shape[1]

    @pl.when(step == 0)
    def _():
        lam[...] = lam_in_ref[...]
        ext[SUB : SUB + 8, :] = edge_in_ref[...]

    @pl.when(step > 0)
    def _():
        ext[SUB : SUB + 8, :] = ext[0:8, :]

    linked = wide(marks_ref[:, 3:4])
    ending = wide(marks_ref[:, 4:5])
    ids = wide(marks_ref[:, 5:6])
    passing = marks_ref[0:1, 6:7]
    later = [wide(marks_ref[:, 7 + k : 8 + k]) for k in range(3)]
    left = lane((SUB, SUB), 1) < 64
    stats = stats_refs[0][...] + stats_refs[1][...] + stats_refs[2][...] + stats_refs[3][...]
    rn_row = lax.rsqrt(stats[0:1, :] / INNER_CHANNELS + EPS_NORM)
    rn = jnp.broadcast_to(rn_row, (SUB, SUB)).T
    kappa = jnp.broadcast_to(rn_row * rn_row * rn_row * stats[1:2, :] / INNER_CHANNELS, (SUB, SUB)).T
    shifted, dt, rate, run = decays(dt_ref[...].astype(F32), par_ref)
    run_rows = run.T
    b_low, c_low = bc_ref[:, 0:SUB], bc_ref[:, SUB : 2 * SUB]
    c_turned = c_low.astype(F32).T.astype(BF)
    allowed = (ids == ids.T) & (lane((SUB, SUB), 0) <= lane((SUB, SUB), 1))
    mask = jnp.where(allowed, 0.0, NEG)
    cross = dot_nt(b_low, c_low)
    d_cross = jnp.zeros((SUB, SUB), F32)
    d_b = jnp.zeros((SUB, SUB), F32)
    d_c = jnp.zeros((SUB, SUB), F32)
    for p in range(inner // SUB):
        sl = slice(p * SUB, (p + 1) * SUB)
        z = z_ref[:, sl].astype(F32)
        sig = jax.nn.sigmoid(z)
        silu = z * sig
        y = y_ref[:, sl].astype(F32)
        d_gated = rn * (dn_ref[:, sl].astype(F32) * gain_ref[:, sl]) - kappa * (y * silu)
        da_ref[:, sl] = (d_gated * y * sig * (1.0 + z * (1.0 - sig))).astype(BF)
        dy = d_gated * silu
        x = xc_ref[:, sl].astype(F32)
        run0, run1 = wide(run[:, 2 * p : 2 * p + 1]), wide(run[:, 2 * p + 1 : 2 * p + 2])
        run_p = jnp.where(left, run0, run1)
        dt_p = jnp.where(left, wide(dt[:, 2 * p : 2 * p + 1]), wide(dt[:, 2 * p + 1 : 2 * p + 2]))
        l0 = jnp.exp(run_rows[2 * p : 2 * p + 1, :] - run0 + mask)
        l1 = jnp.exp(run_rows[2 * p + 1 : 2 * p + 2, :] - run1 + mask)
        xdt = x * dt_p
        x_split = jnp.concatenate([jnp.where(left, xdt, 0.0), jnp.where(left, 0.0, xdt)], 0).astype(BF)
        dy_split = jnp.concatenate([jnp.where(left, dy, 0.0), jnp.where(left, 0.0, dy)], 0).astype(BF)
        d_m = dot_nt(x_split, dy.astype(BF))
        d_cross = d_cross + l0 * d_m[0:SUB] + l1 * d_m[SUB : 2 * SUB]
        m = jnp.concatenate([l0 * cross, l1 * cross], 1).astype(BF)
        lam_p = lam[:, sl]
        lam_low = lam_p.astype(BF)
        last = run_p[SUB - 1 : SUB, :]
        toward = jnp.exp(last - run_p) * ending
        carried = toward * dot_nn(b_low, lam_low)
        d_xt = dot_nn(m, dy_split) + carried
        skip = skip_ref[:, sl]
        ext[0:SUB, sl] = (dt_p * d_xt + skip * dy) * slope_ref[:, sl].astype(F32)
        x_dx = x * d_xt
        to_dt[:, sl] = x_dx
        to_run[:, sl] = dy * (y - skip * x) - dt_p * x_dx
        reached = (jnp.exp(run_p) * linked * dy).astype(BF)
        before_low = states_ref[0, :, sl]
        keep = jnp.exp(last) * passing
        to_end[0:1, sl] = jnp.sum(xdt * carried, 0, keepdims=True) + keep * jnp.sum(
            lam_p * before_low.astype(F32), 0, keepdims=True
        )
        d_b = d_b + dot_nt((xdt * toward).astype(BF), lam_low)
        d_c = d_c + dot_nt(reached, before_low)
        lam[:, sl] = keep * lam_p + dot_nn(c_turned, reached)
    d_cross_low = d_cross.astype(BF)
    d_b = d_b + dot_nn(d_cross_low, c_low)
    d_c = d_c + dot_nn(d_cross.T.astype(BF), b_low)
    ext[0:SUB, inner : inner + SUB] = d_b * slope_ref[:, inner : inner + SUB].astype(F32)
    ext[0:SUB, inner + SUB : chans] = d_c * slope_ref[:, inner + SUB : chans].astype(F32)

    def by_head(v):
        high = v.astype(BF)
        return dot_nn(high, pick_ref[...]) + dot_nn((v - high.astype(F32)).astype(BF), pick_ref[...])

    d_run = by_head(to_run[...])
    d_end = by_head(to_end[...])[0:1, :]
    d_run = d_run + jnp.where(lane((SUB, SUB), 0) == SUB - 1, d_end, 0.0)
    upper = (lane((SUB, SUB), 0) <= lane((SUB, SUB), 1)).astype(F32)
    d_log = jnp.dot(upper, d_run, precision=HIGHEST, preferred_element_type=F32)
    d_dt = by_head(to_dt[...]) + rate * d_log
    da_ref[:, inner + chans : inner + chans + SUB] = (d_dt * jax.nn.sigmoid(shifted)).astype(BF)
    for s in range(chans // SUB):
        sl = slice(s * SUB, (s + 1) * SUB)
        acc = taps_ref[3:4, sl] * ext[0:SUB, sl]
        for k in range(1, 4):
            acc = acc + taps_ref[3 - k : 4 - k, sl] * (ext[k : SUB + k, sl] * later[k - 1])
        da_ref[:, inner + s * SUB : inner + (s + 1) * SUB] = acc.astype(BF)

def whole(a):
    return pl.BlockSpec(a.shape, lambda i, *_: (0,) * a.ndim)


def params(mib=60):
    return pltpu.CompilerParams(vmem_limit_bytes=mib << 20)


def takes(us):
    return pl.CostEstimate(flops=us * 100_000_000, bytes_accessed=us * 300_000, transcendentals=0)


def assemble(me, pieces, out_ref, block):
    own, behind, ahead, far_low, far_high = pieces
    chunks, share = own.shape[0], own.shape[1]
    for c in range(chunks):
        far = far_low[c] if c < chunks // 2 else far_high[c - chunks // 2]
        for d, part in ((0, own[c]), (1, behind[c]), (2, far), (3, ahead[c])):
            at = pl.multiple_of(c * block + ((me + 4 - d) % 4) * share, share)
            out_ref[pl.ds(at, share), :] = part


def low_products(rows_ref, down_ref, rank_ref, rank_t_ref):
    low = dot_nt(rows_ref[...], down_ref[...])
    rank = low.shape[1]
    rank_ref[...] = low.astype(BF)
    low = jnp.concatenate([low, jnp.zeros((low.shape[0], SUB - rank), F32)], 1)
    for k in range(low.shape[0] // SUB):
        here = slice(k * SUB, (k + 1) * SUB)
        rank_t_ref[:, here] = low[here, :].T[0:rank, :].astype(BF)


def ordered(me_ref, pieces, down_ref, rows_ref, rank_ref, rank_t_ref, gain_ref):
    assemble(me_ref[0], pieces, rows_ref, 4 * pieces[0].shape[1])
    for k in range(rows_ref.shape[0] // 64):
        here = slice(k * 64, (k + 1) * 64)
        t = rows_ref[here, :].astype(F32)
        rms = lax.rsqrt(jnp.mean(t * t, -1, keepdims=True) + EPS_NORM)
        rows_ref[here, :] = (t * rms * gain_ref[...]).astype(BF)
    low_products(rows_ref, down_ref, rank_ref, rank_t_ref)


def lane_rows(v):
    return lax.dot_general(
        jnp.ones((8, v.shape[1]), F32), v, (((1,), (1,)), ((), ())), precision=HIGHEST, preferred_element_type=F32
    )


def deal(me, held, outs):
    share = 64
    for c in range(held.shape[0] // (4 * share)):
        for d, out in enumerate(outs):
            at = pl.multiple_of((c * 4 + (me + d) % 4) * share, share)
            out[c * share : (c + 1) * share, :] = held[pl.ds(at, share), :]


def one(a):
    return pl.BlockSpec(a.shape, lambda i, *_: (0,) * a.ndim, pipeline_mode=pl.Buffered(1))


def kept(*shape):
    return pl.BlockSpec(shape, lambda i, *_: (0,) * len(shape))


def run_forward(me, pieces, norm_gain, down, up, weights, out_down, marks, taps, bias, par, skip, gain):
    chunks, share, width = pieces[0].shape
    length = chunks * 4 * share
    inner, chans = skip.shape[1], taps.shape[1]
    rank, columns = up.shape
    tile = 512
    tiles, steps, out_tiles = columns // tile, length // SUB, width // tile
    any_space = pl.BlockSpec(memory_space=pl.ANY)
    sub = lambda i: jnp.clip(i - tiles, 0, steps - 1)
    scan = lambda cols: pl.BlockSpec((SUB, cols), lambda i, me: (sub(i), 0))
    last = lambda i: jnp.maximum(i - tiles - steps, 0)
    at_out = 2 * (weights.shape[1] - inner) // inner
    return pl.pallas_call(
        forward_all,
        grid_spec=pltpu.PrefetchScalarGridSpec(
            num_scalar_prefetch=1,
            grid=(tiles + steps + out_tiles,),
            in_specs=[
                *[one(p) for p in pieces], one(norm_gain), one(down),
                pl.BlockSpec((rank, tile), lambda i, me: (0, jnp.minimum(i, tiles - 1))),
                pl.BlockSpec((width, tile), lambda i, me: (0, jnp.minimum(i, tiles - 1))),
                pl.BlockSpec((tile, inner // 2), lambda i, me: (last(i), at_out)),
                pl.BlockSpec((tile, inner // 2), lambda i, me: (last(i), at_out + 1)),
                one(out_down), scan(marks.shape[1]), one(taps), one(bias), one(par), one(skip), one(gain),
            ],
            out_specs=[
                any_space, any_space, kept(rank, length), kept(8 + rank, length),
                scan(inner), scan(inner), scan(2 * SUB), scan(chans), scan(inner),
                pl.BlockSpec((1, SUB, inner), lambda i, me: (sub(i), 0, 0)),
                pl.BlockSpec((4, length // 4, tile), lambda i, me: (0, 0, last(i))),
            ],
            scratch_shapes=[
                pltpu.VMEM((length, width), BF),
                pltpu.VMEM((tiles, length, tile), BF),
                pltpu.VMEM((length, rank), BF),
                pltpu.VMEM((SUB, inner), F32),
                pltpu.VMEM((SUB + 8, chans), F32),
                pltpu.VMEM((length, inner), BF),
                pltpu.VMEM((length, tile), BF),
                pltpu.SemaphoreType.DMA((1 + tiles,)),
            ],
        ),
        out_shape=[
            jax.ShapeDtypeStruct((length, width), BF),
            jax.ShapeDtypeStruct((length, columns), BF),
            jax.ShapeDtypeStruct((rank, length), BF),
            jax.ShapeDtypeStruct((8 + rank, length), F32),
            jax.ShapeDtypeStruct((length, inner), BF),
            jax.ShapeDtypeStruct((length, inner), BF),
            jax.ShapeDtypeStruct((length, 2 * SUB), BF),
            jax.ShapeDtypeStruct((length, chans), BF),
            jax.ShapeDtypeStruct((length, inner), BF),
            jax.ShapeDtypeStruct((steps, SUB, inner), BF),
            jax.ShapeDtypeStruct((4, length // 4, width), BF),
        ],
        compiler_params=params(),
        cost_estimate=takes(30),
        name="forward_all",
    )(me, *pieces, norm_gain, down, up, weights, weights, weights, out_down, marks, taps, bias, par, skip, gain)


def pull_back(
    me_ref, p0, p1, p2, p3, up_ref, w_ref, g2_ref, part_ref, down_ref,
    dn_ref, stats_ref, cot_hbm, low_t_ref,
    cot, low, dots, sem,
):
    step = pl.program_id(0)
    copy_cot = pltpu.make_async_copy(cot, cot_hbm, sem)

    @pl.when(step == 0)
    def _():
        chunks, share, _ = p0.shape
        for c in range(chunks):
            for d, part in enumerate((p0, p1, p2, p3)):
                at = pl.multiple_of((c * 4 + (me_ref[0] + 4 - d) % 4) * share, share)
                cot[pl.ds(at, share), :] = part[(me_ref[1] + 4 - c) % 4]
        copy_cot.start()
        low_products(cot, up_ref, low, low_t_ref)
        dots[...] = jnp.zeros_like(dots)

    dn = dot_nn(cot[...], w_ref[...]) + dot_nn(low[...], down_ref[...])
    dn_ref[...] = dn.astype(BF)
    both = dn * g2_ref[...].astype(F32)
    total = dots[...]
    for k in range(both.shape[1] // SUB):
        total = total + both[:, k * SUB : (k + 1) * SUB]
    dots[...] = total

    @pl.when(step == pl.num_programs(0) - 1)
    def _():
        first = lane((8, stats_ref.shape[1]), 0) == 0
        stats_ref[0:8, :] = jnp.where(first, part_ref[0:8, :], lane_rows(dots[...]))
        stats_ref[8:, :] = part_ref[8:, :]
        copy_cot.wait()


def run_pull_back(me, pieces, weights, up, g2, part, down, tile=384):
    width = pieces[0].shape[2]
    length, inner = g2.shape
    rank = down.shape[0]
    first = (weights.shape[1] - inner) // tile
    return pl.pallas_call(
        pull_back,
        grid_spec=pltpu.PrefetchScalarGridSpec(
            num_scalar_prefetch=1,
            grid=(inner // tile,),
            in_specs=[
                *[one(p) for p in pieces], one(up),
                pl.BlockSpec((width, tile), lambda j, me: (0, first + j)),
                pl.BlockSpec((length, tile), lambda j, me: (0, j)),
                one(part),
                pl.BlockSpec((rank, tile), lambda j, me: (0, j)),
            ],
            out_specs=[
                pl.BlockSpec((length, tile), lambda j, me: (0, j)), kept(*part.shape),
                pl.BlockSpec(memory_space=pl.ANY), kept(rank, length),
            ],
            scratch_shapes=[
                pltpu.VMEM((length, width), BF),
                pltpu.VMEM((length, rank), BF),
                pltpu.VMEM((length, SUB), F32),
                pltpu.SemaphoreType.DMA,
            ],
        ),
        out_shape=[
            jax.ShapeDtypeStruct((length, inner), BF),
            jax.ShapeDtypeStruct(part.shape, F32),
            jax.ShapeDtypeStruct((length, width), BF),
            jax.ShapeDtypeStruct((rank, length), BF),
        ],
        compiler_params=params(),
        cost_estimate=takes(8),
        name="pull_back",
    )(me, *pieces, up, weights, g2, part, down)


def dealt(rows, width, tile, at):
    spec = pl.BlockSpec((rows, tile), lambda j, me: (0, at(j)))
    return [spec] * 4, [jax.ShapeDtypeStruct((rows, width), BF)] * 4


def run_backward(
    me, half, gx, xc, bc, slope, y, dn, states, stats, marks, taps, par, skip, gain, pick,
    weights, down, up, rank_t, lam, edge, cot=None, g2=None, low_t=None,
):
    length = gx.shape[0] // 2
    inner, chans, width = skip.shape[1], taps.shape[1], weights.shape[0]
    rank = down.shape[0]
    steps = length // SUB
    tile = 512
    assert tile == length
    top = (half + 1) * steps - 1
    sub = lambda i: jnp.maximum(top - i, half * steps)
    col = lambda i: jnp.maximum(i - steps, 0)
    row = lambda cols, at=0: pl.BlockSpec((SUB, cols), lambda i, me, at=at: (sub(i), at))
    lanes = lambda n: pl.BlockSpec((n, SUB), lambda i, me: (0, sub(i)))
    total = inner + chans + SUB
    specs, shapes = dealt(length // 4 + rank, width, tile, col)
    with_grads = cot is not None
    args = [
        gx, gx, xc, bc, slope, y, dn, states, *stats, marks, taps, par, skip, gain, pick, lam, edge,
        weights, down, up, rank_t,
    ]
    in_specs = [
        row(inner), row(SUB, (inner + chans) // SUB), row(inner), row(2 * SUB), row(chans), row(inner), row(inner),
        pl.BlockSpec((1, SUB, inner), lambda i, me: (sub(i), 0, 0)),
        *[lanes(stats[0].shape[0])] * 4,
        row(marks.shape[1]), one(taps), one(par), one(skip), one(gain), one(pick), one(lam), one(edge),
        pl.BlockSpec((tile, total), lambda i, me: (col(i), 0)),
        pl.BlockSpec((rank, tile), lambda i, me: (0, col(i))),
        one(up), lanes(rank),
    ]
    out_specs = [*specs, kept(*lam.shape), kept(*edge.shape), kept(*up.shape)]
    out_shape = [
        *shapes,
        jax.ShapeDtypeStruct(lam.shape, F32),
        jax.ShapeDtypeStruct(edge.shape, F32),
        jax.ShapeDtypeStruct(up.shape, F32),
    ]
    scratch = [
        pltpu.VMEM((length, total), BF),
        pltpu.VMEM((length, rank), BF),
        pltpu.VMEM((rank, length), BF),
        pltpu.VMEM((length, tile), BF),
        pltpu.VMEM((SUB + 8, chans), F32),
        pltpu.VMEM((SUB, inner), F32),
        pltpu.VMEM((SUB, inner), F32),
        pltpu.VMEM((8, inner), F32),
    ]
    if with_grads:
        other = lambda i: sub(i) - steps
        args += [cot, g2, low_t, cot, g2, low_t, *stats]
        in_specs += [row(width), row(inner), lanes(rank)]
        in_specs += [
            pl.BlockSpec((SUB, width), lambda i, me: (other(i), 0)),
            pl.BlockSpec((SUB, inner), lambda i, me: (other(i), 0)),
            pl.BlockSpec((rank, SUB), lambda i, me: (0, other(i))),
            *[pl.BlockSpec((stats[0].shape[0], SUB), lambda i, me: (0, other(i)))] * 4,
        ]
        out_specs.append(kept(rank, inner + width))
        out_shape.append(jax.ShapeDtypeStruct((rank, inner + width), BF))
        scratch = [pltpu.VMEM((rank, inner + width), F32), *scratch]
    return pl.pallas_call(
        functools.partial(backward_half, with_grads=with_grads),
        grid_spec=pltpu.PrefetchScalarGridSpec(
            num_scalar_prefetch=1,
            grid=(steps + width // tile,),
            in_specs=in_specs,
            out_specs=out_specs,
            scratch_shapes=scratch,
        ),
        out_shape=out_shape,
        compiler_params=params(),
        cost_estimate=takes(19),
        name="backward_half",
    )(me, *args)


def place(me_ref, pieces, out):
    own, behind, ahead, far_low, far_high = pieces
    share = own.shape[1]
    y, turn = me_ref[0], (me_ref[1] + 4 - pl.program_id(0)) % 4
    for d, part in ((0, own), (1, behind), (3, ahead)):
        out[pl.ds(pl.multiple_of(((y + 4 - d) % 4) * share, share), share), :] = part[0]
    far = pl.ds(pl.multiple_of(((y + 2) % 4) * share, share), share)

    @pl.when(turn < 2)
    def _():
        out[far, :] = far_low[0]

    @pl.when(turn >= 2)
    def _():
        out[far, :] = far_high[0]


def columns_of(stats_refs, cols):
    total = stats_refs[0][...] + stats_refs[1][...] + stats_refs[2][...] + stats_refs[3][...]
    rows, length = total.shape
    total = jnp.concatenate([total, jnp.zeros((SUB - rows, length), F32)], 0)
    for k in range(length // SUB):
        cols[k * SUB : (k + 1) * SUB, :] = total[:, k * SUB : (k + 1) * SUB].T
    return total


def finish_branch(me_ref, sum_ref, s0, s1, s2, s3, up_ref, o0, o1, o2, o3, cols):
    columns_of((s0, s1, s2, s3), cols)
    share = o0.shape[0]
    rank = up_ref.shape[0]
    for d, out in enumerate((o0, o1, o2, o3)):
        c = (me_ref[1] + d) % 4
        mine = cols[pl.ds(pl.multiple_of((c * 4 + me_ref[0]) * share, share), share), :]
        rn = lax.rsqrt(mine[:, 0:1] / INNER_CHANNELS + EPS_NORM)
        low = (mine[:, 8 : 8 + rank] * rn).astype(BF)
        total = sum_ref[pl.ds(pl.multiple_of(c * share, share), share), :].astype(F32)
        out[...] = (total * rn + dot_nn(low, up_ref[...])).astype(BF)


def run_to_context(kernel, me, args, share, width, scratch, name):
    return pl.pallas_call(
        kernel,
        grid_spec=pltpu.PrefetchScalarGridSpec(
            num_scalar_prefetch=1,
            grid=(1,),
            in_specs=[one(a) for a in args],
            out_specs=[kept(share, width)] * 4,
            scratch_shapes=[scratch],
        ),
        out_shape=[jax.ShapeDtypeStruct((share, width), BF)] * 4,
        compiler_params=params(),
        cost_estimate=takes(3),
        name=name,
    )(me, *args)


def in_grads(me_ref, *refs):
    early, late, (up0_ref, up1_ref, normed_ref, done_ref), outs, (sent_ref, held) = (
        refs[:4], refs[4:8], refs[8:12], refs[12:16], refs[16:]
    )
    half = held.shape[0] // 2
    rank, length = up0_ref.shape[0], normed_ref.shape[0]
    added = lambda refs, *at: sum(r[at].astype(F32) for r in refs[1:]) + refs[0][at].astype(F32)
    for at, parts in ((0, early), (half, late)):
        held[at : at + half, :] = added(parts, slice(0, half)).astype(BF)
    share = outs[0].shape[0]
    for d, out in enumerate(outs):
        c = (me_ref[1] + d) % 4
        out[...] = held[pl.ds(pl.multiple_of(c * share, share), share), :]
    ranks = [added(parts, slice(half, half + rank), slice(0, length // 2)) for parts in (early, late)]
    width, inner2, done = normed_ref.shape[1], up0_ref.shape[1], done_ref.shape[1]
    sent_ref[:, 0:width] = dot_nn(jnp.concatenate(ranks, 1).astype(BF), normed_ref[...]).astype(BF)
    sent_ref[:, width : width + inner2] = (up0_ref[...] + up1_ref[...]).astype(BF)
    sent_ref[:, width + inner2 : width + inner2 + done] = done_ref[...]
    sent_ref[:, width + inner2 + done :] = (lane((rank, SUB), 1) == me_ref[2]).astype(BF)


def run_in_grads(me, early, late, up0, up1, normed, done, share):
    rank, inner2 = up0.shape
    width = normed.shape[1]
    columns = width + inner2 + done.shape[1] + SUB
    args = (*early, *late, up0, up1, normed, done)
    return pl.pallas_call(
        in_grads,
        grid_spec=pltpu.PrefetchScalarGridSpec(
            num_scalar_prefetch=1,
            grid=(1,),
            in_specs=[one(a) for a in args],
            out_specs=[*[kept(share, width)] * 4, kept(rank, columns)],
            scratch_shapes=[pltpu.VMEM((4 * share, width), BF)],
        ),
        out_shape=[*[jax.ShapeDtypeStruct((share, width), BF)] * 4, jax.ShapeDtypeStruct((rank, columns), BF)],
        compiler_params=params(),
        cost_estimate=takes(3),
        name="in_grads",
    )(me, *args)


def finish_out(me_ref, p0, p1, p2, p3, p4, tokens_ref, out_ref, held):
    place(me_ref, (p0, p1, p2, p3, p4), held)
    out_ref[0] = (tokens_ref[0].astype(F32) + held[...].astype(F32)).astype(BF)


def finish_grad(me_ref, p0, p1, p2, p3, p4, tokens_ref, cot_ref, gain_ref, out_ref, held):
    place(me_ref, (p0, p1, p2, p3, p4), held)
    t = tokens_ref[0].astype(F32)
    rms = lax.rsqrt(jnp.mean(t * t, -1, keepdims=True) + EPS_NORM)
    pulled = held[...].astype(F32) * gain_ref[...]
    slope = rms * rms * rms * jnp.mean(pulled * t, -1, keepdims=True)
    out_ref[0] = rms * pulled - t * slope + cot_ref[0].astype(F32)


def piece_specs(pieces):
    share, width = pieces[0].shape[1:]
    half = pieces[0].shape[0] // 2
    turn = lambda s, me: (me[1] + 4 - s) % 4
    full = pl.BlockSpec((1, share, width), lambda s, me: (turn(s, me), 0, 0))
    return [
        full, full, full,
        pl.BlockSpec((1, share, width), lambda s, me: (jnp.minimum(turn(s, me), half - 1), 0, 0)),
        pl.BlockSpec((1, share, width), lambda s, me: (jnp.maximum(turn(s, me) - half, 0), 0, 0)),
    ]


def run_finish(kernel, me, pieces, extra, dtype, name):
    seqs, block, width = extra[0].shape
    seq = pl.BlockSpec((1, block, width), lambda s, me: (s, 0, 0))
    specs = [seq if a.ndim == 3 else whole(a) for a in extra]
    return pl.pallas_call(
        kernel,
        grid_spec=pltpu.PrefetchScalarGridSpec(
            num_scalar_prefetch=1,
            grid=(seqs,),
            in_specs=[*piece_specs(pieces), *specs],
            out_specs=seq,
            scratch_shapes=[pltpu.VMEM((block, width), BF)],
        ),
        out_shape=jax.ShapeDtypeStruct((seqs, block, width), dtype),
        compiler_params=params(30),
        cost_estimate=takes(5),
        name=name,
    )(me, *[pltpu.with_memory_space_constraint(a, pltpu.HBM) if a.ndim == 3 else a for a in (*pieces, *extra)])


def fill_tables(all_ref, *outs):
    table, rank = outs[0].shape[0], outs[0].shape[1]
    rows, columns = all_ref.shape
    spread = (lane((SUB, table * rank), 0) == lane((SUB, table * rank), 1) // rank).astype(BF)
    place = dot_nn(all_ref[:, columns - SUB :], spread)
    same = lane((rows, table * rank), 0) % rank == lane((rows, table * rank), 1) % rank
    place = jnp.where(same, place, 0.0).T.astype(BF)
    at = 0
    for out in outs:
        slots = out.shape[2:-1] or (1,)
        for slot in range(slots[0]):
            here = dot_nn(place, all_ref[:, at : at + out.shape[-1]])
            for a in range(table):
                if out.ndim == 3:
                    out[a] = here[a * rank : (a + 1) * rank, :]
                else:
                    out[a, :, slot, :] = here[a * rank : (a + 1) * rank, :]
            at += out.shape[-1]


def run_tables(everything, table, rank, widths):
    return pl.pallas_call(
        fill_tables,
        out_shape=[jax.ShapeDtypeStruct((table, rank, *w), F32) for w in widths],
        compiler_params=params(),
        cost_estimate=takes(3),
        name="fill_tables",
    )(everything)


def shifted_by(value, axis, distance):
    size = lax.axis_size(axis)
    return lax.ppermute(value, axis, [(i, (i + distance) % size) for i in range(size)])


def tie(*values):
    return lax.optimization_barrier(values)


def ring_near(own, axis):
    return shifted_by(own, axis, 1), shifted_by(own, axis, -1)


def ring_far(near, axis):
    half = near[0].shape[0] // 2
    return shifted_by(near[0][:half], axis, 1), shifted_by(near[1][half:], axis, -1)


def delivered(pieces, axis):
    return [pieces[0]] + [shifted_by(p, axis, d) for d, p in enumerate(pieces) if d]


def added(parts):
    return sum(p.astype(F32) for p in parts[1:]) + parts[0].astype(F32)


def shared(value, axis):
    return [value] + [shifted_by(value, axis, d) for d in range(1, lax.axis_size(axis))]


def swapped(value, axis):
    return lax.all_to_all(value, axis, 0, 0, tiled=True)


def per_device(
    tokens, output_cotangent, segments, sequence_adapter, input_norm_gain,
    gate_x_projection_weight, bc_projection_weight, step_projection_weight,
    x_convolution_taps, x_convolution_bias, bc_convolution_taps, bc_convolution_bias,
    step_size_bias, log_decay_rate, head_skip_gain, gated_norm_gain, output_projection_weight,
    in_adapter_down, in_adapter_up, out_adapter_down, out_adapter_up,
):
    seqs, block, width = tokens.shape
    inner = gate_x_projection_weight.shape[2]
    heads = step_projection_weight.shape[1]
    rank = in_adapter_down.shape[2]
    ny, nz = lax.axis_size("tensor"), lax.axis_size("context")
    my, mz = lax.axis_index("tensor"), lax.axis_index("context")
    me = jnp.stack([my, mz]).astype(jnp.int32)
    length = block * nz
    share = block // ny

    rows = gate_x_projection_weight.shape[0]
    packed = jnp.concatenate(
        [
            gate_x_projection_weight.reshape(rows, 2 * inner),
            bc_projection_weight,
            step_projection_weight,
            jnp.zeros((rows, SUB - heads), BF),
            output_projection_weight.T,
        ],
        1,
    )
    full = lax.all_gather(packed, ("fsdp", "context"), axis=0, tiled=True)

    quarter = lambda a: lax.dynamic_slice_in_dim(a, my * share, share, 1)
    tokens_q = quarter(tokens)
    later = (
        segments, sequence_adapter, x_convolution_taps, x_convolution_bias, bc_convolution_taps, bc_convolution_bias,
        step_size_bias, log_decay_rate, head_skip_gain, gated_norm_gain,
        in_adapter_down, in_adapter_up, out_adapter_down, out_adapter_up,
    )
    tokens_s, cot_later, later = tie(swapped(tokens_q, "context"), output_cotangent, later)
    cot_q = [
        lax.dynamic_slice(cot_later, ((mz + d) % nz, my * share, 0), (1, share, width)) for d in range(nz)
    ]
    (
        segments, sequence_adapter, x_convolution_taps, x_convolution_bias, bc_convolution_taps, bc_convolution_bias,
        step_size_bias, log_decay_rate, head_skip_gain, gated_norm_gain,
        in_adapter_down, in_adapter_up, out_adapter_down, out_adapter_up,
    ) = later
    tokens_near = ring_near(tokens_s, "tensor")

    seg = swapped(segments, "context").reshape(length)
    mine = lax.dynamic_index_in_dim(sequence_adapter, mz, 0, False)
    down_in = lax.dynamic_index_in_dim(in_adapter_down.transpose(0, 2, 1), mine, 0, False)
    up_in = lax.dynamic_index_in_dim(in_adapter_up, mine, 0, False).reshape(rank, 2 * inner)
    down_out = lax.dynamic_index_in_dim(out_adapter_down.transpose(0, 2, 1), mine, 0, False)
    up_out = lax.dynamic_index_in_dim(out_adapter_up, mine, 0, False)

    pos = jnp.arange(length)
    by_sub = seg.reshape(-1, SUB)
    last = by_sub[:, -1]
    before = jnp.concatenate([jnp.full((1,), -1, seg.dtype), last[:-1]])
    back = [jnp.where(pos >= k, jnp.roll(seg, k) == seg, False) for k in (1, 2, 3)]
    forth = [jnp.where(pos < length - k, jnp.roll(seg, -k) == seg, False) for k in (1, 2, 3)]
    same = lambda v: jnp.broadcast_to(v[:, None], by_sub.shape)
    kinds = [
        *back,
        (by_sub == same(before)).reshape(-1),
        (by_sub == same(last)).reshape(-1),
        seg,
        same(last == before).reshape(-1),
        *forth,
    ]
    marks = jnp.stack([c.astype(F32) for c in kinds] + [jnp.zeros((length,), F32)] * 6, -1)

    taps = jnp.concatenate([x_convolution_taps, bc_convolution_taps], 1)
    conv_bias = jnp.concatenate([x_convolution_bias, bc_convolution_bias], 0)[None]
    par = jnp.zeros((8, SUB), F32)
    par = par.at[0, :heads].set(step_size_bias).at[1, :heads].set(-jnp.exp(log_decay_rate))
    skip = jnp.repeat(head_skip_gain, inner // heads)[None]
    gain = gated_norm_gain[None]
    pick = (jnp.arange(inner)[:, None] // (inner // heads) == jnp.arange(SUB)[None, :]).astype(BF)

    up_wide = jnp.pad(up_in, ((0, 0), (0, 512)))
    lam, edge = jnp.zeros((SUB, inner), F32), jnp.zeros((8, taps.shape[1]), F32)
    mine = mine.reshape(1)
    fixed = (lam, edge, mine)
    small = (marks, taps, conv_bias, par, skip, gain, pick, down_in, up_in, up_wide, down_out, up_out, fixed)
    tokens_near, cot_q, small = tie(tokens_near, cot_q, small)
    marks, taps, conv_bias, par, skip, gain, pick, down_in, up_in, up_wide, down_out, up_out, fixed = small
    lam, edge, mine = fixed
    tokens_far, cot_s = tie(ring_far(tokens_near, "tensor"), delivered(cot_q, "context"))
    cot_s = jnp.concatenate(cot_s, 0)
    cot_parts = shared(cot_s, "tensor")
    normed, gx, rank_t, part, y, xc, bc, slope, g2, states, out_all = run_forward(
        me, (tokens_s, *tokens_near, *tokens_far), input_norm_gain[None], down_in, up_wide, full, down_out,
        marks, taps, conv_bias, par, skip, gain,
    )
    g2, out_all, cot_parts = tie(g2, out_all, cot_parts)
    out_sum = lax.psum_scatter(out_all.reshape(length, width), "tensor", scatter_dimension=0, tiled=True)
    dn, stats, cot, d_low_t = run_pull_back(me, cot_parts, full, up_out, g2, part, down_out)
    stats_all = shared(stats, "tensor")

    backward = lambda half, *carried, **more: run_backward(
        me, half, gx, xc, bc, slope, y, dn, states, stats_all, marks, taps, par, skip, gain, pick,
        full, down_in, up_in, rank_t, *carried, **more,
    )
    *late, lam, edge, late_up, out_grads = backward(1, lam, edge, cot=cot, g2=g2, low_t=d_low_t)
    lam, late = tie(lam, late)
    late_parts = delivered(late, "tensor")
    *early, _, _, early_up = backward(0, lam, edge)
    early, late_parts, out_sum = tie(early, late_parts, out_sum)
    early_parts = delivered(early, "tensor")
    scratch = pltpu.VMEM((length, SUB), F32)
    branch = run_to_context(finish_branch, me, (out_sum, *stats_all, up_out), share, width, scratch, "finish_branch")
    branch_parts = delivered(branch, "context")
    early_parts, branch_parts = tie(early_parts, branch_parts)
    branch_q = jnp.stack(branch_parts)
    out_near = ring_near(branch_q, "tensor")
    *d_in, sent = run_in_grads(
        jnp.concatenate([me, mine]), early_parts, late_parts, early_up, late_up, normed, out_grads, share
    )
    sent_all = lax.all_gather(sent, ("fsdp", "context"), axis=0, tiled=True)
    d_in_parts = delivered(d_in, "context")
    d_in_parts, out_near, sent = tie(d_in_parts, out_near, sent)
    d_in_q = jnp.stack(d_in_parts)
    d_in_near = ring_near(d_in_q, "tensor")
    out_far = ring_far(out_near, "tensor")
    d_in_near, out_far = tie(d_in_near, out_far)
    d_in_far = ring_far(d_in_near, "tensor")
    layer_out = run_finish(finish_out, me, (branch_q, *out_near, *out_far), (tokens,), BF, "finish_out")
    table = in_adapter_down.shape[0]
    tables = run_tables(sent_all, table, rank, ((width,), (2, inner), (inner,), (width,)))
    layer_out, d_in_far, tables = tie(layer_out, d_in_far, tables)
    grad_tokens = run_finish(
        finish_grad, me, (d_in_q, *d_in_near, *d_in_far), (tokens, output_cotangent, input_norm_gain[None]), F32, "finish_grad"
    )
    return (
        layer_out,
        grad_tokens,
        tables[0].transpose(0, 2, 1),
        tables[1],
        tables[2].transpose(0, 2, 1),
        tables[3],
    )


def solution(mesh):
    placed = (
        P("fsdp", "context", None),
        P("fsdp", "context", None),
        P("fsdp", "context"),
        P("fsdp"),
        P(),
        P(("fsdp", "context"), None, "tensor"),
        P(("fsdp", "context"), None),
        P(("fsdp", "context"), "tensor"),
        P(None, "tensor"),
        P("tensor"),
        P(),
        P(),
        P("tensor"),
        P("tensor"),
        P("tensor"),
        P("tensor"),
        P("tensor", ("fsdp", "context")),
        P(),
        P(None, None, None, "tensor"),
        P(None, "tensor", None),
        P(),
    )
    return jax.shard_map(
        per_device,
        mesh=mesh,
        in_specs=placed,
        out_specs=(
            P("fsdp", "context", None),
            P("fsdp", "context", None),
            P(),
            P(None, None, None, "tensor"),
            P(None, "tensor", None),
            P(),
        ),
        check_vma=False,
    )
```

```python
import functools

import jax
import jax.numpy as jnp
from jax import lax
from jax.experimental import pallas as pl
from jax.experimental.pallas import tpu as pltpu
from jax.sharding import PartitionSpec as P

INNER_CHANNELS = 3072
EPS_NORM = 1e-05
SUB = 128
NEG = -1e30
BF = jnp.bfloat16
F32 = jnp.float32
HIGHEST = lax.Precision.HIGHEST


def dot_nn(a, b):
    return lax.dot_general(a, b, (((1,), (0,)), ((), ())), preferred_element_type=F32)


def dot_nt(a, b):
    return lax.dot_general(a, b, (((1,), (1,)), ((), ())), preferred_element_type=F32)


def dot_tn(a, b):
    return lax.dot_general(a, b, (((0,), (0,)), ((), ())), preferred_element_type=F32)


def softplus(v):
    return jnp.maximum(v, 0.0) + jnp.log1p(jnp.exp(-jnp.abs(v)))


def lane(shape, dim):
    return lax.broadcasted_iota(jnp.int32, shape, dim)


def wide(column):
    return jnp.broadcast_to(column, (SUB, SUB))


def decays(raw, par_ref):
    dt = softplus(raw + par_ref[0:1, :])
    lower = (lane((SUB, SUB), 0) >= lane((SUB, SUB), 1)).astype(F32)
    run = jnp.dot(lower, dt * par_ref[1:2, :], precision=HIGHEST, preferred_element_type=F32)
    return dt, run


def scan_forward(
    k, gx, dt_ref, run_ref, rows_ref, marks_ref, taps_ref, bias_ref, skip_ref, gain_ref, down_ref,
    y_ref, xc_ref, bc_ref, slope_ref, g2_ref, states_ref, stats_ref, state, ext,
):
    inner = skip_ref.shape[1]
    chans = ext.shape[1]
    rows = pl.ds(pl.multiple_of(k * SUB, SUB), SUB)

    def strip(ref, at):
        each = ref.shape[2] // SUB
        return ref[at // each, rows, (at % each) * SUB : (at % each + 1) * SUB].astype(F32)

    @pl.when(k == 0)
    def _():
        state[...] = jnp.zeros_like(state)
        ext[0:8, :] = jnp.zeros((8, chans), F32)

    @pl.when(k > 0)
    def _():
        ext[0:8, :] = ext[SUB : SUB + 8, :]

    for c in range(chans // SUB):
        ext[8 : SUB + 8, c * SUB : (c + 1) * SUB] = strip(gx, inner // SUB + c)
    near = [wide(marks_ref[:, k : k + 1]) for k in range(3)]
    linked = wide(marks_ref[:, 3:4])
    ending = wide(marks_ref[:, 4:5])
    ids = wide(marks_ref[:, 5:6])
    passing = marks_ref[0:1, 6:7]
    left = lane((SUB, SUB), 1) < 64

    def conv(sl):
        pre = bias_ref[:, sl] + taps_ref[3:4, sl] * ext[8 : SUB + 8, sl]
        for k in range(1, 4):
            pre = pre + taps_ref[3 - k : 4 - k, sl] * (ext[8 - k : SUB + 8 - k, sl] * near[k - 1])
        sig = jax.nn.sigmoid(pre)
        out = (pre * sig).astype(BF)
        slope_ref[:, sl] = (sig * (1.0 + pre * (1.0 - sig))).astype(BF)
        return out

    b_low = conv(slice(inner, inner + SUB))
    c_low = conv(slice(inner + SUB, inner + 2 * SUB))
    bc_ref[:, 0:SUB] = b_low
    bc_ref[:, SUB : 2 * SUB] = c_low
    b_turned = b_low.astype(F32).T.astype(BF)
    dt, run = dt_ref[rows, :], run_ref[rows, :]
    run_rows = rows_ref[pl.ds(pl.multiple_of(k * 16, 16), 16), :]
    allowed = (ids == ids.T) & (lane((SUB, SUB), 0) >= lane((SUB, SUB), 1))
    mask = jnp.where(allowed, 0.0, NEG)
    cross = dot_nt(c_low, b_low)
    square = jnp.zeros((SUB, SUB), F32)
    for p in range(inner // SUB):
        sl = slice(p * SUB, (p + 1) * SUB)
        x_low = conv(sl)
        xc_ref[:, sl] = x_low
        x = x_low.astype(F32)
        run0, run1 = wide(run[:, 2 * p : 2 * p + 1]), wide(run[:, 2 * p + 1 : 2 * p + 2])
        run_p = jnp.where(left, run0, run1)
        dt_p = jnp.where(left, wide(dt[:, 2 * p : 2 * p + 1]), wide(dt[:, 2 * p + 1 : 2 * p + 2]))
        m0 = (jnp.exp(run0 - run_rows[2 * p : 2 * p + 1, :] + mask) * cross).astype(BF)
        m1 = (jnp.exp(run1 - run_rows[2 * p + 1 : 2 * p + 2, :] + mask) * cross).astype(BF)
        xdt = x * dt_p
        split = jnp.concatenate([jnp.where(left, xdt, 0.0), jnp.where(left, 0.0, xdt)], 0).astype(BF)
        before = state[:, sl]
        before_low = before.astype(BF)
        states_ref[0, :, sl] = before_low
        y = dot_nn(jnp.concatenate([m0, m1], 1), split)
        y = y + jnp.exp(run_p) * linked * dot_nn(c_low, before_low) + skip_ref[:, sl] * x
        last = run_p[SUB - 1 : SUB, :]
        toward = (xdt * (jnp.exp(last - run_p) * ending)).astype(BF)
        state[:, sl] = (jnp.exp(last) * passing) * before + dot_nn(b_turned, toward)
        z = strip(gx, p)
        gated = y * (z * jax.nn.sigmoid(z))
        y_ref[:, sl] = y.astype(BF)
        g2_ref[:, sl] = (gated * gain_ref[:, sl]).astype(BF)
        square = square + gated * gated
    stats_ref[0:8, rows] = lane_rows(square)
    stats_ref[8:, rows] = dot_nt(down_ref[...], g2_ref[...])


def forward_all(
    normed, rank, up_ref, w_ref, w0_ref, w1_ref, out_down_ref, marks_ref, taps_ref, bias_ref, par_ref, skip_ref, gain_ref,
    gx_hbm, rank_t_ref, stats_ref, dt_ref, run_ref, rows_ref, y_ref, xc_ref, bc_ref, slope_ref, g2_ref, states_ref, out_ref,
    gx, state, ext, g2_all, held, sems,
):
    step = pl.program_id(0)
    tiles, length, tile = gx.shape

    def copy_gx(j):
        return pltpu.make_async_copy(gx.at[j], gx_hbm.at[:, pl.ds(j * tile, tile)], sems.at[j])

    @pl.when(step == 0)
    def _():
        turn_rank(rank[...].astype(F32), rank_t_ref)

    for j in range(tiles):

        @pl.when(step == j)
        def _():
            gx[j] = (dot_nn(normed[...], w_ref[...]) + dot_nn(rank[...], up_ref[...])).astype(BF)
            copy_gx(j).start()

    @pl.when(step == tiles - 1)
    def _():
        inner, chans = skip_ref.shape[1], taps_ref.shape[1]
        at, col = divmod(2 * inner + chans - inner, tile)
        for i in range(length // SUB):
            here = slice(i * SUB, (i + 1) * SUB)
            dt, run = decays(gx[at, here, col : col + SUB].astype(F32), par_ref)
            dt_ref[here, :] = dt
            run_ref[here, :] = run
            rows_ref[i * 16 : (i + 1) * 16, :] = run.T[0:16, :]

    done = tiles + length // SUB

    @pl.when((step >= tiles) & (step < done))
    def _():
        scan_forward(
            step - tiles, gx, dt_ref, run_ref, rows_ref, marks_ref, taps_ref, bias_ref, skip_ref, gain_ref, out_down_ref,
            y_ref, xc_ref, bc_ref, slope_ref, g2_ref, states_ref, stats_ref, state, ext,
        )
        g2_all[pl.ds(pl.multiple_of((step - tiles) * SUB, SUB), SUB), :] = g2_ref[...]

    @pl.when(step >= done)
    def _():
        cut = w0_ref.shape[1]
        held[...] = (dot_nt(g2_all[:, 0:cut], w0_ref[...]) + dot_nt(g2_all[:, cut:], w1_ref[...])).astype(BF)
        owners, rows, _ = out_ref.shape
        share = 64
        for c in range(rows // share):
            for y in range(owners):
                at = (c * owners + y) * share
                out_ref[y, c * share : (c + 1) * share, :] = held[at : at + share, :]

    @pl.when(step == pl.num_programs(0) - 1)
    def _():
        for j in range(tiles):
            copy_gx(j).wait()


def backward_half(
    me_ref, z_ref, raw_ref, dt_ref, run_ref, rows_ref, xc_ref, bc_ref, slope_ref, y_ref, dn_ref, states_ref, s0_ref, s1_ref, s2_ref, s3_ref, marks_ref,
    taps_ref, par_ref, skip_ref, gain_ref, pick_ref, lam_in_ref, edge_in_ref,
    w_ref, down_ref, up_ref, rank_t_ref, *rest, with_grads,
):
    if with_grads:
        (cot0_ref, g20_ref, low0_ref, cot1_ref, g21_ref, low1_ref, q0_ref, q1_ref, q2_ref, q3_ref, chosen_ref), rest = rest[:11], rest[11:]
        o0, o1, o2, o3, lam, edge_ref, up_grad_ref, grads_ref, *scratch = rest
        grads, *scratch = scratch
    else:
        o0, o1, o2, o3, lam, edge_ref, up_grad_ref, *scratch = rest
    d_all, low, pushed, held, ext, to_dt, to_run, to_end, shifted = scratch
    step = pl.program_id(0)
    steps = d_all.shape[0] // SUB
    if with_grads:

        @pl.when(step == 0)
        def _():
            grads[...] = jnp.zeros_like(grads)

        @pl.when(step < steps)
        def _():
            cut = g20_ref.shape[1]
            for stats, low_t_ref, cot_ref, g2_ref in (
                (s0_ref[...] + s1_ref[...] + s2_ref[...] + s3_ref[...], low0_ref, cot0_ref, g20_ref),
                (q0_ref[...] + q1_ref[...] + q2_ref[...] + q3_ref[...], low1_ref, cot1_ref, g21_ref),
            ):
                rn_row = lax.rsqrt(stats[0:1, :] / INNER_CHANNELS + EPS_NORM)
                grads[:, 0:cut] += dot_nn((low_t_ref[...].astype(F32) * rn_row).astype(BF), g2_ref[...])
                grads[:, cut:] += dot_nn((stats[8:, :] * rn_row).astype(BF), cot_ref[...])

        @pl.when(step == steps)
        def _():
            grads_ref[:, 0 : grads.shape[1]] = grads[...].astype(BF)
            mine = lane((grads.shape[0], SUB), 1).astype(F32) == chosen_ref[...]
            grads_ref[:, grads.shape[1] :] = jnp.where(mine, 1.0, 0.0).astype(BF)

    @pl.when(step < steps)
    def _():
        at = pl.multiple_of((steps - 1 - step) * SUB, SUB)
        scan_backward(
            step, at, d_all.at[pl.ds(at, SUB), :], z_ref, dt_ref, run_ref, rows_ref, xc_ref, bc_ref, slope_ref, y_ref, dn_ref, states_ref,
            (s0_ref, s1_ref, s2_ref, s3_ref), marks_ref, taps_ref, par_ref, skip_ref, gain_ref, pick_ref, lam_in_ref, edge_in_ref,
            lam, ext, to_dt, to_run, to_end,
        )
        gate = d_all[pl.ds(at, SUB), 0 : up_ref.shape[1]]
        part = dot_nt(gate, up_ref[...])
        rank = part.shape[1]
        low[pl.ds(at, SUB), :] = part.astype(BF)
        part = jnp.concatenate([part, jnp.zeros((SUB, SUB - rank), F32)], 1)
        pushed[:, pl.ds(at, SUB)] = part.T[0:rank, :].astype(BF)
        up_grad = dot_nn(rank_t_ref[...], gate)

        @pl.when(step == 0)
        def _():
            up_grad_ref[...] = up_grad

        @pl.when(step > 0)
        def _():
            up_grad_ref[...] += up_grad

        shifted[pl.ds(at, SUB), :] = raw_ref[...].astype(F32) + par_ref[0:1, :]

    @pl.when(step == steps - 1)
    def _():
        edge_ref[...] = ext[0:8, :]

    @pl.when(step == steps)
    def _():
        def by_head(v):
            high = v.astype(BF)
            return dot_nn(high, pick_ref[...]) + dot_nn((v - high.astype(F32)).astype(BF), pick_ref[...])

        d_run, d_dt, d_end = by_head(to_run[...]), by_head(to_dt[...]), by_head(to_end[...])
        upper = (lane((SUB, SUB), 0) <= lane((SUB, SUB), 1)).astype(F32)
        for i in range(steps):
            here = slice(i * SUB, (i + 1) * SUB)
            block = d_run[here] + jnp.where(lane((SUB, SUB), 0) == SUB - 1, d_end[i * 8 : i * 8 + 1], 0.0)
            d_log = jnp.dot(upper, block, precision=HIGHEST, preferred_element_type=F32)
            d_raw = (d_dt[here] + par_ref[1:2, :] * d_log) * jax.nn.sigmoid(shifted[here, :])
            d_all[here, d_all.shape[1] - SUB :] = d_raw.astype(BF)

    @pl.when(step >= steps)
    def _():
        held[...] = (dot_nt(d_all[...], w_ref[...]) + dot_nn(low[...], down_ref[...])).astype(BF)
        deal(me_ref[0], held, (o0, o1, o2, o3))

    for out in (o0, o1, o2, o3):

        @pl.when(step == steps)
        def _():
            out[out.shape[0] - pushed.shape[0] :, :] = pushed[...]

        @pl.when(step > steps)
        def _():
            out[out.shape[0] - pushed.shape[0] :, :] = jnp.zeros_like(pushed)


def scan_backward(
    step, at, da_ref, z_ref, dt_ref, run_ref, rows_ref, xc_ref, bc_ref, slope_ref, y_ref, dn_ref, states_ref, stats_refs, marks_ref,
    taps_ref, par_ref, skip_ref, gain_ref, pick_ref, lam_in_ref, edge_in_ref,
    lam, ext, to_dt, to_run, to_end,
):
    inner = z_ref.shape[1]
    chans = ext.shape[1]

    @pl.when(step == 0)
    def _():
        lam[...] = lam_in_ref[...]
        ext[SUB : SUB + 8, :] = edge_in_ref[...]

    @pl.when(step > 0)
    def _():
        ext[SUB : SUB + 8, :] = ext[0:8, :]

    linked = wide(marks_ref[:, 3:4])
    ending = wide(marks_ref[:, 4:5])
    ids = wide(marks_ref[:, 5:6])
    passing = marks_ref[0:1, 6:7]
    later = [wide(marks_ref[:, 7 + k : 8 + k]) for k in range(3)]
    left = lane((SUB, SUB), 1) < 64
    stats = stats_refs[0][...] + stats_refs[1][...] + stats_refs[2][...] + stats_refs[3][...]
    rn_row = lax.rsqrt(stats[0:1, :] / INNER_CHANNELS + EPS_NORM)
    rn = jnp.broadcast_to(rn_row, (SUB, SUB)).T
    kappa = jnp.broadcast_to(rn_row * rn_row * rn_row * stats[1:2, :] / INNER_CHANNELS, (SUB, SUB)).T
    dt, run, run_rows = dt_ref[...], run_ref[...], rows_ref[...]
    tokens = pl.ds(at, SUB)
    b_low, c_low = bc_ref[:, 0:SUB], bc_ref[:, SUB : 2 * SUB]
    c_turned = c_low.astype(F32).T.astype(BF)
    allowed = (ids == ids.T) & (lane((SUB, SUB), 0) <= lane((SUB, SUB), 1))
    mask = jnp.where(allowed, 0.0, NEG)
    cross = dot_nt(b_low, c_low)
    d_cross = jnp.zeros((SUB, SUB), F32)
    d_b = jnp.zeros((SUB, SUB), F32)
    d_c = jnp.zeros((SUB, SUB), F32)
    for p in range(inner // SUB):
        sl = slice(p * SUB, (p + 1) * SUB)
        z = z_ref[:, sl].astype(F32)
        sig = jax.nn.sigmoid(z)
        silu = z * sig
        y = y_ref[:, sl].astype(F32)
        d_gated = rn * (dn_ref[:, sl].astype(F32) * gain_ref[:, sl]) - kappa * (y * silu)
        da_ref[:, sl] = (d_gated * y * sig * (1.0 + z * (1.0 - sig))).astype(BF)
        dy = d_gated * silu
        x = xc_ref[:, sl].astype(F32)
        run0, run1 = wide(run[:, 2 * p : 2 * p + 1]), wide(run[:, 2 * p + 1 : 2 * p + 2])
        run_p = jnp.where(left, run0, run1)
        dt_p = jnp.where(left, wide(dt[:, 2 * p : 2 * p + 1]), wide(dt[:, 2 * p + 1 : 2 * p + 2]))
        l0 = jnp.exp(run_rows[2 * p : 2 * p + 1, :] - run0 + mask)
        l1 = jnp.exp(run_rows[2 * p + 1 : 2 * p + 2, :] - run1 + mask)
        xdt = x * dt_p
        x_split = jnp.concatenate([jnp.where(left, xdt, 0.0), jnp.where(left, 0.0, xdt)], 0).astype(BF)
        dy_split = jnp.concatenate([jnp.where(left, dy, 0.0), jnp.where(left, 0.0, dy)], 0).astype(BF)
        d_m = dot_nt(x_split, dy.astype(BF))
        d_cross = d_cross + l0 * d_m[0:SUB] + l1 * d_m[SUB : 2 * SUB]
        m = jnp.concatenate([l0 * cross, l1 * cross], 1).astype(BF)
        lam_p = lam[:, sl]
        lam_low = lam_p.astype(BF)
        last = run_p[SUB - 1 : SUB, :]
        toward = jnp.exp(last - run_p) * ending
        carried = toward * dot_nn(b_low, lam_low)
        d_xt = dot_nn(m, dy_split) + carried
        skip = skip_ref[:, sl]
        ext[0:SUB, sl] = (dt_p * d_xt + skip * dy) * slope_ref[:, sl].astype(F32)
        x_dx = x * d_xt
        to_dt[tokens, sl] = x_dx
        to_run[tokens, sl] = dy * (y - skip * x) - dt_p * x_dx
        reached = (jnp.exp(run_p) * linked * dy).astype(BF)
        before_low = states_ref[0, :, sl]
        keep = jnp.exp(last) * passing
        end = jnp.sum(xdt * carried, 0, keepdims=True) + keep * jnp.sum(
            lam_p * before_low.astype(F32), 0, keepdims=True
        )
        to_end[pl.ds(pl.multiple_of(at // 16, 8), 8), sl] = jnp.broadcast_to(end, (8, SUB))
        d_b = d_b + dot_nt((xdt * toward).astype(BF), lam_low)
        d_c = d_c + dot_nt(reached, before_low)
        lam[:, sl] = keep * lam_p + dot_nn(c_turned, reached)
    d_cross_low = d_cross.astype(BF)
    d_b = d_b + dot_nn(d_cross_low, c_low)
    d_c = d_c + dot_nn(d_cross.T.astype(BF), b_low)
    ext[0:SUB, inner : inner + SUB] = d_b * slope_ref[:, inner : inner + SUB].astype(F32)
    ext[0:SUB, inner + SUB : chans] = d_c * slope_ref[:, inner + SUB : chans].astype(F32)

    for s in range(chans // SUB):
        sl = slice(s * SUB, (s + 1) * SUB)
        acc = taps_ref[3:4, sl] * ext[0:SUB, sl]
        for k in range(1, 4):
            acc = acc + taps_ref[3 - k : 4 - k, sl] * (ext[k : SUB + k, sl] * later[k - 1])
        da_ref[:, inner + s * SUB : inner + (s + 1) * SUB] = acc.astype(BF)

def whole(a):
    return pl.BlockSpec(a.shape, lambda i, *_: (0,) * a.ndim)


def params(mib=60):
    return pltpu.CompilerParams(vmem_limit_bytes=mib << 20)


def takes(us):
    return pl.CostEstimate(flops=us * 100_000_000, bytes_accessed=us * 300_000, transcendentals=0)


def turn_rank(low, rank_t_ref):
    rank = low.shape[1]
    low = jnp.concatenate([low, jnp.zeros((low.shape[0], SUB - rank), F32)], 1)
    for k in range(low.shape[0] // SUB):
        here = slice(k * SUB, (k + 1) * SUB)
        rank_t_ref[:, here] = low[here, :].T[0:rank, :].astype(BF)


def low_products(rows_ref, down_ref, rank_ref, rank_t_ref):
    low = dot_nt(rows_ref[...], down_ref[...])
    rank_ref[...] = low.astype(BF)
    turn_rank(low, rank_t_ref)


def lane_rows(v):
    return lax.dot_general(
        jnp.ones((8, v.shape[1]), F32), v, (((1,), (1,)), ((), ())), precision=HIGHEST, preferred_element_type=F32
    )


def deal(me, held, outs):
    share = 64
    for c in range(held.shape[0] // (4 * share)):
        for d, out in enumerate(outs):
            at = pl.multiple_of((c * 4 + (me + d) % 4) * share, share)
            out[c * share : (c + 1) * share, :] = held[pl.ds(at, share), :]


def one(a):
    return pl.BlockSpec(a.shape, lambda i, *_: (0,) * a.ndim, pipeline_mode=pl.Buffered(1))


def kept(*shape):
    return pl.BlockSpec(shape, lambda i, *_: (0,) * len(shape))


def run_forward(normed, low_rank, up, weights, out_down, marks, taps, bias, par, skip, gain):
    length, width = normed.shape
    inner, chans = skip.shape[1], taps.shape[1]
    rank, columns = up.shape
    tile = 512
    tiles, steps, out_tiles = columns // tile, length // SUB, width // tile
    sub = lambda i: jnp.clip(i - tiles, 0, steps - 1)
    scan = lambda cols: pl.BlockSpec((SUB, cols), lambda i: (sub(i), 0))
    first = lambda i: jnp.minimum(i, tiles - 1)
    last = lambda i: jnp.maximum(i - tiles - steps, 0)
    at_out = 2 * (weights.shape[1] - inner) // inner
    return pl.pallas_call(
        forward_all,
        grid=(tiles + steps + out_tiles,),
        in_specs=[
            one(normed), one(low_rank),
            pl.BlockSpec((rank, tile), lambda i: (0, first(i))),
            pl.BlockSpec((width, tile), lambda i: (0, first(i))),
            pl.BlockSpec((tile, inner // 2), lambda i: (last(i), at_out)),
            pl.BlockSpec((tile, inner // 2), lambda i: (last(i), at_out + 1)),
            one(out_down), scan(marks.shape[1]), one(taps), one(bias), one(par), one(skip), one(gain),
        ],
        out_specs=[
            pl.BlockSpec(memory_space=pl.ANY), kept(rank, length), kept(8 + rank, length),
            kept(length, SUB), kept(length, SUB), kept(steps * 16, SUB),
            scan(inner), scan(inner), scan(2 * SUB), scan(chans), scan(inner),
            pl.BlockSpec((1, SUB, inner), lambda i: (sub(i), 0, 0)),
            pl.BlockSpec((4, length // 4, tile), lambda i: (0, 0, last(i))),
        ],
        scratch_shapes=[
            pltpu.VMEM((tiles, length, tile), BF),
            pltpu.VMEM((SUB, inner), F32),
            pltpu.VMEM((SUB + 8, chans), F32),
            pltpu.VMEM((length, inner), BF),
            pltpu.VMEM((length, tile), BF),
            pltpu.SemaphoreType.DMA((tiles,)),
        ],
        out_shape=[
            jax.ShapeDtypeStruct((length, columns), BF),
            jax.ShapeDtypeStruct((rank, length), BF),
            jax.ShapeDtypeStruct((8 + rank, length), F32),
            jax.ShapeDtypeStruct((length, SUB), F32),
            jax.ShapeDtypeStruct((length, SUB), F32),
            jax.ShapeDtypeStruct((steps * 16, SUB), F32),
            jax.ShapeDtypeStruct((length, inner), BF),
            jax.ShapeDtypeStruct((length, inner), BF),
            jax.ShapeDtypeStruct((length, 2 * SUB), BF),
            jax.ShapeDtypeStruct((length, chans), BF),
            jax.ShapeDtypeStruct((length, inner), BF),
            jax.ShapeDtypeStruct((steps, SUB, inner), BF),
            jax.ShapeDtypeStruct((4, length // 4, width), BF),
        ],
        compiler_params=params(),
        cost_estimate=takes(30),
        name="forward_all",
    )(normed, low_rank, up, weights, weights, weights, out_down, marks, taps, bias, par, skip, gain)


def prepare(
    me_ref, adapters_ref, seg_ref, vec_ref, x_taps_ref, bc_taps_ref, down_in_ref, up_in_ref, down_out_ref, up_out_ref,
    marks_ref, taps_ref, bias_ref, par_ref, skip_ref, gain_ref, norm_gain_ref, down_in, up_wide, down_out, up_out,
):
    chunks, block = seg_ref.shape
    each = block // SUB
    subs = chunks * each
    seg = seg_ref[...].astype(F32)
    rows = [seg[c : c + 1, h * SUB : (h + 1) * SUB] for c in range(chunks) for h in range(each)]
    own = jnp.concatenate(rows, 0)
    none = jnp.full((1, SUB), -1.0, F32)
    before = jnp.concatenate([none, *rows[:-1]], 0)
    after = jnp.concatenate([*rows[1:], none], 0)
    at = lane((subs, SUB), 1)
    last, last_before = (jnp.broadcast_to(v[:, SUB - 1 : SUB], own.shape) for v in (own, before))
    kinds = [own == jnp.where(at >= k, pltpu.roll(own, k, 1), pltpu.roll(before, k, 1)) for k in (1, 2, 3)]
    kinds += [own == last_before, own == last, None, last == last_before]
    kinds += [
        own == jnp.where(at < SUB - k, pltpu.roll(own, SUB - k, 1), pltpu.roll(after, SUB - k, 1)) for k in (1, 2, 3)
    ]
    kinds = [own if v is None else jnp.where(v, 1.0, 0.0) for v in kinds]
    count = marks_ref.shape[1]
    for i in range(subs):
        here = [v[i : i + 1, :] for v in kinds]
        full = jnp.concatenate([*here, jnp.zeros((SUB - len(here), SUB), F32)], 0)
        marks_ref[i * SUB : (i + 1) * SUB, :] = full.T[:, 0:count]
    inner = x_taps_ref.shape[1]
    chans = taps_ref.shape[1]
    taps_ref[:, 0:inner] = x_taps_ref[...]
    taps_ref[:, inner:] = bc_taps_ref[...]
    cuts = [0]
    for n in (chans, inner, norm_gain_ref.shape[1], SUB, SUB, SUB):
        cuts.append(cuts[-1] + n)
    piece = [vec_ref[:, a:b] for a, b in zip(cuts, cuts[1:])]
    bias_ref[...], gain_ref[...], norm_gain_ref[...] = piece[:3]
    par_ref[...] = jnp.concatenate([piece[3], -jnp.exp(piece[4]), jnp.zeros((6, SUB), F32)], 0)
    spread = jnp.where(lane((SUB, inner), 0) == lane((SUB, inner), 1) // 64, 1.0, 0.0)
    skip = jnp.dot(jnp.broadcast_to(piece[5], (8, SUB)), spread, precision=HIGHEST, preferred_element_type=F32)
    skip_ref[...] = skip[0:1, :]
    down_in[...], down_out[...], up_out[...] = down_in_ref[0], down_out_ref[0], up_out_ref[0]
    up_wide[...] = jnp.zeros_like(up_wide)
    for k in range(2):
        up_wide[:, k * inner : (k + 1) * inner] = up_in_ref[0, :, k, :]


def run_prepare(me, adapters, seg, vec, x_taps, bc_taps, down_in, up_in, down_out, up_out, norm_width):
    length = seg.shape[0] * seg.shape[1]
    inner, bc = x_taps.shape[1], bc_taps.shape[1]
    rank = up_in.shape[1]
    mine = lambda a: pl.BlockSpec((1, *a.shape[1:]), lambda i, me, ad: (ad[me[1]],) + (0,) * (a.ndim - 1))
    outs = [
        ((length, 16), F32), ((4, inner + bc), F32), ((1, inner + bc), F32), ((8, SUB), F32), ((1, inner), F32),
        ((1, inner), F32), ((1, norm_width), F32), (down_in.shape[1:], BF), ((rank, 2 * inner + 512), BF),
        (down_out.shape[1:], BF), (up_out.shape[1:], BF),
    ]
    return pl.pallas_call(
        prepare,
        grid_spec=pltpu.PrefetchScalarGridSpec(
            num_scalar_prefetch=2,
            grid=(1,),
            in_specs=[one(seg), one(vec), one(x_taps), one(bc_taps), mine(down_in), mine(up_in), mine(down_out), mine(up_out)],
            out_specs=[kept(*n) for n, _ in outs],
        ),
        out_shape=[jax.ShapeDtypeStruct(n, t) for n, t in outs],
        compiler_params=params(),
        cost_estimate=takes(2),
        name="prepare",
    )(me, adapters, seg, vec, x_taps, bc_taps, down_in, up_in, down_out, up_out)


def normed_rows(me_ref, blocks, down_ref, gain_ref, held, rows_hbm, rank_ref, sems):
    share = held.shape[1]
    copies = []
    for k, (c, back, rows) in enumerate(blocks):
        t = rows.astype(F32)
        rms = lax.rsqrt(jnp.mean(t * t, -1, keepdims=True) + EPS_NORM)
        held[k] = (t * rms * gain_ref[...]).astype(BF)
        at = pl.multiple_of((c * 4 + (me_ref[0] + 4 - back) % 4) * share, share)
        copies.append(pltpu.make_async_copy(held.at[k], rows_hbm.at[pl.ds(at, share), :], sems.at[k]))
        copies[-1].start()
        rank_ref[pl.ds(at, share), :] = dot_nt(held[k], down_ref[...]).astype(BF)
    for copy in copies:
        copy.wait()


def near_rows(me_ref, p0, p1, p2, down_ref, gain_ref, rows_hbm, rank_ref, held, sems):
    rank_ref[...] = jnp.zeros_like(rank_ref)
    blocks = [
        (c, back, part[(me_ref[1] + 4 - c) % 4]) for c in range(4) for back, part in ((0, p0), (1, p1), (3, p2))
    ]
    normed_rows(me_ref, blocks, down_ref, gain_ref, held, rows_hbm, rank_ref, sems)


def far_rows(me_ref, p3, p4, down_ref, gain_ref, rows_in, rank_in, rows_hbm, rank_ref, held, sems):
    rank_ref[...] = rank_in[...]
    blocks = []
    for c in range(4):
        turn = (me_ref[1] + 4 - c) % 4
        blocks.append((c, 2, jnp.where(turn < 2, p3[turn % 2], p4[turn % 2])))
    normed_rows(me_ref, blocks, down_ref, gain_ref, held, rows_hbm, rank_ref, sems)


def run_rows(kernel, me, pieces, down, gain, before, name):
    share, width = pieces[0].shape[1:]
    length = 16 * share
    rank = down.shape[0]
    count = sum(p.shape[0] for p in pieces)
    any_space = pl.BlockSpec(memory_space=pl.ANY)
    args = (*pieces, down, gain, *before)
    return pl.pallas_call(
        kernel,
        grid_spec=pltpu.PrefetchScalarGridSpec(
            num_scalar_prefetch=1,
            grid=(1,),
            in_specs=[*[one(a) for a in (*pieces, down, gain)], *([any_space, one(before[1])] if before else [])],
            out_specs=[any_space, kept(length, rank)],
            scratch_shapes=[pltpu.VMEM((count, share, width), BF), pltpu.SemaphoreType.DMA((count,))],
        ),
        out_shape=[jax.ShapeDtypeStruct((length, width), BF), jax.ShapeDtypeStruct((length, rank), BF)],
        input_output_aliases={len(args) - 1: 0} if before else {},
        compiler_params=params(),
        cost_estimate=takes(3),
        name=name,
    )(me, *args)


def pull_back(
    me_ref, p0, p1, p2, p3, up_ref, w_ref, g2_ref, part_ref, down_ref,
    dn_ref, stats_ref, cot_hbm, low_t_ref,
    cot, low, dots, sem,
):
    step = pl.program_id(0)
    copy_cot = pltpu.make_async_copy(cot, cot_hbm, sem)

    @pl.when(step == 0)
    def _():
        chunks, share, _ = p0.shape
        for c in range(chunks):
            for d, part in enumerate((p0, p1, p2, p3)):
                at = pl.multiple_of((c * 4 + (me_ref[0] + 4 - d) % 4) * share, share)
                cot[pl.ds(at, share), :] = part[(me_ref[1] + 4 - c) % 4]
        copy_cot.start()
        low_products(cot, up_ref, low, low_t_ref)
        dots[...] = jnp.zeros_like(dots)

    dn = dot_nn(cot[...], w_ref[...]) + dot_nn(low[...], down_ref[...])
    dn_ref[...] = dn.astype(BF)
    both = dn * g2_ref[...].astype(F32)
    total = dots[...]
    for k in range(both.shape[1] // SUB):
        total = total + both[:, k * SUB : (k + 1) * SUB]
    dots[...] = total

    @pl.when(step == pl.num_programs(0) - 1)
    def _():
        first = lane((8, stats_ref.shape[1]), 0) == 0
        stats_ref[0:8, :] = jnp.where(first, part_ref[0:8, :], lane_rows(dots[...]))
        stats_ref[8:, :] = part_ref[8:, :]
        copy_cot.wait()


def run_pull_back(me, pieces, weights, up, g2, part, down, tile=384):
    width = pieces[0].shape[2]
    length, inner = g2.shape
    rank = down.shape[0]
    first = (weights.shape[1] - inner) // tile
    return pl.pallas_call(
        pull_back,
        grid_spec=pltpu.PrefetchScalarGridSpec(
            num_scalar_prefetch=1,
            grid=(inner // tile,),
            in_specs=[
                *[one(p) for p in pieces], one(up),
                pl.BlockSpec((width, tile), lambda j, me: (0, first + j)),
                pl.BlockSpec((length, tile), lambda j, me: (0, j)),
                one(part),
                pl.BlockSpec((rank, tile), lambda j, me: (0, j)),
            ],
            out_specs=[
                pl.BlockSpec((length, tile), lambda j, me: (0, j)), kept(*part.shape),
                pl.BlockSpec(memory_space=pl.ANY), kept(rank, length),
            ],
            scratch_shapes=[
                pltpu.VMEM((length, width), BF),
                pltpu.VMEM((length, rank), BF),
                pltpu.VMEM((length, SUB), F32),
                pltpu.SemaphoreType.DMA,
            ],
        ),
        out_shape=[
            jax.ShapeDtypeStruct((length, inner), BF),
            jax.ShapeDtypeStruct(part.shape, F32),
            jax.ShapeDtypeStruct((length, width), BF),
            jax.ShapeDtypeStruct((rank, length), BF),
        ],
        compiler_params=params(),
        cost_estimate=takes(8),
        name="pull_back",
    )(me, *pieces, up, weights, g2, part, down)


def dealt(rows, width, tile, at):
    spec = pl.BlockSpec((rows, tile), lambda j, me: (0, at(j)))
    return [spec] * 4, [jax.ShapeDtypeStruct((rows, width), BF)] * 4


def run_backward(
    me, half, gx, dt, run, run_rows, xc, bc, slope, y, dn, states, stats, marks, taps, par, skip, gain, pick,
    weights, down, up, rank_t, lam, edge, cot=None, g2=None, low_t=None, chosen=None,
):
    length = gx.shape[0] // 2
    inner, chans, width = skip.shape[1], taps.shape[1], weights.shape[0]
    rank = down.shape[0]
    up_block = pl.BlockSpec((rank, 2 * inner), lambda i, me: (0, 0), pipeline_mode=pl.Buffered(1))
    steps = length // SUB
    tile = 512
    assert tile == length
    top = (half + 1) * steps - 1
    sub = lambda i: jnp.maximum(top - i, half * steps)
    col = lambda i: jnp.maximum(i - steps, 0)
    row = lambda cols, at=0: pl.BlockSpec((SUB, cols), lambda i, me, at=at: (sub(i), at))
    lanes = lambda n: pl.BlockSpec((n, SUB), lambda i, me: (0, sub(i)))
    total = inner + chans + SUB
    specs, shapes = dealt(length // 4 + rank, width, tile, col)
    with_grads = cot is not None
    args = [
        gx, gx, dt, run, run_rows, xc, bc, slope, y, dn, states, *stats, marks, taps, par, skip, gain, pick, lam, edge,
        weights, down, up, rank_t,
    ]
    in_specs = [
        row(inner), row(SUB, (inner + chans) // SUB), row(SUB), row(SUB), pl.BlockSpec((16, SUB), lambda i, me: (sub(i), 0)),
        row(inner), row(2 * SUB), row(chans), row(inner), row(inner),
        pl.BlockSpec((1, SUB, inner), lambda i, me: (sub(i), 0, 0)),
        *[lanes(stats[0].shape[0])] * 4,
        row(marks.shape[1]), one(taps), one(par), one(skip), one(gain), one(pick), one(lam), one(edge),
        pl.BlockSpec((tile, total), lambda i, me: (col(i), 0)),
        pl.BlockSpec((rank, tile), lambda i, me: (0, col(i))),
        up_block, lanes(rank),
    ]
    out_specs = [*specs, kept(*lam.shape), kept(*edge.shape), kept(rank, 2 * inner)]
    out_shape = [
        *shapes,
        jax.ShapeDtypeStruct(lam.shape, F32),
        jax.ShapeDtypeStruct(edge.shape, F32),
        jax.ShapeDtypeStruct((rank, 2 * inner), F32),
    ]
    scratch = [
        pltpu.VMEM((length, total), BF),
        pltpu.VMEM((length, rank), BF),
        pltpu.VMEM((rank, length), BF),
        pltpu.VMEM((length, tile), BF),
        pltpu.VMEM((SUB + 8, chans), F32),
        pltpu.VMEM((length, inner), F32),
        pltpu.VMEM((length, inner), F32),
        pltpu.VMEM((steps * 8, inner), F32),
        pltpu.VMEM((length, SUB), F32),
    ]
    if with_grads:
        other = lambda i: sub(i) - steps
        args += [cot, g2, low_t, cot, g2, low_t, *stats, chosen]
        in_specs += [row(width), row(inner), lanes(rank)]
        in_specs += [
            pl.BlockSpec((SUB, width), lambda i, me: (other(i), 0)),
            pl.BlockSpec((SUB, inner), lambda i, me: (other(i), 0)),
            pl.BlockSpec((rank, SUB), lambda i, me: (0, other(i))),
            *[pl.BlockSpec((stats[0].shape[0], SUB), lambda i, me: (0, other(i)))] * 4,
            one(chosen),
        ]
        out_specs.append(kept(rank, inner + width + SUB))
        out_shape.append(jax.ShapeDtypeStruct((rank, inner + width + SUB), BF))
        scratch = [pltpu.VMEM((rank, inner + width), F32), *scratch]
    return pl.pallas_call(
        functools.partial(backward_half, with_grads=with_grads),
        grid_spec=pltpu.PrefetchScalarGridSpec(
            num_scalar_prefetch=1,
            grid=(steps + width // tile,),
            in_specs=in_specs,
            out_specs=out_specs,
            scratch_shapes=scratch,
        ),
        out_shape=out_shape,
        compiler_params=params(),
        cost_estimate=takes(19),
        name="backward_half",
    )(me, *args)


def place(me_ref, pieces, out):
    own, behind, ahead, far_low, far_high = pieces
    share = own.shape[1]
    y, turn = me_ref[0], (me_ref[1] + 4 - pl.program_id(0)) % 4
    for d, part in ((0, own), (1, behind), (3, ahead)):
        out[pl.ds(pl.multiple_of(((y + 4 - d) % 4) * share, share), share), :] = part[0]
    far = pl.ds(pl.multiple_of(((y + 2) % 4) * share, share), share)

    @pl.when(turn < 2)
    def _():
        out[far, :] = far_low[0]

    @pl.when(turn >= 2)
    def _():
        out[far, :] = far_high[0]


def columns_of(stats_refs, cols):
    total = stats_refs[0][...] + stats_refs[1][...] + stats_refs[2][...] + stats_refs[3][...]
    rows, length = total.shape
    total = jnp.concatenate([total, jnp.zeros((SUB - rows, length), F32)], 0)
    for k in range(length // SUB):
        cols[k * SUB : (k + 1) * SUB, :] = total[:, k * SUB : (k + 1) * SUB].T
    return total


def finish_branch(me_ref, sum_ref, s0, s1, s2, s3, up_ref, o0, o1, o2, o3, cols):
    columns_of((s0, s1, s2, s3), cols)
    share = o0.shape[0]
    rank = up_ref.shape[0]
    for d, out in enumerate((o0, o1, o2, o3)):
        c = (me_ref[1] + d) % 4
        mine = cols[pl.ds(pl.multiple_of((c * 4 + me_ref[0]) * share, share), share), :]
        rn = lax.rsqrt(mine[:, 0:1] / INNER_CHANNELS + EPS_NORM)
        low = (mine[:, 8 : 8 + rank] * rn).astype(BF)
        total = sum_ref[pl.ds(pl.multiple_of(c * share, share), share), :].astype(F32)
        out[...] = (total * rn + dot_nn(low, up_ref[...])).astype(BF)


def run_to_context(kernel, me, args, share, width, scratch, name):
    return pl.pallas_call(
        kernel,
        grid_spec=pltpu.PrefetchScalarGridSpec(
            num_scalar_prefetch=1,
            grid=(1,),
            in_specs=[one(a) for a in args],
            out_specs=[kept(share, width)] * 4,
            scratch_shapes=[scratch],
        ),
        out_shape=[jax.ShapeDtypeStruct((share, width), BF)] * 4,
        compiler_params=params(),
        cost_estimate=takes(3),
        name=name,
    )(me, *args)


def in_grads(me_ref, adapters_ref, *refs):
    early, late, (up0_ref, up1_ref, normed_ref), outs, (sent_ref, held) = (
        refs[:4], refs[4:8], refs[8:11], refs[11:15], refs[15:]
    )
    half = held.shape[0] // 2
    rank, length = up0_ref.shape[0], normed_ref.shape[0]
    added = lambda refs, *at: sum(r[at].astype(F32) for r in refs[1:]) + refs[0][at].astype(F32)
    for at, parts in ((0, early), (half, late)):
        held[at : at + half, :] = added(parts, slice(0, half)).astype(BF)
    share = outs[0].shape[0]
    for d, out in enumerate(outs):
        c = (me_ref[1] + d) % 4
        out[...] = held[pl.ds(pl.multiple_of(c * share, share), share), :]
    ranks = [added(parts, slice(half, half + rank), slice(0, length // 2)) for parts in (early, late)]
    width, inner2 = normed_ref.shape[1], up0_ref.shape[1]
    sent_ref[:, 0:width] = dot_nn(jnp.concatenate(ranks, 1).astype(BF), normed_ref[...]).astype(BF)
    sent_ref[:, width : width + inner2] = (up0_ref[...] + up1_ref[...]).astype(BF)
    sent_ref[:, width + inner2 :] = (lane((rank, SUB), 1) == adapters_ref[me_ref[1]]).astype(BF)


def run_in_grads(me, adapters, early, late, up0, up1, normed, share):
    rank, inner2 = up0.shape
    width = normed.shape[1]
    columns = width + inner2 + SUB
    args = (*early, *late, up0, up1, normed)
    return pl.pallas_call(
        in_grads,
        grid_spec=pltpu.PrefetchScalarGridSpec(
            num_scalar_prefetch=2,
            grid=(1,),
            in_specs=[one(a) for a in args],
            out_specs=[*[kept(share, width)] * 4, kept(rank, columns)],
            scratch_shapes=[pltpu.VMEM((4 * share, width), BF)],
        ),
        out_shape=[*[jax.ShapeDtypeStruct((share, width), BF)] * 4, jax.ShapeDtypeStruct((rank, columns), BF)],
        compiler_params=params(),
        cost_estimate=takes(3),
        name="in_grads",
    )(me, adapters, *args)


def finish_out(me_ref, p0, p1, p2, p3, p4, tokens_ref, out_ref, held):
    place(me_ref, (p0, p1, p2, p3, p4), held)
    out_ref[0] = (tokens_ref[0].astype(F32) + held[...].astype(F32)).astype(BF)


def finish_grad(me_ref, p0, p1, p2, p3, p4, tokens_ref, cot_ref, gain_ref, out_ref, held):
    place(me_ref, (p0, p1, p2, p3, p4), held)
    t = tokens_ref[0].astype(F32)
    rms = lax.rsqrt(jnp.mean(t * t, -1, keepdims=True) + EPS_NORM)
    pulled = held[...].astype(F32) * gain_ref[...]
    slope = rms * rms * rms * jnp.mean(pulled * t, -1, keepdims=True)
    out_ref[0] = rms * pulled - t * slope + cot_ref[0].astype(F32)


def piece_specs(pieces):
    share, width = pieces[0].shape[1:]
    half = pieces[0].shape[0] // 2
    turn = lambda s, me: (me[1] + 4 - s) % 4
    full = pl.BlockSpec((1, share, width), lambda s, me: (turn(s, me), 0, 0))
    return [
        full, full, full,
        pl.BlockSpec((1, share, width), lambda s, me: (jnp.minimum(turn(s, me), half - 1), 0, 0)),
        pl.BlockSpec((1, share, width), lambda s, me: (jnp.maximum(turn(s, me) - half, 0), 0, 0)),
    ]


def run_finish(kernel, me, pieces, extra, dtype, name):
    seqs, block, width = extra[0].shape
    seq = pl.BlockSpec((1, block, width), lambda s, me: (s, 0, 0))
    specs = [seq if a.ndim == 3 else whole(a) for a in extra]
    return pl.pallas_call(
        kernel,
        grid_spec=pltpu.PrefetchScalarGridSpec(
            num_scalar_prefetch=1,
            grid=(seqs,),
            in_specs=[*piece_specs(pieces), *specs],
            out_specs=seq,
            scratch_shapes=[pltpu.VMEM((block, width), BF)],
        ),
        out_shape=jax.ShapeDtypeStruct((seqs, block, width), dtype),
        compiler_params=params(30),
        cost_estimate=takes(5),
        name=name,
    )(me, *[pltpu.with_memory_space_constraint(a, pltpu.HBM) if a.ndim == 3 else a for a in (*pieces, *extra)])


def fill_tables(all_ref, *outs):
    table, rank = outs[0].shape[0], outs[0].shape[1]
    rows, columns = all_ref.shape
    spread = (lane((SUB, table * rank), 0) == lane((SUB, table * rank), 1) // rank).astype(BF)
    place = dot_nn(all_ref[:, columns - SUB :], spread)
    same = lane((rows, table * rank), 0) % rank == lane((rows, table * rank), 1) % rank
    place = jnp.where(same, place, 0.0).T.astype(BF)
    at = 0
    for out in outs:
        slots = out.shape[2:-1] or (1,)
        for slot in range(slots[0]):
            here = dot_nn(place, all_ref[:, at : at + out.shape[-1]])
            for a in range(table):
                if out.ndim == 3:
                    out[a] = here[a * rank : (a + 1) * rank, :]
                else:
                    out[a, :, slot, :] = here[a * rank : (a + 1) * rank, :]
            at += out.shape[-1]


def run_tables(everything, table, rank, widths):
    return pl.pallas_call(
        fill_tables,
        out_shape=[jax.ShapeDtypeStruct((table, rank, *w), F32) for w in widths],
        compiler_params=params(),
        cost_estimate=takes(3),
        name="fill_tables",
    )(everything)


def shifted_by(value, axis, distance):
    size = lax.axis_size(axis)
    return lax.ppermute(value, axis, [(i, (i + distance) % size) for i in range(size)])


def tie(*values):
    return lax.optimization_barrier(values)


def ring_near(own, axis):
    return shifted_by(own, axis, 1), shifted_by(own, axis, -1)


def ring_far(near, axis):
    half = near[0].shape[0] // 2
    return shifted_by(near[0][:half], axis, 1), shifted_by(near[1][half:], axis, -1)


def delivered(pieces, axis):
    return [pieces[0]] + [shifted_by(p, axis, d) for d, p in enumerate(pieces) if d]


def added(parts):
    return sum(p.astype(F32) for p in parts[1:]) + parts[0].astype(F32)


def shared(value, axis):
    return [value] + [shifted_by(value, axis, d) for d in range(1, lax.axis_size(axis))]


def swapped(value, axis):
    return lax.all_to_all(value, axis, 0, 0, tiled=True)


def per_device(
    tokens, output_cotangent, segments, sequence_adapter, input_norm_gain,
    gate_x_projection_weight, bc_projection_weight, step_projection_weight,
    x_convolution_taps, x_convolution_bias, bc_convolution_taps, bc_convolution_bias,
    step_size_bias, log_decay_rate, head_skip_gain, gated_norm_gain, output_projection_weight,
    in_adapter_down, in_adapter_up, out_adapter_down, out_adapter_up,
):
    seqs, block, width = tokens.shape
    inner = gate_x_projection_weight.shape[2]
    heads = step_projection_weight.shape[1]
    rank = in_adapter_down.shape[2]
    ny, nz = lax.axis_size("tensor"), lax.axis_size("context")
    my, mz = lax.axis_index("tensor"), lax.axis_index("context")
    me = jnp.stack([my, mz]).astype(jnp.int32)
    length = block * nz
    share = block // ny

    rows = gate_x_projection_weight.shape[0]
    packed = jnp.concatenate(
        [
            gate_x_projection_weight.reshape(rows, 2 * inner),
            bc_projection_weight,
            step_projection_weight,
            jnp.zeros((rows, SUB - heads), BF),
            output_projection_weight.T,
        ],
        1,
    )
    full = lax.all_gather(packed, ("fsdp", "context"), axis=0, tiled=True)

    quarters = lambda a: [
        lax.dynamic_slice(a, ((mz + d) % nz, my * share, 0), (1, share, width)) for d in range(nz)
    ]
    tokens_s, cot_later, segments = tie(delivered(quarters(tokens), "context"), output_cotangent, segments)
    tokens_near = ring_near(jnp.concatenate(tokens_s, 0), "tensor")
    tokens_s = jnp.concatenate(tokens_s, 0)
    to_lanes = lambda a: jnp.pad(a, (0, SUB - heads))
    vec = jnp.concatenate(
        [
            x_convolution_bias, bc_convolution_bias, gated_norm_gain, input_norm_gain,
            to_lanes(step_size_bias), to_lanes(log_decay_rate), to_lanes(head_skip_gain),
        ]
    )[None]
    marks, taps, conv_bias, par, skip, gain, norm_gain, down_in, up_in, down_out, up_out = run_prepare(
        me, sequence_adapter, swapped(segments, "context").reshape(nz, block), vec, x_convolution_taps, bc_convolution_taps,
        in_adapter_down.transpose(0, 2, 1), in_adapter_up, out_adapter_down.transpose(0, 2, 1), out_adapter_up, width,
    )
    chosen = jnp.full((1, SUB), lax.dynamic_index_in_dim(sequence_adapter, mz, 0, False).astype(F32))
    pick = (jnp.arange(inner)[:, None] // (inner // heads) == jnp.arange(SUB)[None, :]).astype(BF)
    lam, edge = jnp.zeros((SUB, inner), F32), jnp.zeros((8, taps.shape[1]), F32)

    tokens_near, marks, cot_s = tie(tokens_near, marks, delivered(quarters(cot_later), "context"))
    normed, low_rank = run_rows(near_rows, me, (tokens_s, *tokens_near), down_in, norm_gain, (), "near_rows")
    tokens_far, cot_s, normed = tie(ring_far(tokens_near, "tensor"), jnp.concatenate(cot_s, 0), normed)
    cot_parts = shared(cot_s, "tensor")
    normed, low_rank = run_rows(far_rows, me, tokens_far, down_in, norm_gain, (normed, low_rank), "far_rows")
    gx, rank_t, part, dt, run, run_turned, y, xc, bc, slope, g2, states, out_all = run_forward(
        normed, low_rank, up_in, full, down_out, marks, taps, conv_bias, par, skip, gain
    )
    g2, out_all, cot_parts = tie(g2, out_all, cot_parts)
    out_sum = lax.psum_scatter(out_all.reshape(length, width), "tensor", scatter_dimension=0, tiled=True)
    dn, stats, cot, d_low_t = run_pull_back(me, cot_parts, full, up_out, g2, part, down_out)
    stats_all = shared(stats, "tensor")

    backward = lambda half, *carried, **more: run_backward(
        me, half, gx, dt, run, run_turned, xc, bc, slope, y, dn, states, stats_all, marks, taps, par, skip, gain, pick,
        full, down_in, up_in, rank_t, *carried, **more,
    )
    *late, lam, edge, late_up, sent = backward(1, lam, edge, cot=cot, g2=g2, low_t=d_low_t, chosen=chosen)
    sent_out = lax.all_gather(sent, ("fsdp", "context"), axis=0, tiled=True)
    lam, late = tie(lam, late)
    late_parts = delivered(late, "tensor")
    *early, _, _, early_up = backward(0, lam, edge)
    early, late_parts, out_sum = tie(early, late_parts, out_sum)
    early_parts = delivered(early, "tensor")
    scratch = pltpu.VMEM((length, SUB), F32)
    branch = run_to_context(finish_branch, me, (out_sum, *stats_all, up_out), share, width, scratch, "finish_branch")
    branch_parts = delivered(branch, "context")
    early_parts, branch_parts = tie(early_parts, branch_parts)
    branch_q = jnp.stack(branch_parts)
    out_near = ring_near(branch_q, "tensor")
    *d_in, sent = run_in_grads(
        me, sequence_adapter, early_parts, late_parts, early_up, late_up, normed, share
    )
    sent_all = lax.all_gather(sent, ("fsdp", "context"), axis=0, tiled=True)
    d_in_parts = delivered(d_in, "context")
    d_in_parts, out_near, sent = tie(d_in_parts, out_near, sent)
    d_in_q = jnp.stack(d_in_parts)
    d_in_near = ring_near(d_in_q, "tensor")
    out_far = ring_far(out_near, "tensor")
    table = in_adapter_down.shape[0]
    out_tables = run_tables(sent_out, table, rank, ((inner,), (width,)))
    d_in_near, out_far, out_tables = tie(d_in_near, out_far, out_tables)
    d_in_far = ring_far(d_in_near, "tensor")
    layer_out = run_finish(finish_out, me, (branch_q, *out_near, *out_far), (tokens,), BF, "finish_out")
    layer_out, d_in_far = tie(layer_out, d_in_far)
    grad_tokens = run_finish(
        finish_grad, me, (d_in_q, *d_in_near, *d_in_far), (tokens, output_cotangent, norm_gain), F32, "finish_grad"
    )
    in_tables = run_tables(sent_all, table, rank, ((width,), (2, inner)))
    return (
        layer_out,
        grad_tokens,
        in_tables[0].transpose(0, 2, 1),
        in_tables[1],
        out_tables[0].transpose(0, 2, 1),
        out_tables[1],
    )


def solution(mesh):
    placed = (
        P("fsdp", "context", None),
        P("fsdp", "context", None),
        P("fsdp", "context"),
        P("fsdp"),
        P(),
        P(("fsdp", "context"), None, "tensor"),
        P(("fsdp", "context"), None),
        P(("fsdp", "context"), "tensor"),
        P(None, "tensor"),
        P("tensor"),
        P(),
        P(),
        P("tensor"),
        P("tensor"),
        P("tensor"),
        P("tensor"),
        P("tensor", ("fsdp", "context")),
        P(),
        P(None, None, None, "tensor"),
        P(None, "tensor", None),
        P(),
    )
    return jax.shard_map(
        per_device,
        mesh=mesh,
        in_specs=placed,
        out_specs=(
            P("fsdp", "context", None),
            P("fsdp", "context", None),
            P(),
            P(None, None, None, "tensor"),
            P(None, "tensor", None),
            P(),
        ),
        check_vma=False,
    )
```

```python
import functools

import jax
import jax.numpy as jnp
from jax import lax
from jax.experimental import pallas as pl
from jax.experimental.pallas import tpu as pltpu
from jax.sharding import PartitionSpec as P

INNER_CHANNELS = 3072
EPS_NORM = 1e-05
SUB = 128
NEG = -1e30
BF = jnp.bfloat16
F32 = jnp.float32
HIGHEST = lax.Precision.HIGHEST


def dot_nn(a, b):
    return lax.dot_general(a, b, (((1,), (0,)), ((), ())), preferred_element_type=F32)


def dot_nt(a, b):
    return lax.dot_general(a, b, (((1,), (1,)), ((), ())), preferred_element_type=F32)


def dot_tn(a, b):
    return lax.dot_general(a, b, (((0,), (0,)), ((), ())), preferred_element_type=F32)


def softplus(v):
    return jnp.maximum(v, 0.0) + jnp.log1p(jnp.exp(-jnp.abs(v)))


def lane(shape, dim):
    return lax.broadcasted_iota(jnp.int32, shape, dim)


def wide(column):
    return jnp.broadcast_to(column, (SUB, SUB))


def decays(raw, par_ref):
    dt = softplus(raw + par_ref[0:1, :])
    lower = (lane((SUB, SUB), 0) >= lane((SUB, SUB), 1)).astype(F32)
    run = jnp.dot(lower, dt * par_ref[1:2, :], precision=HIGHEST, preferred_element_type=F32)
    return dt, run


def scan_forward(
    k, gx, dt_ref, run_ref, rows_ref, marks_ref, taps_ref, bias_ref, skip_ref, gain_ref, down_ref,
    y_ref, xc_ref, bc_ref, slope_ref, g2_ref, states_ref, stats_ref, state, ext,
):
    inner = skip_ref.shape[1]
    chans = ext.shape[1]
    rows = pl.ds(pl.multiple_of(k * SUB, SUB), SUB)

    def strip(ref, at):
        each = ref.shape[2] // SUB
        return ref[at // each, rows, (at % each) * SUB : (at % each + 1) * SUB].astype(F32)

    @pl.when(k == 0)
    def _():
        state[...] = jnp.zeros_like(state)
        ext[0:8, :] = jnp.zeros((8, chans), F32)

    @pl.when(k > 0)
    def _():
        ext[0:8, :] = ext[SUB : SUB + 8, :]

    for c in range(chans // SUB):
        ext[8 : SUB + 8, c * SUB : (c + 1) * SUB] = strip(gx, inner // SUB + c)
    near = [wide(marks_ref[:, k : k + 1]) for k in range(3)]
    linked = wide(marks_ref[:, 3:4])
    ending = wide(marks_ref[:, 4:5])
    ids = wide(marks_ref[:, 5:6])
    passing = marks_ref[0:1, 6:7]
    left = lane((SUB, SUB), 1) < 64

    def conv(sl):
        pre = bias_ref[:, sl] + taps_ref[3:4, sl] * ext[8 : SUB + 8, sl]
        for k in range(1, 4):
            pre = pre + taps_ref[3 - k : 4 - k, sl] * (ext[8 - k : SUB + 8 - k, sl] * near[k - 1])
        sig = jax.nn.sigmoid(pre)
        out = (pre * sig).astype(BF)
        slope_ref[:, sl] = (sig * (1.0 + pre * (1.0 - sig))).astype(BF)
        return out

    b_low = conv(slice(inner, inner + SUB))
    c_low = conv(slice(inner + SUB, inner + 2 * SUB))
    bc_ref[:, 0:SUB] = b_low
    bc_ref[:, SUB : 2 * SUB] = c_low
    b_turned = b_low.astype(F32).T.astype(BF)
    dt, run = dt_ref[rows, :], run_ref[rows, :]
    run_rows = rows_ref[pl.ds(pl.multiple_of(k * 16, 16), 16), :]
    allowed = (ids == ids.T) & (lane((SUB, SUB), 0) >= lane((SUB, SUB), 1))
    mask = jnp.where(allowed, 0.0, NEG)
    cross = dot_nt(c_low, b_low)
    square = jnp.zeros((SUB, SUB), F32)
    for p in range(inner // SUB):
        sl = slice(p * SUB, (p + 1) * SUB)
        x_low = conv(sl)
        xc_ref[:, sl] = x_low
        x = x_low.astype(F32)
        run0, run1 = wide(run[:, 2 * p : 2 * p + 1]), wide(run[:, 2 * p + 1 : 2 * p + 2])
        run_p = jnp.where(left, run0, run1)
        dt_p = jnp.where(left, wide(dt[:, 2 * p : 2 * p + 1]), wide(dt[:, 2 * p + 1 : 2 * p + 2]))
        m0 = (jnp.exp(run0 - run_rows[2 * p : 2 * p + 1, :] + mask) * cross).astype(BF)
        m1 = (jnp.exp(run1 - run_rows[2 * p + 1 : 2 * p + 2, :] + mask) * cross).astype(BF)
        xdt = x * dt_p
        split = jnp.concatenate([jnp.where(left, xdt, 0.0), jnp.where(left, 0.0, xdt)], 0).astype(BF)
        before = state[:, sl]
        before_low = before.astype(BF)
        states_ref[0, :, sl] = before_low
        y = dot_nn(jnp.concatenate([m0, m1], 1), split)
        y = y + jnp.exp(run_p) * linked * dot_nn(c_low, before_low) + skip_ref[:, sl] * x
        last = run_p[SUB - 1 : SUB, :]
        toward = (xdt * (jnp.exp(last - run_p) * ending)).astype(BF)
        state[:, sl] = (jnp.exp(last) * passing) * before + dot_nn(b_turned, toward)
        z = strip(gx, p)
        gated = y * (z * jax.nn.sigmoid(z))
        y_ref[:, sl] = y.astype(BF)
        g2_ref[:, sl] = (gated * gain_ref[:, sl]).astype(BF)
        square = square + gated * gated
    stats_ref[0:8, rows] = lane_rows(square)
    stats_ref[8:, rows] = dot_nt(down_ref[...], g2_ref[...])


def forward_all(
    normed, rank, up_ref, w_ref, w0_ref, w1_ref, out_down_ref, marks_ref, taps_ref, bias_ref, par_ref, skip_ref, gain_ref,
    gx_hbm, rank_t_ref, stats_ref, dt_ref, run_ref, rows_ref, y_ref, xc_ref, bc_ref, slope_ref, g2_ref, states_ref, out_ref,
    gx, state, ext, g2_all, held, sems,
):
    step = pl.program_id(0)
    tiles, length, tile = gx.shape

    def copy_gx(j):
        return pltpu.make_async_copy(gx.at[j], gx_hbm.at[:, pl.ds(j * tile, tile)], sems.at[j])

    @pl.when(step == 0)
    def _():
        turn_rank(rank[...].astype(F32), rank_t_ref)

    for j in range(tiles):

        @pl.when(step == j)
        def _():
            gx[j] = (dot_nn(normed[...], w_ref[...]) + dot_nn(rank[...], up_ref[...])).astype(BF)
            copy_gx(j).start()

    @pl.when(step == tiles - 1)
    def _():
        inner, chans = skip_ref.shape[1], taps_ref.shape[1]
        at, col = divmod(2 * inner + chans - inner, tile)
        for i in range(length // SUB):
            here = slice(i * SUB, (i + 1) * SUB)
            dt, run = decays(gx[at, here, col : col + SUB].astype(F32), par_ref)
            dt_ref[here, :] = dt
            run_ref[here, :] = run
            rows_ref[i * 16 : (i + 1) * 16, :] = run.T[0:16, :]

    done = tiles + length // SUB

    @pl.when((step >= tiles) & (step < done))
    def _():
        scan_forward(
            step - tiles, gx, dt_ref, run_ref, rows_ref, marks_ref, taps_ref, bias_ref, skip_ref, gain_ref, out_down_ref,
            y_ref, xc_ref, bc_ref, slope_ref, g2_ref, states_ref, stats_ref, state, ext,
        )
        g2_all[pl.ds(pl.multiple_of((step - tiles) * SUB, SUB), SUB), :] = g2_ref[...]

    @pl.when(step >= done)
    def _():
        cut = w0_ref.shape[1]
        held[...] = (dot_nt(g2_all[:, 0:cut], w0_ref[...]) + dot_nt(g2_all[:, cut:], w1_ref[...])).astype(BF)
        owners, rows, _ = out_ref.shape
        share = 64
        for c in range(rows // share):
            for y in range(owners):
                at = (c * owners + y) * share
                out_ref[y, c * share : (c + 1) * share, :] = held[at : at + share, :]

    @pl.when(step == pl.num_programs(0) - 1)
    def _():
        for j in range(tiles):
            copy_gx(j).wait()


def backward_half(
    me_ref, z_ref, raw_ref, dt_ref, run_ref, rows_ref, xc_ref, bc_ref, slope_ref, y_ref, dn_ref, states_ref, s0_ref, s1_ref, s2_ref, s3_ref, marks_ref,
    taps_ref, par_ref, skip_ref, gain_ref, pick_ref, lam_in_ref, edge_in_ref,
    w_hbm, down_ref, up_ref, rank_t_ref, *rest, with_grads,
):
    if with_grads:
        (cot0_ref, g20_ref, low0_ref, cot1_ref, g21_ref, low1_ref, q0_ref, q1_ref, q2_ref, q3_ref, chosen_ref), rest = rest[:11], rest[11:]
        o0, o1, o2, o3, lam, edge_ref, up_grad_ref, grads_ref, *scratch = rest
        grads, *scratch = scratch
    else:
        o0, o1, o2, o3, lam, edge_ref, up_grad_ref, *scratch = rest
    d_all, low, pushed, held, ext, to_dt, to_run, to_end, shifted, w_all, sems = scratch
    step = pl.program_id(0)
    steps = d_all.shape[0] // SUB
    tiles, tile, columns = w_all.shape

    def copy_w(j):
        return pltpu.make_async_copy(w_hbm.at[pl.ds(j * tile, tile), pl.ds(0, columns)], w_all.at[j], sems.at[j])

    @pl.when(step == 0)
    def _():
        for j in range(tiles):
            copy_w(j).start()

    if with_grads:

        @pl.when(step == 0)
        def _():
            grads[...] = jnp.zeros_like(grads)

        @pl.when(step < steps)
        def _():
            cut = g20_ref.shape[1]
            for stats, low_t_ref, cot_ref, g2_ref in (
                (summed((s0_ref, s1_ref, s2_ref, s3_ref)), low0_ref, cot0_ref, g20_ref),
                (summed((q0_ref, q1_ref, q2_ref, q3_ref)), low1_ref, cot1_ref, g21_ref),
            ):
                rn_row = lax.rsqrt(stats[0:1, :] / INNER_CHANNELS + EPS_NORM)
                grads[:, 0:cut] += dot_nn((low_t_ref[...].astype(F32) * rn_row).astype(BF), g2_ref[...])
                grads[:, cut:] += dot_nn((stats[8:, :] * rn_row).astype(BF), cot_ref[...])

        @pl.when(step == steps)
        def _():
            grads_ref[:, 0 : grads.shape[1]] = grads[...].astype(BF)
            mine = lane((grads.shape[0], SUB), 1).astype(F32) == chosen_ref[...]
            grads_ref[:, grads.shape[1] :] = jnp.where(mine, 1.0, 0.0).astype(BF)

    @pl.when(step < steps)
    def _():
        at = pl.multiple_of((steps - 1 - step) * SUB, SUB)
        scan_backward(
            step, at, d_all.at[pl.ds(at, SUB), :], z_ref, dt_ref, run_ref, rows_ref, xc_ref, bc_ref, slope_ref, y_ref, dn_ref, states_ref,
            (s0_ref, s1_ref, s2_ref, s3_ref), marks_ref, taps_ref, par_ref, skip_ref, gain_ref, pick_ref, lam_in_ref, edge_in_ref,
            lam, ext, to_dt, to_run, to_end,
        )
        gate = d_all[pl.ds(at, SUB), 0 : up_ref.shape[1]]
        part = dot_nt(gate, up_ref[...])
        rank = part.shape[1]
        low[pl.ds(at, SUB), :] = part.astype(BF)
        part = jnp.concatenate([part, jnp.zeros((SUB, SUB - rank), F32)], 1)
        pushed[:, pl.ds(at, SUB)] = part.T[0:rank, :].astype(BF)
        up_grad = dot_nn(rank_t_ref[...], gate)

        @pl.when(step == 0)
        def _():
            up_grad_ref[...] = up_grad

        @pl.when(step > 0)
        def _():
            up_grad_ref[...] += up_grad

        shifted[pl.ds(at, SUB), :] = raw_ref[...].astype(F32) + par_ref[0:1, :]

    @pl.when(step == steps - 1)
    def _():
        edge_ref[...] = ext[0:8, :]

    @pl.when(step == steps)
    def _():
        def by_head(v):
            high = v.astype(BF)
            return dot_nn(high, pick_ref[...]) + dot_nn((v - high.astype(F32)).astype(BF), pick_ref[...])

        d_run, d_dt, d_end = by_head(to_run[...]), by_head(to_dt[...]), by_head(to_end[...])
        upper = (lane((SUB, SUB), 0) <= lane((SUB, SUB), 1)).astype(F32)
        for i in range(steps):
            here = slice(i * SUB, (i + 1) * SUB)
            block = d_run[here] + jnp.where(lane((SUB, SUB), 0) == SUB - 1, d_end[i * 8 : i * 8 + 1], 0.0)
            d_log = jnp.dot(upper, block, precision=HIGHEST, preferred_element_type=F32)
            d_raw = (d_dt[here] + par_ref[1:2, :] * d_log) * jax.nn.sigmoid(shifted[here, :])
            d_all[here, d_all.shape[1] - SUB :] = d_raw.astype(BF)

    for j in range(tiles):

        @pl.when(step == steps + j)
        def _():
            copy_w(j).wait()

    @pl.when(step >= steps)
    def _():
        held[...] = (dot_nt(d_all[...], w_all[step - steps]) + dot_nn(low[...], down_ref[...])).astype(BF)
        deal(me_ref[0], held, (o0, o1, o2, o3))

    for out in (o0, o1, o2, o3):

        @pl.when(step == steps)
        def _():
            out[out.shape[0] - pushed.shape[0] :, :] = pushed[...]

        @pl.when(step > steps)
        def _():
            out[out.shape[0] - pushed.shape[0] :, :] = jnp.zeros_like(pushed)


def scan_backward(
    step, at, da_ref, z_ref, dt_ref, run_ref, rows_ref, xc_ref, bc_ref, slope_ref, y_ref, dn_ref, states_ref, stats_refs, marks_ref,
    taps_ref, par_ref, skip_ref, gain_ref, pick_ref, lam_in_ref, edge_in_ref,
    lam, ext, to_dt, to_run, to_end,
):
    inner = z_ref.shape[1]
    chans = ext.shape[1]

    @pl.when(step == 0)
    def _():
        lam[...] = lam_in_ref[...]
        ext[SUB : SUB + 8, :] = edge_in_ref[...]

    @pl.when(step > 0)
    def _():
        ext[SUB : SUB + 8, :] = ext[0:8, :]

    linked = wide(marks_ref[:, 3:4])
    ending = wide(marks_ref[:, 4:5])
    ids = wide(marks_ref[:, 5:6])
    passing = marks_ref[0:1, 6:7]
    later = [wide(marks_ref[:, 7 + k : 8 + k]) for k in range(3)]
    left = lane((SUB, SUB), 1) < 64
    stats = summed(stats_refs)
    rn_row = lax.rsqrt(stats[0:1, :] / INNER_CHANNELS + EPS_NORM)
    rn = jnp.broadcast_to(rn_row, (SUB, SUB)).T
    kappa = jnp.broadcast_to(rn_row * rn_row * rn_row * stats[1:2, :] / INNER_CHANNELS, (SUB, SUB)).T
    dt, run, run_rows = dt_ref[...], run_ref[...], rows_ref[...]
    tokens = pl.ds(at, SUB)
    b_low, c_low = bc_ref[:, 0:SUB], bc_ref[:, SUB : 2 * SUB]
    c_turned = c_low.astype(F32).T.astype(BF)
    allowed = (ids == ids.T) & (lane((SUB, SUB), 0) <= lane((SUB, SUB), 1))
    mask = jnp.where(allowed, 0.0, NEG)
    cross = dot_nt(b_low, c_low)
    d_cross = jnp.zeros((SUB, SUB), F32)
    d_b = jnp.zeros((SUB, SUB), F32)
    d_c = jnp.zeros((SUB, SUB), F32)
    for p in range(inner // SUB):
        sl = slice(p * SUB, (p + 1) * SUB)
        z = z_ref[:, sl].astype(F32)
        sig = jax.nn.sigmoid(z)
        silu = z * sig
        y = y_ref[:, sl].astype(F32)
        d_gated = rn * (dn_ref[:, sl].astype(F32) * gain_ref[:, sl]) - kappa * (y * silu)
        da_ref[:, sl] = (d_gated * y * sig * (1.0 + z * (1.0 - sig))).astype(BF)
        dy = d_gated * silu
        x = xc_ref[:, sl].astype(F32)
        run0, run1 = wide(run[:, 2 * p : 2 * p + 1]), wide(run[:, 2 * p + 1 : 2 * p + 2])
        run_p = jnp.where(left, run0, run1)
        dt_p = jnp.where(left, wide(dt[:, 2 * p : 2 * p + 1]), wide(dt[:, 2 * p + 1 : 2 * p + 2]))
        l0 = jnp.exp(run_rows[2 * p : 2 * p + 1, :] - run0 + mask)
        l1 = jnp.exp(run_rows[2 * p + 1 : 2 * p + 2, :] - run1 + mask)
        xdt = x * dt_p
        x_split = jnp.concatenate([jnp.where(left, xdt, 0.0), jnp.where(left, 0.0, xdt)], 0).astype(BF)
        dy_split = jnp.concatenate([jnp.where(left, dy, 0.0), jnp.where(left, 0.0, dy)], 0).astype(BF)
        d_m = dot_nt(x_split, dy.astype(BF))
        d_cross = d_cross + l0 * d_m[0:SUB] + l1 * d_m[SUB : 2 * SUB]
        m = jnp.concatenate([l0 * cross, l1 * cross], 1).astype(BF)
        lam_p = lam[:, sl]
        lam_low = lam_p.astype(BF)
        last = run_p[SUB - 1 : SUB, :]
        toward = jnp.exp(last - run_p) * ending
        carried = toward * dot_nn(b_low, lam_low)
        d_xt = dot_nn(m, dy_split) + carried
        skip = skip_ref[:, sl]
        ext[0:SUB, sl] = (dt_p * d_xt + skip * dy) * slope_ref[:, sl].astype(F32)
        x_dx = x * d_xt
        to_dt[tokens, sl] = x_dx
        to_run[tokens, sl] = dy * (y - skip * x) - dt_p * x_dx
        reached = (jnp.exp(run_p) * linked * dy).astype(BF)
        before_low = states_ref[0, :, sl]
        keep = jnp.exp(last) * passing
        end = jnp.sum(xdt * carried, 0, keepdims=True) + keep * jnp.sum(
            lam_p * before_low.astype(F32), 0, keepdims=True
        )
        to_end[pl.ds(pl.multiple_of(at // 16, 8), 8), sl] = jnp.broadcast_to(end, (8, SUB))
        d_b = d_b + dot_nt((xdt * toward).astype(BF), lam_low)
        d_c = d_c + dot_nt(reached, before_low)
        lam[:, sl] = keep * lam_p + dot_nn(c_turned, reached)
    d_cross_low = d_cross.astype(BF)
    d_b = d_b + dot_nn(d_cross_low, c_low)
    d_c = d_c + dot_nn(d_cross.T.astype(BF), b_low)
    ext[0:SUB, inner : inner + SUB] = d_b * slope_ref[:, inner : inner + SUB].astype(F32)
    ext[0:SUB, inner + SUB : chans] = d_c * slope_ref[:, inner + SUB : chans].astype(F32)

    for s in range(chans // SUB):
        sl = slice(s * SUB, (s + 1) * SUB)
        acc = taps_ref[3:4, sl] * ext[0:SUB, sl]
        for k in range(1, 4):
            acc = acc + taps_ref[3 - k : 4 - k, sl] * (ext[k : SUB + k, sl] * later[k - 1])
        da_ref[:, inner + s * SUB : inner + (s + 1) * SUB] = acc.astype(BF)

def whole(a):
    return pl.BlockSpec(a.shape, lambda i, *_: (0,) * a.ndim)


def params(mib=60):
    return pltpu.CompilerParams(vmem_limit_bytes=mib << 20)


def takes(us):
    return pl.CostEstimate(flops=us * 100_000_000, bytes_accessed=us * 300_000, transcendentals=0)


def turn_rank(low, rank_t_ref):
    rank = low.shape[1]
    low = jnp.concatenate([low, jnp.zeros((low.shape[0], SUB - rank), F32)], 1)
    for k in range(low.shape[0] // SUB):
        here = slice(k * SUB, (k + 1) * SUB)
        rank_t_ref[:, here] = low[here, :].T[0:rank, :].astype(BF)


def low_products(rows_ref, down_ref, rank_ref, rank_t_ref):
    low = dot_nt(rows_ref[...], down_ref[...])
    rank_ref[...] = low.astype(BF)
    turn_rank(low, rank_t_ref)


def summed(refs):
    return refs[0][...].astype(F32) + refs[1][...].astype(F32) + refs[2][...].astype(F32) + refs[3][...].astype(F32)


def lane_rows(v):
    return lax.dot_general(
        jnp.ones((8, v.shape[1]), F32), v, (((1,), (1,)), ((), ())), precision=HIGHEST, preferred_element_type=F32
    )


def deal(me, held, outs):
    share = 64
    for c in range(held.shape[0] // (4 * share)):
        for d, out in enumerate(outs):
            at = pl.multiple_of((c * 4 + (me + d) % 4) * share, share)
            out[c * share : (c + 1) * share, :] = held[pl.ds(at, share), :]


def one(a):
    return pl.BlockSpec(a.shape, lambda i, *_: (0,) * a.ndim, pipeline_mode=pl.Buffered(1))


def kept(*shape):
    return pl.BlockSpec(shape, lambda i, *_: (0,) * len(shape))


def run_forward(normed, low_rank, up, weights, out_down, marks, taps, bias, par, skip, gain):
    length, width = normed.shape
    inner, chans = skip.shape[1], taps.shape[1]
    rank, columns = up.shape
    tile = 512
    tiles, steps, out_tiles = columns // tile, length // SUB, width // tile
    sub = lambda i: jnp.clip(i - tiles, 0, steps - 1)
    scan = lambda cols: pl.BlockSpec((SUB, cols), lambda i: (sub(i), 0))
    first = lambda i: jnp.minimum(i, tiles - 1)
    last = lambda i: jnp.maximum(i - tiles - steps, 0)
    at_out = 2 * (weights.shape[1] - inner) // inner
    return pl.pallas_call(
        forward_all,
        grid=(tiles + steps + out_tiles,),
        in_specs=[
            one(normed), one(low_rank),
            pl.BlockSpec((rank, tile), lambda i: (0, first(i))),
            pl.BlockSpec((width, tile), lambda i: (0, first(i))),
            pl.BlockSpec((tile, inner // 2), lambda i: (last(i), at_out)),
            pl.BlockSpec((tile, inner // 2), lambda i: (last(i), at_out + 1)),
            one(out_down), scan(marks.shape[1]), one(taps), one(bias), one(par), one(skip), one(gain),
        ],
        out_specs=[
            pl.BlockSpec(memory_space=pl.ANY), kept(rank, length), kept(8 + rank, length),
            kept(length, SUB), kept(length, SUB), kept(steps * 16, SUB),
            scan(inner), scan(inner), scan(2 * SUB), scan(chans), scan(inner),
            pl.BlockSpec((1, SUB, inner), lambda i: (sub(i), 0, 0)),
            pl.BlockSpec((4, length // 4, tile), lambda i: (0, 0, last(i))),
        ],
        scratch_shapes=[
            pltpu.VMEM((tiles, length, tile), BF),
            pltpu.VMEM((SUB, inner), F32),
            pltpu.VMEM((SUB + 8, chans), F32),
            pltpu.VMEM((length, inner), BF),
            pltpu.VMEM((length, tile), BF),
            pltpu.SemaphoreType.DMA((tiles,)),
        ],
        out_shape=[
            jax.ShapeDtypeStruct((length, columns), BF),
            jax.ShapeDtypeStruct((rank, length), BF),
            jax.ShapeDtypeStruct((8 + rank, length), F32),
            jax.ShapeDtypeStruct((length, SUB), F32),
            jax.ShapeDtypeStruct((length, SUB), F32),
            jax.ShapeDtypeStruct((steps * 16, SUB), F32),
            jax.ShapeDtypeStruct((length, inner), BF),
            jax.ShapeDtypeStruct((length, inner), BF),
            jax.ShapeDtypeStruct((length, 2 * SUB), BF),
            jax.ShapeDtypeStruct((length, chans), BF),
            jax.ShapeDtypeStruct((length, inner), BF),
            jax.ShapeDtypeStruct((steps, SUB, inner), BF),
            jax.ShapeDtypeStruct((4, length // 4, width), BF),
        ],
        compiler_params=params(),
        cost_estimate=takes(30),
        name="forward_all",
    )(normed, low_rank, up, weights, weights, weights, out_down, marks, taps, bias, par, skip, gain)


def prepare(
    me_ref, adapters_ref, seg_ref, vec_ref, x_taps_ref, bc_taps_ref, down_in_ref, up_in_ref, down_out_ref, up_out_ref,
    marks_ref, taps_ref, bias_ref, par_ref, skip_ref, gain_ref, norm_gain_ref, down_in, up_wide, down_out, up_out,
):
    chunks, block = seg_ref.shape
    each = block // SUB
    subs = chunks * each
    seg = seg_ref[...].astype(F32)
    rows = [seg[c : c + 1, h * SUB : (h + 1) * SUB] for c in range(chunks) for h in range(each)]
    own = jnp.concatenate(rows, 0)
    none = jnp.full((1, SUB), -1.0, F32)
    before = jnp.concatenate([none, *rows[:-1]], 0)
    after = jnp.concatenate([*rows[1:], none], 0)
    at = lane((subs, SUB), 1)
    last, last_before = (jnp.broadcast_to(v[:, SUB - 1 : SUB], own.shape) for v in (own, before))
    kinds = [own == jnp.where(at >= k, pltpu.roll(own, k, 1), pltpu.roll(before, k, 1)) for k in (1, 2, 3)]
    kinds += [own == last_before, own == last, None, last == last_before]
    kinds += [
        own == jnp.where(at < SUB - k, pltpu.roll(own, SUB - k, 1), pltpu.roll(after, SUB - k, 1)) for k in (1, 2, 3)
    ]
    kinds = [own if v is None else jnp.where(v, 1.0, 0.0) for v in kinds]
    count = marks_ref.shape[1]
    for i in range(subs):
        here = [v[i : i + 1, :] for v in kinds]
        full = jnp.concatenate([*here, jnp.zeros((SUB - len(here), SUB), F32)], 0)
        marks_ref[i * SUB : (i + 1) * SUB, :] = full.T[:, 0:count]
    inner = x_taps_ref.shape[1]
    chans = taps_ref.shape[1]
    taps_ref[:, 0:inner] = x_taps_ref[...]
    taps_ref[:, inner:] = bc_taps_ref[...]
    cuts = [0]
    for n in (chans, inner, norm_gain_ref.shape[1], SUB, SUB, SUB):
        cuts.append(cuts[-1] + n)
    piece = [vec_ref[:, a:b] for a, b in zip(cuts, cuts[1:])]
    bias_ref[...], gain_ref[...], norm_gain_ref[...] = piece[:3]
    par_ref[...] = jnp.concatenate([piece[3], -jnp.exp(piece[4]), jnp.zeros((6, SUB), F32)], 0)
    spread = jnp.where(lane((SUB, inner), 0) == lane((SUB, inner), 1) // 64, 1.0, 0.0)
    skip = jnp.dot(jnp.broadcast_to(piece[5], (8, SUB)), spread, precision=HIGHEST, preferred_element_type=F32)
    skip_ref[...] = skip[0:1, :]
    down_in[...], down_out[...], up_out[...] = down_in_ref[0], down_out_ref[0], up_out_ref[0]
    up_wide[...] = jnp.zeros_like(up_wide)
    for k in range(2):
        up_wide[:, k * inner : (k + 1) * inner] = up_in_ref[0, :, k, :]


def run_prepare(me, adapters, seg, vec, x_taps, bc_taps, down_in, up_in, down_out, up_out, norm_width):
    length = seg.shape[0] * seg.shape[1]
    inner, bc = x_taps.shape[1], bc_taps.shape[1]
    rank = up_in.shape[1]
    mine = lambda a: pl.BlockSpec((1, *a.shape[1:]), lambda i, me, ad: (ad[me[1]],) + (0,) * (a.ndim - 1))
    outs = [
        ((length, 16), F32), ((4, inner + bc), F32), ((1, inner + bc), F32), ((8, SUB), F32), ((1, inner), F32),
        ((1, inner), F32), ((1, norm_width), F32), (down_in.shape[1:], BF), ((rank, 2 * inner + 512), BF),
        (down_out.shape[1:], BF), (up_out.shape[1:], BF),
    ]
    return pl.pallas_call(
        prepare,
        grid_spec=pltpu.PrefetchScalarGridSpec(
            num_scalar_prefetch=2,
            grid=(1,),
            in_specs=[one(seg), one(vec), one(x_taps), one(bc_taps), mine(down_in), mine(up_in), mine(down_out), mine(up_out)],
            out_specs=[kept(*n) for n, _ in outs],
        ),
        out_shape=[jax.ShapeDtypeStruct(n, t) for n, t in outs],
        compiler_params=params(),
        cost_estimate=takes(2),
        name="prepare",
    )(me, adapters, seg, vec, x_taps, bc_taps, down_in, up_in, down_out, up_out)


def normed_rows(me_ref, blocks, down_ref, gain_ref, held, rows_hbm, rank_ref, sems):
    share = held.shape[1]
    copies = []
    for k, (c, back, rows) in enumerate(blocks):
        t = rows.astype(F32)
        rms = lax.rsqrt(jnp.mean(t * t, -1, keepdims=True) + EPS_NORM)
        held[k] = (t * rms * gain_ref[...]).astype(BF)
        at = pl.multiple_of((c * 4 + (me_ref[0] + 4 - back) % 4) * share, share)
        copies.append(pltpu.make_async_copy(held.at[k], rows_hbm.at[pl.ds(at, share), :], sems.at[k]))
        copies[-1].start()
        rank_ref[pl.ds(at, share), :] = dot_nt(held[k], down_ref[...]).astype(BF)
    for copy in copies:
        copy.wait()


def near_rows(me_ref, p0, p1, p2, down_ref, gain_ref, rows_hbm, rank_ref, held, sems):
    rank_ref[...] = jnp.zeros_like(rank_ref)
    blocks = [
        (c, back, part[(me_ref[1] + 4 - c) % 4]) for c in range(4) for back, part in ((0, p0), (1, p1), (3, p2))
    ]
    normed_rows(me_ref, blocks, down_ref, gain_ref, held, rows_hbm, rank_ref, sems)


def far_rows(me_ref, p3, p4, down_ref, gain_ref, rows_in, rank_in, rows_hbm, rank_ref, held, sems):
    rank_ref[...] = rank_in[...]
    blocks = []
    for c in range(4):
        turn = (me_ref[1] + 4 - c) % 4
        blocks.append((c, 2, jnp.where(turn < 2, p3[turn % 2], p4[turn % 2])))
    normed_rows(me_ref, blocks, down_ref, gain_ref, held, rows_hbm, rank_ref, sems)


def run_rows(kernel, me, pieces, down, gain, before, name):
    share, width = pieces[0].shape[1:]
    length = 16 * share
    rank = down.shape[0]
    count = sum(p.shape[0] for p in pieces)
    any_space = pl.BlockSpec(memory_space=pl.ANY)
    args = (*pieces, down, gain, *before)
    return pl.pallas_call(
        kernel,
        grid_spec=pltpu.PrefetchScalarGridSpec(
            num_scalar_prefetch=1,
            grid=(1,),
            in_specs=[*[one(a) for a in (*pieces, down, gain)], *([any_space, one(before[1])] if before else [])],
            out_specs=[any_space, kept(length, rank)],
            scratch_shapes=[pltpu.VMEM((count, share, width), BF), pltpu.SemaphoreType.DMA((count,))],
        ),
        out_shape=[jax.ShapeDtypeStruct((length, width), BF), jax.ShapeDtypeStruct((length, rank), BF)],
        input_output_aliases={len(args) - 1: 0} if before else {},
        compiler_params=params(),
        cost_estimate=takes(3),
        name=name,
    )(me, *args)


def pull_back(
    me_ref, p0, p1, p2, p3, up_ref, w_ref, g2_ref, part_ref, down_ref,
    dn_ref, stats_ref, cot_hbm, low_t_ref,
    cot, low, dots, sem,
):
    step = pl.program_id(0)
    copy_cot = pltpu.make_async_copy(cot, cot_hbm, sem)

    @pl.when(step == 0)
    def _():
        chunks, share, _ = p0.shape
        for c in range(chunks):
            for d, part in enumerate((p0, p1, p2, p3)):
                at = pl.multiple_of((c * 4 + (me_ref[0] + 4 - d) % 4) * share, share)
                cot[pl.ds(at, share), :] = part[(me_ref[1] + 4 - c) % 4]
        copy_cot.start()
        low_products(cot, up_ref, low, low_t_ref)
        dots[...] = jnp.zeros_like(dots)

    dn = dot_nn(cot[...], w_ref[...]) + dot_nn(low[...], down_ref[...])
    dn_ref[...] = dn.astype(BF)
    both = dn * g2_ref[...].astype(F32)
    total = dots[...]
    for k in range(both.shape[1] // SUB):
        total = total + both[:, k * SUB : (k + 1) * SUB]
    dots[...] = total

    @pl.when(step == pl.num_programs(0) - 1)
    def _():
        first = lane((8, stats_ref.shape[1]), 0) == 0
        top = jnp.where(first, part_ref[0:8, :], lane_rows(dots[...]))
        stats_ref[...] = jnp.concatenate([top, part_ref[8:, :]], 0).astype(BF)
        copy_cot.wait()


def run_pull_back(me, pieces, weights, up, g2, part, down, tile=384):
    width = pieces[0].shape[2]
    length, inner = g2.shape
    rank = down.shape[0]
    first = (weights.shape[1] - inner) // tile
    return pl.pallas_call(
        pull_back,
        grid_spec=pltpu.PrefetchScalarGridSpec(
            num_scalar_prefetch=1,
            grid=(inner // tile,),
            in_specs=[
                *[one(p) for p in pieces], one(up),
                pl.BlockSpec((width, tile), lambda j, me: (0, first + j)),
                pl.BlockSpec((length, tile), lambda j, me: (0, j)),
                one(part),
                pl.BlockSpec((rank, tile), lambda j, me: (0, j)),
            ],
            out_specs=[
                pl.BlockSpec((length, tile), lambda j, me: (0, j)), kept(*part.shape),
                pl.BlockSpec(memory_space=pl.ANY), kept(rank, length),
            ],
            scratch_shapes=[
                pltpu.VMEM((length, width), BF),
                pltpu.VMEM((length, rank), BF),
                pltpu.VMEM((length, SUB), F32),
                pltpu.SemaphoreType.DMA,
            ],
        ),
        out_shape=[
            jax.ShapeDtypeStruct((length, inner), BF),
            jax.ShapeDtypeStruct(part.shape, BF),
            jax.ShapeDtypeStruct((length, width), BF),
            jax.ShapeDtypeStruct((rank, length), BF),
        ],
        compiler_params=params(),
        cost_estimate=takes(8),
        name="pull_back",
    )(me, *pieces, up, weights, g2, part, down)


def dealt(rows, width, tile, at):
    spec = pl.BlockSpec((rows, tile), lambda j, me: (0, at(j)))
    return [spec] * 4, [jax.ShapeDtypeStruct((rows, width), BF)] * 4


def run_backward(
    me, half, gx, dt, run, run_rows, xc, bc, slope, y, dn, states, stats, marks, taps, par, skip, gain, pick,
    weights, down, up, rank_t, lam, edge, cot=None, g2=None, low_t=None, chosen=None,
):
    length = gx.shape[0] // 2
    inner, chans, width = skip.shape[1], taps.shape[1], weights.shape[0]
    rank = down.shape[0]
    up_block = pl.BlockSpec((rank, 2 * inner), lambda i, me: (0, 0), pipeline_mode=pl.Buffered(1))
    steps = length // SUB
    tile = 512
    assert tile == length
    top = (half + 1) * steps - 1
    sub = lambda i: jnp.maximum(top - i, half * steps)
    col = lambda i: jnp.maximum(i - steps, 0)
    row = lambda cols, at=0: pl.BlockSpec((SUB, cols), lambda i, me, at=at: (sub(i), at))
    lanes = lambda n: pl.BlockSpec((n, SUB), lambda i, me: (0, sub(i)))
    total = inner + chans + SUB
    specs, shapes = dealt(length // 4 + rank, width, tile, col)
    with_grads = cot is not None
    args = [
        gx, gx, dt, run, run_rows, xc, bc, slope, y, dn, states, *stats, marks, taps, par, skip, gain, pick, lam, edge,
        weights, down, up, rank_t,
    ]
    in_specs = [
        row(inner), row(SUB, (inner + chans) // SUB), row(SUB), row(SUB), pl.BlockSpec((16, SUB), lambda i, me: (sub(i), 0)),
        row(inner), row(2 * SUB), row(chans), row(inner), row(inner),
        pl.BlockSpec((1, SUB, inner), lambda i, me: (sub(i), 0, 0)),
        *[lanes(stats[0].shape[0])] * 4,
        row(marks.shape[1]), one(taps), one(par), one(skip), one(gain), one(pick), one(lam), one(edge),
        pl.BlockSpec(memory_space=pl.ANY),
        pl.BlockSpec((rank, tile), lambda i, me: (0, col(i))),
        up_block, lanes(rank),
    ]
    out_specs = [*specs, kept(*lam.shape), kept(*edge.shape), kept(rank, 2 * inner)]
    out_shape = [
        *shapes,
        jax.ShapeDtypeStruct(lam.shape, F32),
        jax.ShapeDtypeStruct(edge.shape, F32),
        jax.ShapeDtypeStruct((rank, 2 * inner), F32),
    ]
    scratch = [
        pltpu.VMEM((length, total), BF),
        pltpu.VMEM((length, rank), BF),
        pltpu.VMEM((rank, length), BF),
        pltpu.VMEM((length, tile), BF),
        pltpu.VMEM((SUB + 8, chans), F32),
        pltpu.VMEM((length, inner), F32),
        pltpu.VMEM((length, inner), F32),
        pltpu.VMEM((steps * 8, inner), F32),
        pltpu.VMEM((length, SUB), F32),
        pltpu.VMEM((width // tile, tile, total), BF),
        pltpu.SemaphoreType.DMA((width // tile,)),
    ]
    if with_grads:
        other = lambda i: sub(i) - steps
        args += [cot, g2, low_t, cot, g2, low_t, *stats, chosen]
        in_specs += [row(width), row(inner), lanes(rank)]
        in_specs += [
            pl.BlockSpec((SUB, width), lambda i, me: (other(i), 0)),
            pl.BlockSpec((SUB, inner), lambda i, me: (other(i), 0)),
            pl.BlockSpec((rank, SUB), lambda i, me: (0, other(i))),
            *[pl.BlockSpec((stats[0].shape[0], SUB), lambda i, me: (0, other(i)))] * 4,
            one(chosen),
        ]
        out_specs.append(kept(rank, inner + width + SUB))
        out_shape.append(jax.ShapeDtypeStruct((rank, inner + width + SUB), BF))
        scratch = [pltpu.VMEM((rank, inner + width), F32), *scratch]
    return pl.pallas_call(
        functools.partial(backward_half, with_grads=with_grads),
        grid_spec=pltpu.PrefetchScalarGridSpec(
            num_scalar_prefetch=1,
            grid=(steps + width // tile,),
            in_specs=in_specs,
            out_specs=out_specs,
            scratch_shapes=scratch,
        ),
        out_shape=out_shape,
        compiler_params=params(),
        cost_estimate=takes(19),
        name="backward_half",
    )(me, *args)


def place(me_ref, pieces, out):
    own, behind, ahead, far_low, far_high = pieces
    share = own.shape[1]
    y, turn = me_ref[0], (me_ref[1] + 4 - pl.program_id(0)) % 4
    for d, part in ((0, own), (1, behind), (3, ahead)):
        out[pl.ds(pl.multiple_of(((y + 4 - d) % 4) * share, share), share), :] = part[0]
    far = pl.ds(pl.multiple_of(((y + 2) % 4) * share, share), share)

    @pl.when(turn < 2)
    def _():
        out[far, :] = far_low[0]

    @pl.when(turn >= 2)
    def _():
        out[far, :] = far_high[0]


def columns_of(stats_refs, cols):
    total = summed(stats_refs)
    rows, length = total.shape
    total = jnp.concatenate([total, jnp.zeros((SUB - rows, length), F32)], 0)
    for k in range(length // SUB):
        cols[k * SUB : (k + 1) * SUB, :] = total[:, k * SUB : (k + 1) * SUB].T
    return total


def finish_branch(me_ref, sum_ref, s0, s1, s2, s3, up_ref, o0, o1, o2, o3, cols):
    columns_of((s0, s1, s2, s3), cols)
    share = o0.shape[0]
    rank = up_ref.shape[0]
    for d, out in enumerate((o0, o1, o2, o3)):
        c = (me_ref[1] + d) % 4
        mine = cols[pl.ds(pl.multiple_of((c * 4 + me_ref[0]) * share, share), share), :]
        rn = lax.rsqrt(mine[:, 0:1] / INNER_CHANNELS + EPS_NORM)
        low = (mine[:, 8 : 8 + rank] * rn).astype(BF)
        total = sum_ref[pl.ds(pl.multiple_of(c * share, share), share), :].astype(F32)
        out[...] = (total * rn + dot_nn(low, up_ref[...])).astype(BF)


def run_to_context(kernel, me, args, share, width, scratch, name):
    return pl.pallas_call(
        kernel,
        grid_spec=pltpu.PrefetchScalarGridSpec(
            num_scalar_prefetch=1,
            grid=(1,),
            in_specs=[one(a) for a in args],
            out_specs=[kept(share, width)] * 4,
            scratch_shapes=[scratch],
        ),
        out_shape=[jax.ShapeDtypeStruct((share, width), BF)] * 4,
        compiler_params=params(),
        cost_estimate=takes(3),
        name=name,
    )(me, *args)


def in_grads(me_ref, adapters_ref, *refs):
    early, late, (up0_ref, up1_ref, normed_ref), outs, (sent_ref, held) = (
        refs[:4], refs[4:8], refs[8:11], refs[11:15], refs[15:]
    )
    half = held.shape[0] // 2
    rank, length = up0_ref.shape[0], normed_ref.shape[0]
    added = lambda refs, *at: sum(r[at].astype(F32) for r in refs[1:]) + refs[0][at].astype(F32)
    for at, parts in ((0, early), (half, late)):
        held[at : at + half, :] = added(parts, slice(0, half)).astype(BF)
    share = outs[0].shape[0]
    for d, out in enumerate(outs):
        c = (me_ref[1] + d) % 4
        out[...] = held[pl.ds(pl.multiple_of(c * share, share), share), :]
    ranks = [added(parts, slice(half, half + rank), slice(0, length // 2)) for parts in (early, late)]
    width, inner2 = normed_ref.shape[1], up0_ref.shape[1]
    sent_ref[:, 0:width] = dot_nn(jnp.concatenate(ranks, 1).astype(BF), normed_ref[...]).astype(BF)
    sent_ref[:, width : width + inner2] = (up0_ref[...] + up1_ref[...]).astype(BF)
    sent_ref[:, width + inner2 :] = (lane((rank, SUB), 1) == adapters_ref[me_ref[1]]).astype(BF)


def run_in_grads(me, adapters, early, late, up0, up1, normed, share):
    rank, inner2 = up0.shape
    width = normed.shape[1]
    columns = width + inner2 + SUB
    args = (*early, *late, up0, up1, normed)
    return pl.pallas_call(
        in_grads,
        grid_spec=pltpu.PrefetchScalarGridSpec(
            num_scalar_prefetch=2,
            grid=(1,),
            in_specs=[one(a) for a in args],
            out_specs=[*[kept(share, width)] * 4, kept(rank, columns)],
            scratch_shapes=[pltpu.VMEM((4 * share, width), BF)],
        ),
        out_shape=[*[jax.ShapeDtypeStruct((share, width), BF)] * 4, jax.ShapeDtypeStruct((rank, columns), BF)],
        compiler_params=params(),
        cost_estimate=takes(3),
        name="in_grads",
    )(me, adapters, *args)


def finish_out(me_ref, p0, p1, p2, p3, p4, tokens_ref, out_ref, held):
    place(me_ref, (p0, p1, p2, p3, p4), held)
    for k in range(held.shape[0] // 16):
        here = slice(k * 16, (k + 1) * 16)
        out_ref[0, here, :] = (tokens_ref[0, here, :].astype(F32) + held[here, :].astype(F32)).astype(BF)


def finish_grad(me_ref, p0, p1, p2, p3, p4, tokens_ref, cot_ref, gain_ref, out_ref, held):
    place(me_ref, (p0, p1, p2, p3, p4), held)
    for k in range(held.shape[0] // 16):
        here = slice(k * 16, (k + 1) * 16)
        t = tokens_ref[0, here, :].astype(F32)
        rms = lax.rsqrt(jnp.mean(t * t, -1, keepdims=True) + EPS_NORM)
        pulled = held[here, :].astype(F32) * gain_ref[...]
        slope = rms * rms * rms * jnp.mean(pulled * t, -1, keepdims=True)
        out_ref[0, here, :] = rms * pulled - t * slope + cot_ref[0, here, :].astype(F32)


def piece_specs(pieces):
    share, width = pieces[0].shape[1:]
    half = pieces[0].shape[0] // 2
    turn = lambda s, me: (me[1] + 4 - s) % 4
    full = pl.BlockSpec((1, share, width), lambda s, me: (turn(s, me), 0, 0))
    return [
        full, full, full,
        pl.BlockSpec((1, share, width), lambda s, me: (jnp.minimum(turn(s, me), half - 1), 0, 0)),
        pl.BlockSpec((1, share, width), lambda s, me: (jnp.maximum(turn(s, me) - half, 0), 0, 0)),
    ]


def run_finish(kernel, me, pieces, extra, dtype, name):
    seqs, block, width = extra[0].shape
    seq = pl.BlockSpec((1, block, width), lambda s, me: (s, 0, 0))
    specs = [seq if a.ndim == 3 else whole(a) for a in extra]
    return pl.pallas_call(
        kernel,
        grid_spec=pltpu.PrefetchScalarGridSpec(
            num_scalar_prefetch=1,
            grid=(seqs,),
            in_specs=[*piece_specs(pieces), *specs],
            out_specs=seq,
            scratch_shapes=[pltpu.VMEM((block, width), BF)],
        ),
        out_shape=jax.ShapeDtypeStruct((seqs, block, width), dtype),
        compiler_params=params(30),
        cost_estimate=takes(5),
        name=name,
    )(me, *[pltpu.with_memory_space_constraint(a, pltpu.HBM) if a.ndim == 3 else a for a in (*pieces, *extra)])


def fill_tables(all_ref, *outs):
    table, rank = outs[0].shape[0], outs[0].shape[1]
    rows, columns = all_ref.shape
    spread = (lane((SUB, table * rank), 0) == lane((SUB, table * rank), 1) // rank).astype(BF)
    place = dot_nn(all_ref[:, columns - SUB :], spread)
    same = lane((rows, table * rank), 0) % rank == lane((rows, table * rank), 1) % rank
    place = jnp.where(same, place, 0.0).T.astype(BF)
    at = 0
    for out in outs:
        slots = out.shape[2:-1] or (1,)
        for slot in range(slots[0]):
            here = dot_nn(place, all_ref[:, at : at + out.shape[-1]])
            for a in range(table):
                if out.ndim == 3:
                    out[a] = here[a * rank : (a + 1) * rank, :]
                else:
                    out[a, :, slot, :] = here[a * rank : (a + 1) * rank, :]
            at += out.shape[-1]


def run_tables(everything, table, rank, widths):
    return pl.pallas_call(
        fill_tables,
        out_shape=[jax.ShapeDtypeStruct((table, rank, *w), F32) for w in widths],
        compiler_params=params(),
        cost_estimate=takes(3),
        name="fill_tables",
    )(everything)


def shifted_by(value, axis, distance):
    size = lax.axis_size(axis)
    return lax.ppermute(value, axis, [(i, (i + distance) % size) for i in range(size)])


def tie(*values):
    return lax.optimization_barrier(values)


def ring_near(own, axis):
    return shifted_by(own, axis, 1), shifted_by(own, axis, -1)


def ring_far(near, axis):
    half = near[0].shape[0] // 2
    return shifted_by(near[0][:half], axis, 1), shifted_by(near[1][half:], axis, -1)


def delivered(pieces, axis):
    return [pieces[0]] + [shifted_by(p, axis, d) for d, p in enumerate(pieces) if d]


def added(parts):
    return sum(p.astype(F32) for p in parts[1:]) + parts[0].astype(F32)


def shared(value, axis):
    return [value] + [shifted_by(value, axis, d) for d in range(1, lax.axis_size(axis))]


def swapped(value, axis):
    return lax.all_to_all(value, axis, 0, 0, tiled=True)


def per_device(
    tokens, output_cotangent, segments, sequence_adapter, input_norm_gain,
    gate_x_projection_weight, bc_projection_weight, step_projection_weight,
    x_convolution_taps, x_convolution_bias, bc_convolution_taps, bc_convolution_bias,
    step_size_bias, log_decay_rate, head_skip_gain, gated_norm_gain, output_projection_weight,
    in_adapter_down, in_adapter_up, out_adapter_down, out_adapter_up,
):
    seqs, block, width = tokens.shape
    inner = gate_x_projection_weight.shape[2]
    heads = step_projection_weight.shape[1]
    rank = in_adapter_down.shape[2]
    ny, nz = lax.axis_size("tensor"), lax.axis_size("context")
    my, mz = lax.axis_index("tensor"), lax.axis_index("context")
    me = jnp.stack([my, mz]).astype(jnp.int32)
    length = block * nz
    share = block // ny

    rows = gate_x_projection_weight.shape[0]
    packed = jnp.concatenate(
        [
            gate_x_projection_weight.reshape(rows, 2 * inner),
            bc_projection_weight,
            step_projection_weight,
            jnp.zeros((rows, SUB - heads), BF),
            output_projection_weight.T,
        ],
        1,
    )
    full = lax.all_gather(packed, ("fsdp", "context"), axis=0, tiled=True)

    quarters = lambda a: [
        lax.dynamic_slice(a, ((mz + d) % nz, my * share, 0), (1, share, width)) for d in range(nz)
    ]
    tokens_s, cot_later, segments = tie(delivered(quarters(tokens), "context"), output_cotangent, segments)
    tokens_near = ring_near(jnp.concatenate(tokens_s, 0), "tensor")
    tokens_s = jnp.concatenate(tokens_s, 0)
    to_lanes = lambda a: jnp.pad(a, (0, SUB - heads))
    vec = jnp.concatenate(
        [
            x_convolution_bias, bc_convolution_bias, gated_norm_gain, input_norm_gain,
            to_lanes(step_size_bias), to_lanes(log_decay_rate), to_lanes(head_skip_gain),
        ]
    )[None]
    marks, taps, conv_bias, par, skip, gain, norm_gain, down_in, up_in, down_out, up_out = run_prepare(
        me, sequence_adapter, swapped(segments, "context").reshape(nz, block), vec, x_convolution_taps, bc_convolution_taps,
        in_adapter_down.transpose(0, 2, 1), in_adapter_up, out_adapter_down.transpose(0, 2, 1), out_adapter_up, width,
    )
    chosen = jnp.full((1, SUB), lax.dynamic_index_in_dim(sequence_adapter, mz, 0, False).astype(F32))
    pick = (jnp.arange(inner)[:, None] // (inner // heads) == jnp.arange(SUB)[None, :]).astype(BF)
    lam, edge = jnp.zeros((SUB, inner), F32), jnp.zeros((8, taps.shape[1]), F32)

    tokens_near, marks, cot_s = tie(tokens_near, marks, delivered(quarters(cot_later), "context"))
    normed, low_rank = run_rows(near_rows, me, (tokens_s, *tokens_near), down_in, norm_gain, (), "near_rows")
    tokens_far, cot_s, normed = tie(ring_far(tokens_near, "tensor"), jnp.concatenate(cot_s, 0), normed)
    cot_parts = shared(cot_s, "tensor")
    normed, low_rank = run_rows(far_rows, me, tokens_far, down_in, norm_gain, (normed, low_rank), "far_rows")
    gx, rank_t, part, dt, run, run_turned, y, xc, bc, slope, g2, states, out_all = run_forward(
        normed, low_rank, up_in, full, down_out, marks, taps, conv_bias, par, skip, gain
    )
    g2, cot_parts = tie(g2, cot_parts)
    dn, stats, cot, d_low_t = run_pull_back(me, cot_parts, full, up_out, g2, part, down_out)
    out_all, stats = tie(out_all, stats)
    out_sum = lax.psum_scatter(out_all.reshape(length, width), "tensor", scatter_dimension=0, tiled=True)
    stats_all = shared(stats, "tensor")

    backward = lambda half, *carried, **more: run_backward(
        me, half, gx, dt, run, run_turned, xc, bc, slope, y, dn, states, stats_all, marks, taps, par, skip, gain, pick,
        full, down_in, up_in, rank_t, *carried, **more,
    )
    *late, lam, edge, late_up, sent = backward(1, lam, edge, cot=cot, g2=g2, low_t=d_low_t, chosen=chosen)
    sent_out = lax.all_gather(sent, ("fsdp", "context"), axis=0, tiled=True)
    lam, late = tie(lam, late)
    late_parts = delivered(late, "tensor")
    *early, _, _, early_up = backward(0, lam, edge)
    early, late_parts, out_sum = tie(early, late_parts, out_sum)
    early_parts = delivered(early, "tensor")
    scratch = pltpu.VMEM((length, SUB), F32)
    branch = run_to_context(finish_branch, me, (out_sum, *stats_all, up_out), share, width, scratch, "finish_branch")
    branch_parts = delivered(branch, "context")
    early_parts, branch_parts = tie(early_parts, branch_parts)
    branch_q = jnp.stack(branch_parts)
    out_near = ring_near(branch_q, "tensor")
    *d_in, sent = run_in_grads(
        me, sequence_adapter, early_parts, late_parts, early_up, late_up, normed, share
    )
    sent_all = lax.all_gather(sent, ("fsdp", "context"), axis=0, tiled=True)
    d_in_parts = delivered(d_in, "context")
    d_in_parts, out_near, sent = tie(d_in_parts, out_near, sent)
    d_in_q = jnp.stack(d_in_parts)
    d_in_near = ring_near(d_in_q, "tensor")
    out_far = ring_far(out_near, "tensor")
    table = in_adapter_down.shape[0]
    out_tables = run_tables(sent_out, table, rank, ((inner,), (width,)))
    d_in_near, out_far, out_tables = tie(d_in_near, out_far, out_tables)
    d_in_far = ring_far(d_in_near, "tensor")
    layer_out = run_finish(finish_out, me, (branch_q, *out_near, *out_far), (tokens,), BF, "finish_out")
    layer_out, d_in_far = tie(layer_out, d_in_far)
    grad_tokens = run_finish(
        finish_grad, me, (d_in_q, *d_in_near, *d_in_far), (tokens, output_cotangent, norm_gain), F32, "finish_grad"
    )
    in_tables = run_tables(sent_all, table, rank, ((width,), (2, inner)))
    return (
        layer_out,
        grad_tokens,
        in_tables[0].transpose(0, 2, 1),
        in_tables[1],
        out_tables[0].transpose(0, 2, 1),
        out_tables[1],
    )


def solution(mesh):
    placed = (
        P("fsdp", "context", None),
        P("fsdp", "context", None),
        P("fsdp", "context"),
        P("fsdp"),
        P(),
        P(("fsdp", "context"), None, "tensor"),
        P(("fsdp", "context"), None),
        P(("fsdp", "context"), "tensor"),
        P(None, "tensor"),
        P("tensor"),
        P(),
        P(),
        P("tensor"),
        P("tensor"),
        P("tensor"),
        P("tensor"),
        P("tensor", ("fsdp", "context")),
        P(),
        P(None, None, None, "tensor"),
        P(None, "tensor", None),
        P(),
    )
    return jax.shard_map(
        per_device,
        mesh=mesh,
        in_specs=placed,
        out_specs=(
            P("fsdp", "context", None),
            P("fsdp", "context", None),
            P(),
            P(None, None, None, "tensor"),
            P(None, "tensor", None),
            P(),
        ),
        check_vma=False,
    )
```

```python
import functools

import jax
import jax.numpy as jnp
from jax import lax
from jax.experimental import pallas as pl
from jax.experimental.pallas import tpu as pltpu
from jax.sharding import PartitionSpec as P

INNER_CHANNELS = 3072
EPS_NORM = 1e-05
SUB = 128
NEG = -1e30
BF = jnp.bfloat16
F32 = jnp.float32
HIGHEST = lax.Precision.HIGHEST


def dot_nn(a, b):
    return lax.dot_general(a, b, (((1,), (0,)), ((), ())), preferred_element_type=F32)


def dot_nt(a, b):
    return lax.dot_general(a, b, (((1,), (1,)), ((), ())), preferred_element_type=F32)


def dot_tn(a, b):
    return lax.dot_general(a, b, (((0,), (0,)), ((), ())), preferred_element_type=F32)


def softplus(v):
    return jnp.maximum(v, 0.0) + jnp.log1p(jnp.exp(-jnp.abs(v)))


def lane(shape, dim):
    return lax.broadcasted_iota(jnp.int32, shape, dim)


def wide(column):
    return jnp.broadcast_to(column, (SUB, SUB))


def decays(raw, par_ref):
    dt = softplus(raw + par_ref[0:1, :])
    lower = (lane((SUB, SUB), 0) >= lane((SUB, SUB), 1)).astype(F32)
    run = jnp.dot(lower, dt * par_ref[1:2, :], precision=HIGHEST, preferred_element_type=F32)
    return dt, run


def scan_forward(
    k, gx, dt_ref, run_ref, rows_ref, marks_ref, taps_ref, bias_ref, skip_ref, gain_ref, down_ref,
    y_ref, xc_ref, bc_ref, slope_ref, g2_ref, states_ref, stats_ref, state, ext,
):
    inner = skip_ref.shape[1]
    chans = ext.shape[1]
    rows = pl.ds(pl.multiple_of(k * SUB, SUB), SUB)

    def strip(ref, at):
        each = ref.shape[2] // SUB
        return ref[at // each, rows, (at % each) * SUB : (at % each + 1) * SUB].astype(F32)

    @pl.when(k == 0)
    def _():
        state[...] = jnp.zeros_like(state)
        ext[0:8, :] = jnp.zeros((8, chans), F32)

    @pl.when(k > 0)
    def _():
        ext[0:8, :] = ext[SUB : SUB + 8, :]

    for c in range(chans // SUB):
        ext[8 : SUB + 8, c * SUB : (c + 1) * SUB] = strip(gx, inner // SUB + c)
    near = [wide(marks_ref[:, k : k + 1]) for k in range(3)]
    linked = wide(marks_ref[:, 3:4])
    ending = wide(marks_ref[:, 4:5])
    ids = wide(marks_ref[:, 5:6])
    passing = marks_ref[0:1, 6:7]
    left = lane((SUB, SUB), 1) < 64

    def conv(sl):
        pre = bias_ref[:, sl] + taps_ref[3:4, sl] * ext[8 : SUB + 8, sl]
        for k in range(1, 4):
            pre = pre + taps_ref[3 - k : 4 - k, sl] * (ext[8 - k : SUB + 8 - k, sl] * near[k - 1])
        sig = jax.nn.sigmoid(pre)
        out = (pre * sig).astype(BF)
        slope_ref[:, sl] = (sig * (1.0 + pre * (1.0 - sig))).astype(BF)
        return out

    b_low = conv(slice(inner, inner + SUB))
    c_low = conv(slice(inner + SUB, inner + 2 * SUB))
    bc_ref[:, 0:SUB] = b_low
    bc_ref[:, SUB : 2 * SUB] = c_low
    b_turned = b_low.astype(F32).T.astype(BF)
    dt, run = dt_ref[rows, :], run_ref[rows, :]
    run_rows = rows_ref[pl.ds(pl.multiple_of(k * 16, 16), 16), :]
    allowed = (ids == ids.T) & (lane((SUB, SUB), 0) >= lane((SUB, SUB), 1))
    mask = jnp.where(allowed, 0.0, NEG)
    cross = dot_nt(c_low, b_low)
    square = jnp.zeros((SUB, SUB), F32)
    for p in range(inner // SUB):
        sl = slice(p * SUB, (p + 1) * SUB)
        x_low = conv(sl)
        xc_ref[:, sl] = x_low
        x = x_low.astype(F32)
        run0, run1 = wide(run[:, 2 * p : 2 * p + 1]), wide(run[:, 2 * p + 1 : 2 * p + 2])
        run_p = jnp.where(left, run0, run1)
        dt_p = jnp.where(left, wide(dt[:, 2 * p : 2 * p + 1]), wide(dt[:, 2 * p + 1 : 2 * p + 2]))
        m0 = (jnp.exp(run0 - run_rows[2 * p : 2 * p + 1, :] + mask) * cross).astype(BF)
        m1 = (jnp.exp(run1 - run_rows[2 * p + 1 : 2 * p + 2, :] + mask) * cross).astype(BF)
        xdt = x * dt_p
        split = jnp.concatenate([jnp.where(left, xdt, 0.0), jnp.where(left, 0.0, xdt)], 0).astype(BF)
        before = state[:, sl]
        before_low = before.astype(BF)
        states_ref[0, :, sl] = before_low
        y = dot_nn(jnp.concatenate([m0, m1], 1), split)
        y = y + jnp.exp(run_p) * linked * dot_nn(c_low, before_low) + skip_ref[:, sl] * x
        last = run_p[SUB - 1 : SUB, :]
        toward = (xdt * (jnp.exp(last - run_p) * ending)).astype(BF)
        state[:, sl] = (jnp.exp(last) * passing) * before + dot_nn(b_turned, toward)
        z = strip(gx, p)
        gated = y * (z * jax.nn.sigmoid(z))
        y_ref[:, sl] = y.astype(BF)
        g2_ref[:, sl] = (gated * gain_ref[:, sl]).astype(BF)
        square = square + gated * gated
    stats_ref[0:8, rows] = lane_rows(square)
    stats_ref[8:, rows] = dot_nt(down_ref[...], g2_ref[...])


def forward_all(
    normed, rank, up_ref, w_ref, w0_ref, w1_ref, out_down_ref, marks_ref, taps_ref, bias_ref, par_ref, skip_ref, gain_ref,
    gx_hbm, rank_t_ref, stats_ref, dt_ref, run_ref, rows_ref, y_ref, xc_ref, bc_ref, slope_ref, g2_ref, states_ref, out_ref,
    gx, state, ext, g2_all, held, sems,
):
    step = pl.program_id(0)
    tiles, length, tile = gx.shape

    def copy_gx(j):
        return pltpu.make_async_copy(gx.at[j], gx_hbm.at[:, pl.ds(j * tile, tile)], sems.at[j])

    @pl.when(step == 0)
    def _():
        turn_rank(rank[...].astype(F32), rank_t_ref)

    for j in range(tiles):

        @pl.when(step == j)
        def _():
            gx[j] = (dot_nn(normed[...], w_ref[...]) + dot_nn(rank[...], up_ref[...])).astype(BF)
            copy_gx(j).start()

    @pl.when(step == tiles - 1)
    def _():
        inner, chans = skip_ref.shape[1], taps_ref.shape[1]
        at, col = divmod(2 * inner + chans - inner, tile)
        for i in range(length // SUB):
            here = slice(i * SUB, (i + 1) * SUB)
            dt, run = decays(gx[at, here, col : col + SUB].astype(F32), par_ref)
            dt_ref[here, :] = dt
            run_ref[here, :] = run
            rows_ref[i * 16 : (i + 1) * 16, :] = run.T[0:16, :]

    done = tiles + length // SUB

    @pl.when((step >= tiles) & (step < done))
    def _():
        scan_forward(
            step - tiles, gx, dt_ref, run_ref, rows_ref, marks_ref, taps_ref, bias_ref, skip_ref, gain_ref, out_down_ref,
            y_ref, xc_ref, bc_ref, slope_ref, g2_ref, states_ref, stats_ref, state, ext,
        )
        g2_all[pl.ds(pl.multiple_of((step - tiles) * SUB, SUB), SUB), :] = g2_ref[...]

    @pl.when(step >= done)
    def _():
        cut = w0_ref.shape[1]
        held[...] = (dot_nt(g2_all[:, 0:cut], w0_ref[...]) + dot_nt(g2_all[:, cut:], w1_ref[...])).astype(BF)
        owners, rows, _ = out_ref.shape
        share = 64
        for c in range(rows // share):
            for y in range(owners):
                at = (c * owners + y) * share
                out_ref[y, c * share : (c + 1) * share, :] = held[at : at + share, :]

    @pl.when(step == pl.num_programs(0) - 1)
    def _():
        for j in range(tiles):
            copy_gx(j).wait()


def backward_half(
    me_ref, z_ref, raw_ref, dt_ref, run_ref, rows_ref, xc_ref, bc_ref, slope_ref, y_ref, dn_ref, states_ref, s0_ref, s1_ref, s2_ref, s3_ref, marks_ref,
    taps_ref, par_ref, skip_ref, gain_ref, pick_ref, lam_in_ref, edge_in_ref,
    w_hbm, down_ref, up_ref, rank_t_ref, *rest, with_grads,
):
    if with_grads:
        (cot0_ref, g20_ref, low0_ref, cot1_ref, g21_ref, low1_ref, q0_ref, q1_ref, q2_ref, q3_ref, chosen_ref), rest = rest[:11], rest[11:]
        o0, o1, o2, o3, lam, edge_ref, up_grad_ref, grads_ref, *scratch = rest
        grads, *scratch = scratch
    else:
        o0, o1, o2, o3, lam, edge_ref, up_grad_ref, *scratch = rest
    d_all, low, pushed, held, ext, to_dt, to_run, to_end, shifted, w_all, sems = scratch
    step = pl.program_id(0)
    steps = d_all.shape[0] // SUB
    tiles, tile, columns = w_all.shape

    def copy_w(j):
        return pltpu.make_async_copy(w_hbm.at[pl.ds(j * tile, tile), pl.ds(0, columns)], w_all.at[j], sems.at[j])

    @pl.when(step == 0)
    def _():
        for j in range(tiles):
            copy_w(j).start()

    if with_grads:

        @pl.when(step == 0)
        def _():
            grads[...] = jnp.zeros_like(grads)

        @pl.when(step < steps)
        def _():
            cut = g20_ref.shape[1]
            for stats, low_t_ref, cot_ref, g2_ref in (
                (summed((s0_ref, s1_ref, s2_ref, s3_ref)), low0_ref, cot0_ref, g20_ref),
                (summed((q0_ref, q1_ref, q2_ref, q3_ref)), low1_ref, cot1_ref, g21_ref),
            ):
                rn_row = lax.rsqrt(stats[0:1, :] / INNER_CHANNELS + EPS_NORM)
                grads[:, 0:cut] += dot_nn((low_t_ref[...].astype(F32) * rn_row).astype(BF), g2_ref[...])
                grads[:, cut:] += dot_nn((stats[8:, :] * rn_row).astype(BF), cot_ref[...])

        @pl.when(step == steps)
        def _():
            grads_ref[:, 0 : grads.shape[1]] = grads[...].astype(BF)
            mine = lane((grads.shape[0], SUB), 1).astype(F32) == chosen_ref[...]
            grads_ref[:, grads.shape[1] :] = jnp.where(mine, 1.0, 0.0).astype(BF)

    @pl.when(step < steps)
    def _():
        at = pl.multiple_of((steps - 1 - step) * SUB, SUB)
        scan_backward(
            step, at, d_all.at[pl.ds(at, SUB), :], z_ref, dt_ref, run_ref, rows_ref, xc_ref, bc_ref, slope_ref, y_ref, dn_ref, states_ref,
            (s0_ref, s1_ref, s2_ref, s3_ref), marks_ref, taps_ref, par_ref, skip_ref, gain_ref, pick_ref, lam_in_ref, edge_in_ref,
            lam, ext, to_dt, to_run, to_end,
        )
        gate = d_all[pl.ds(at, SUB), 0 : up_ref.shape[1]]
        part = dot_nt(gate, up_ref[...])
        rank = part.shape[1]
        low[pl.ds(at, SUB), :] = part.astype(BF)
        part = jnp.concatenate([part, jnp.zeros((SUB, SUB - rank), F32)], 1)
        pushed[:, pl.ds(at, SUB)] = part.T[0:rank, :].astype(BF)
        up_grad = dot_nn(rank_t_ref[...], gate)

        @pl.when(step == 0)
        def _():
            up_grad_ref[...] = up_grad

        @pl.when(step > 0)
        def _():
            up_grad_ref[...] += up_grad

        shifted[pl.ds(at, SUB), :] = raw_ref[...].astype(F32) + par_ref[0:1, :]

    @pl.when(step == steps - 1)
    def _():
        edge_ref[...] = ext[0:8, :]

    @pl.when(step == steps)
    def _():
        def by_head(v):
            high = v.astype(BF)
            return dot_nn(high, pick_ref[...]) + dot_nn((v - high.astype(F32)).astype(BF), pick_ref[...])

        d_run, d_dt, d_end = by_head(to_run[...]), by_head(to_dt[...]), by_head(to_end[...])
        upper = (lane((SUB, SUB), 0) <= lane((SUB, SUB), 1)).astype(F32)
        for i in range(steps):
            here = slice(i * SUB, (i + 1) * SUB)
            block = d_run[here] + jnp.where(lane((SUB, SUB), 0) == SUB - 1, d_end[i * 8 : i * 8 + 1], 0.0)
            d_log = jnp.dot(upper, block, precision=HIGHEST, preferred_element_type=F32)
            d_raw = (d_dt[here] + par_ref[1:2, :] * d_log) * jax.nn.sigmoid(shifted[here, :])
            d_all[here, d_all.shape[1] - SUB :] = d_raw.astype(BF)

    for j in range(tiles):

        @pl.when(step == steps + j)
        def _():
            copy_w(j).wait()

    @pl.when(step >= steps)
    def _():
        held[...] = (dot_nt(d_all[...], w_all[step - steps]) + dot_nn(low[...], down_ref[...])).astype(BF)
        deal(me_ref[0], held, (o0, o1, o2, o3))

    for out in (o0, o1, o2, o3):

        @pl.when(step == steps)
        def _():
            out[out.shape[0] - pushed.shape[0] :, :] = pushed[...]

        @pl.when(step > steps)
        def _():
            out[out.shape[0] - pushed.shape[0] :, :] = jnp.zeros_like(pushed)


def scan_backward(
    step, at, da_ref, z_ref, dt_ref, run_ref, rows_ref, xc_ref, bc_ref, slope_ref, y_ref, dn_ref, states_ref, stats_refs, marks_ref,
    taps_ref, par_ref, skip_ref, gain_ref, pick_ref, lam_in_ref, edge_in_ref,
    lam, ext, to_dt, to_run, to_end,
):
    inner = z_ref.shape[1]
    chans = ext.shape[1]

    @pl.when(step == 0)
    def _():
        lam[...] = lam_in_ref[...]
        ext[SUB : SUB + 8, :] = edge_in_ref[...]

    @pl.when(step > 0)
    def _():
        ext[SUB : SUB + 8, :] = ext[0:8, :]

    linked = wide(marks_ref[:, 3:4])
    ending = wide(marks_ref[:, 4:5])
    ids = wide(marks_ref[:, 5:6])
    passing = marks_ref[0:1, 6:7]
    later = [wide(marks_ref[:, 7 + k : 8 + k]) for k in range(3)]
    left = lane((SUB, SUB), 1) < 64
    stats = summed(stats_refs)
    rn_row = lax.rsqrt(stats[0:1, :] / INNER_CHANNELS + EPS_NORM)
    rn = jnp.broadcast_to(rn_row, (SUB, SUB)).T
    kappa = jnp.broadcast_to(rn_row * rn_row * rn_row * stats[1:2, :] / INNER_CHANNELS, (SUB, SUB)).T
    dt, run, run_rows = dt_ref[...], run_ref[...], rows_ref[...]
    tokens = pl.ds(at, SUB)
    b_low, c_low = bc_ref[:, 0:SUB], bc_ref[:, SUB : 2 * SUB]
    c_turned = c_low.astype(F32).T.astype(BF)
    allowed = (ids == ids.T) & (lane((SUB, SUB), 0) <= lane((SUB, SUB), 1))
    mask = jnp.where(allowed, 0.0, NEG)
    cross = dot_nt(b_low, c_low)
    d_cross = jnp.zeros((SUB, SUB), F32)
    d_b = jnp.zeros((SUB, SUB), F32)
    d_c = jnp.zeros((SUB, SUB), F32)
    for p in range(inner // SUB):
        sl = slice(p * SUB, (p + 1) * SUB)
        z = z_ref[:, sl].astype(F32)
        sig = jax.nn.sigmoid(z)
        silu = z * sig
        y = y_ref[:, sl].astype(F32)
        d_gated = rn * (dn_ref[:, sl].astype(F32) * gain_ref[:, sl]) - kappa * (y * silu)
        da_ref[:, sl] = (d_gated * y * sig * (1.0 + z * (1.0 - sig))).astype(BF)
        dy = d_gated * silu
        x = xc_ref[:, sl].astype(F32)
        run0, run1 = wide(run[:, 2 * p : 2 * p + 1]), wide(run[:, 2 * p + 1 : 2 * p + 2])
        run_p = jnp.where(left, run0, run1)
        dt_p = jnp.where(left, wide(dt[:, 2 * p : 2 * p + 1]), wide(dt[:, 2 * p + 1 : 2 * p + 2]))
        l0 = jnp.exp(run_rows[2 * p : 2 * p + 1, :] - run0 + mask)
        l1 = jnp.exp(run_rows[2 * p + 1 : 2 * p + 2, :] - run1 + mask)
        xdt = x * dt_p
        x_split = jnp.concatenate([jnp.where(left, xdt, 0.0), jnp.where(left, 0.0, xdt)], 0).astype(BF)
        dy_split = jnp.concatenate([jnp.where(left, dy, 0.0), jnp.where(left, 0.0, dy)], 0).astype(BF)
        d_m = dot_nt(x_split, dy.astype(BF))
        d_cross = d_cross + l0 * d_m[0:SUB] + l1 * d_m[SUB : 2 * SUB]
        m = jnp.concatenate([l0 * cross, l1 * cross], 1).astype(BF)
        lam_p = lam[:, sl]
        lam_low = lam_p.astype(BF)
        last = run_p[SUB - 1 : SUB, :]
        toward = jnp.exp(last - run_p) * ending
        carried = toward * dot_nn(b_low, lam_low)
        d_xt = dot_nn(m, dy_split) + carried
        skip = skip_ref[:, sl]
        ext[0:SUB, sl] = (dt_p * d_xt + skip * dy) * slope_ref[:, sl].astype(F32)
        x_dx = x * d_xt
        to_dt[tokens, sl] = x_dx
        to_run[tokens, sl] = dy * (y - skip * x) - dt_p * x_dx
        reached = (jnp.exp(run_p) * linked * dy).astype(BF)
        before_low = states_ref[0, :, sl]
        keep = jnp.exp(last) * passing
        end = jnp.sum(xdt * carried, 0, keepdims=True) + keep * jnp.sum(
            lam_p * before_low.astype(F32), 0, keepdims=True
        )
        to_end[pl.ds(pl.multiple_of(at // 16, 8), 8), sl] = jnp.broadcast_to(end, (8, SUB))
        d_b = d_b + dot_nt((xdt * toward).astype(BF), lam_low)
        d_c = d_c + dot_nt(reached, before_low)
        lam[:, sl] = keep * lam_p + dot_nn(c_turned, reached)
    d_cross_low = d_cross.astype(BF)
    d_b = d_b + dot_nn(d_cross_low, c_low)
    d_c = d_c + dot_nn(d_cross.T.astype(BF), b_low)
    ext[0:SUB, inner : inner + SUB] = d_b * slope_ref[:, inner : inner + SUB].astype(F32)
    ext[0:SUB, inner + SUB : chans] = d_c * slope_ref[:, inner + SUB : chans].astype(F32)

    for s in range(chans // SUB):
        sl = slice(s * SUB, (s + 1) * SUB)
        acc = taps_ref[3:4, sl] * ext[0:SUB, sl]
        for k in range(1, 4):
            acc = acc + taps_ref[3 - k : 4 - k, sl] * (ext[k : SUB + k, sl] * later[k - 1])
        da_ref[:, inner + s * SUB : inner + (s + 1) * SUB] = acc.astype(BF)

def whole(a):
    return pl.BlockSpec(a.shape, lambda i, *_: (0,) * a.ndim)


def params(mib=60):
    return pltpu.CompilerParams(vmem_limit_bytes=mib << 20)


def takes(us):
    return pl.CostEstimate(flops=us * 100_000_000, bytes_accessed=us * 300_000, transcendentals=0)


def turn_rank(low, rank_t_ref):
    rank = low.shape[1]
    low = jnp.concatenate([low, jnp.zeros((low.shape[0], SUB - rank), F32)], 1)
    for k in range(low.shape[0] // SUB):
        here = slice(k * SUB, (k + 1) * SUB)
        rank_t_ref[:, here] = low[here, :].T[0:rank, :].astype(BF)


def low_products(rows_ref, down_ref, rank_ref, rank_t_ref):
    low = dot_nt(rows_ref[...], down_ref[...])
    rank_ref[...] = low.astype(BF)
    turn_rank(low, rank_t_ref)


def summed(refs):
    return refs[0][...].astype(F32) + refs[1][...].astype(F32) + refs[2][...].astype(F32) + refs[3][...].astype(F32)


def lane_rows(v):
    return lax.dot_general(
        jnp.ones((8, v.shape[1]), F32), v, (((1,), (1,)), ((), ())), precision=HIGHEST, preferred_element_type=F32
    )


def deal(me, held, outs):
    share = 64
    for c in range(held.shape[0] // (4 * share)):
        for d, out in enumerate(outs):
            at = pl.multiple_of((c * 4 + (me + d) % 4) * share, share)
            out[c * share : (c + 1) * share, :] = held[pl.ds(at, share), :]


def one(a):
    return pl.BlockSpec(a.shape, lambda i, *_: (0,) * a.ndim, pipeline_mode=pl.Buffered(1))


def kept(*shape):
    return pl.BlockSpec(shape, lambda i, *_: (0,) * len(shape))


def run_forward(normed, low_rank, up, weights, out_down, marks, taps, bias, par, skip, gain):
    length, width = normed.shape
    inner, chans = skip.shape[1], taps.shape[1]
    rank, columns = up.shape
    tile = 512
    tiles, steps, out_tiles = columns // tile, length // SUB, width // tile
    sub = lambda i: jnp.clip(i - tiles, 0, steps - 1)
    scan = lambda cols: pl.BlockSpec((SUB, cols), lambda i: (sub(i), 0))
    first = lambda i: jnp.minimum(i, tiles - 1)
    last = lambda i: jnp.maximum(i - tiles - steps, 0)
    at_out = 2 * (weights.shape[1] - inner) // inner
    return pl.pallas_call(
        forward_all,
        grid=(tiles + steps + out_tiles,),
        in_specs=[
            one(normed), one(low_rank),
            pl.BlockSpec((rank, tile), lambda i: (0, first(i))),
            pl.BlockSpec((width, tile), lambda i: (0, first(i))),
            pl.BlockSpec((tile, inner // 2), lambda i: (last(i), at_out)),
            pl.BlockSpec((tile, inner // 2), lambda i: (last(i), at_out + 1)),
            one(out_down), scan(marks.shape[1]), one(taps), one(bias), one(par), one(skip), one(gain),
        ],
        out_specs=[
            pl.BlockSpec(memory_space=pl.ANY), kept(rank, length), kept(8 + rank, length),
            kept(length, SUB), kept(length, SUB), kept(steps * 16, SUB),
            scan(inner), scan(inner), scan(2 * SUB), scan(chans), scan(inner),
            pl.BlockSpec((1, SUB, inner), lambda i: (sub(i), 0, 0)),
            pl.BlockSpec((4, length // 4, tile), lambda i: (0, 0, last(i))),
        ],
        scratch_shapes=[
            pltpu.VMEM((tiles, length, tile), BF),
            pltpu.VMEM((SUB, inner), F32),
            pltpu.VMEM((SUB + 8, chans), F32),
            pltpu.VMEM((length, inner), BF),
            pltpu.VMEM((length, tile), BF),
            pltpu.SemaphoreType.DMA((tiles,)),
        ],
        out_shape=[
            jax.ShapeDtypeStruct((length, columns), BF),
            jax.ShapeDtypeStruct((rank, length), BF),
            jax.ShapeDtypeStruct((8 + rank, length), F32),
            jax.ShapeDtypeStruct((length, SUB), F32),
            jax.ShapeDtypeStruct((length, SUB), F32),
            jax.ShapeDtypeStruct((steps * 16, SUB), F32),
            jax.ShapeDtypeStruct((length, inner), BF),
            jax.ShapeDtypeStruct((length, inner), BF),
            jax.ShapeDtypeStruct((length, 2 * SUB), BF),
            jax.ShapeDtypeStruct((length, chans), BF),
            jax.ShapeDtypeStruct((length, inner), BF),
            jax.ShapeDtypeStruct((steps, SUB, inner), BF),
            jax.ShapeDtypeStruct((4, length // 4, width), BF),
        ],
        compiler_params=params(),
        cost_estimate=takes(30),
        name="forward_all",
    )(normed, low_rank, up, weights, weights, weights, out_down, marks, taps, bias, par, skip, gain)


def prepare(
    me_ref, adapters_ref, seg_ref, vec_ref, x_taps_ref, bc_taps_ref, down_in_ref, up_in_ref, down_out_ref, up_out_ref,
    marks_ref, taps_ref, bias_ref, par_ref, skip_ref, gain_ref, norm_gain_ref, down_in, up_wide, down_out, up_out,
):
    chunks, block = seg_ref.shape
    each = block // SUB
    subs = chunks * each
    seg = seg_ref[...].astype(F32)
    rows = [seg[c : c + 1, h * SUB : (h + 1) * SUB] for c in range(chunks) for h in range(each)]
    own = jnp.concatenate(rows, 0)
    none = jnp.full((1, SUB), -1.0, F32)
    before = jnp.concatenate([none, *rows[:-1]], 0)
    after = jnp.concatenate([*rows[1:], none], 0)
    at = lane((subs, SUB), 1)
    last, last_before = (jnp.broadcast_to(v[:, SUB - 1 : SUB], own.shape) for v in (own, before))
    kinds = [own == jnp.where(at >= k, pltpu.roll(own, k, 1), pltpu.roll(before, k, 1)) for k in (1, 2, 3)]
    kinds += [own == last_before, own == last, None, last == last_before]
    kinds += [
        own == jnp.where(at < SUB - k, pltpu.roll(own, SUB - k, 1), pltpu.roll(after, SUB - k, 1)) for k in (1, 2, 3)
    ]
    kinds = [own if v is None else jnp.where(v, 1.0, 0.0) for v in kinds]
    count = marks_ref.shape[1]
    for i in range(subs):
        here = [v[i : i + 1, :] for v in kinds]
        full = jnp.concatenate([*here, jnp.zeros((SUB - len(here), SUB), F32)], 0)
        marks_ref[i * SUB : (i + 1) * SUB, :] = full.T[:, 0:count]
    inner = x_taps_ref.shape[1]
    chans = taps_ref.shape[1]
    taps_ref[:, 0:inner] = x_taps_ref[...]
    taps_ref[:, inner:] = bc_taps_ref[...]
    cuts = [0]
    for n in (chans, inner, norm_gain_ref.shape[1], SUB, SUB, SUB):
        cuts.append(cuts[-1] + n)
    piece = [vec_ref[:, a:b] for a, b in zip(cuts, cuts[1:])]
    bias_ref[...], gain_ref[...], norm_gain_ref[...] = piece[:3]
    par_ref[...] = jnp.concatenate([piece[3], -jnp.exp(piece[4]), jnp.zeros((6, SUB), F32)], 0)
    spread = jnp.where(lane((SUB, inner), 0) == lane((SUB, inner), 1) // 64, 1.0, 0.0)
    skip = jnp.dot(jnp.broadcast_to(piece[5], (8, SUB)), spread, precision=HIGHEST, preferred_element_type=F32)
    skip_ref[...] = skip[0:1, :]
    down_in[...], down_out[...], up_out[...] = down_in_ref[0], down_out_ref[0], up_out_ref[0]
    up_wide[...] = jnp.zeros_like(up_wide)
    for k in range(2):
        up_wide[:, k * inner : (k + 1) * inner] = up_in_ref[0, :, k, :]


def run_prepare(me, adapters, seg, vec, x_taps, bc_taps, down_in, up_in, down_out, up_out, norm_width):
    length = seg.shape[0] * seg.shape[1]
    inner, bc = x_taps.shape[1], bc_taps.shape[1]
    rank = up_in.shape[1]
    mine = lambda a: pl.BlockSpec((1, *a.shape[1:]), lambda i, me, ad: (ad[me[1]],) + (0,) * (a.ndim - 1))
    outs = [
        ((length, 16), F32), ((4, inner + bc), F32), ((1, inner + bc), F32), ((8, SUB), F32), ((1, inner), F32),
        ((1, inner), F32), ((1, norm_width), F32), (down_in.shape[1:], BF), ((rank, 2 * inner + 512), BF),
        (down_out.shape[1:], BF), (up_out.shape[1:], BF),
    ]
    return pl.pallas_call(
        prepare,
        grid_spec=pltpu.PrefetchScalarGridSpec(
            num_scalar_prefetch=2,
            grid=(1,),
            in_specs=[one(seg), one(vec), one(x_taps), one(bc_taps), mine(down_in), mine(up_in), mine(down_out), mine(up_out)],
            out_specs=[kept(*n) for n, _ in outs],
        ),
        out_shape=[jax.ShapeDtypeStruct(n, t) for n, t in outs],
        compiler_params=params(),
        cost_estimate=takes(2),
        name="prepare",
    )(me, adapters, seg, vec, x_taps, bc_taps, down_in, up_in, down_out, up_out)


def normed_rows(me_ref, blocks, down_ref, gain_ref, held, rows_hbm, rank_ref, sems):
    share = held.shape[1]
    copies = []
    for k, (c, back, rows) in enumerate(blocks):
        t = rows.astype(F32)
        rms = lax.rsqrt(jnp.mean(t * t, -1, keepdims=True) + EPS_NORM)
        held[k] = (t * rms * gain_ref[...]).astype(BF)
        at = pl.multiple_of((c * 4 + (me_ref[0] + 4 - back) % 4) * share, share)
        copies.append(pltpu.make_async_copy(held.at[k], rows_hbm.at[pl.ds(at, share), :], sems.at[k]))
        copies[-1].start()
        rank_ref[pl.ds(at, share), :] = dot_nt(held[k], down_ref[...]).astype(BF)
    for copy in copies:
        copy.wait()


def near_rows(me_ref, p0, p1, p2, down_ref, gain_ref, rows_hbm, rank_ref, held, sems):
    rank_ref[...] = jnp.zeros_like(rank_ref)
    blocks = [
        (c, back, part[(me_ref[1] + 4 - c) % 4]) for c in range(4) for back, part in ((0, p0), (1, p1), (3, p2))
    ]
    normed_rows(me_ref, blocks, down_ref, gain_ref, held, rows_hbm, rank_ref, sems)


def far_rows(me_ref, p3, p4, down_ref, gain_ref, rows_in, rank_in, rows_hbm, rank_ref, held, sems):
    rank_ref[...] = rank_in[...]
    blocks = []
    for c in range(4):
        turn = (me_ref[1] + 4 - c) % 4
        blocks.append((c, 2, jnp.where(turn < 2, p3[turn % 2], p4[turn % 2])))
    normed_rows(me_ref, blocks, down_ref, gain_ref, held, rows_hbm, rank_ref, sems)


def run_rows(kernel, me, pieces, down, gain, before, name):
    share, width = pieces[0].shape[1:]
    length = 16 * share
    rank = down.shape[0]
    count = sum(p.shape[0] for p in pieces)
    any_space = pl.BlockSpec(memory_space=pl.ANY)
    args = (*pieces, down, gain, *before)
    return pl.pallas_call(
        kernel,
        grid_spec=pltpu.PrefetchScalarGridSpec(
            num_scalar_prefetch=1,
            grid=(1,),
            in_specs=[*[one(a) for a in (*pieces, down, gain)], *([any_space, one(before[1])] if before else [])],
            out_specs=[any_space, kept(length, rank)],
            scratch_shapes=[pltpu.VMEM((count, share, width), BF), pltpu.SemaphoreType.DMA((count,))],
        ),
        out_shape=[jax.ShapeDtypeStruct((length, width), BF), jax.ShapeDtypeStruct((length, rank), BF)],
        input_output_aliases={len(args) - 1: 0} if before else {},
        compiler_params=params(),
        cost_estimate=takes(3),
        name=name,
    )(me, *args)


def pull_back(
    me_ref, p0, p1, p2, p3, up_ref, w_ref, g2_ref, part_ref, down_ref,
    dn_ref, stats_ref, cot_hbm, low_t_ref,
    cot, low, dots, sem, piece_sems,
):
    step = pl.program_id(0)
    copy_cot = pltpu.make_async_copy(cot, cot_hbm, sem)

    @pl.when(step == 0)
    def _():
        chunks, share, _ = p0.shape
        copies = []
        for c in range(chunks):
            for d, part in enumerate((p0, p1, p2, p3)):
                at = pl.multiple_of((c * 4 + (me_ref[0] + 4 - d) % 4) * share, share)
                source = part.at[(me_ref[1] + 4 - c) % 4]
                copies.append(pltpu.make_async_copy(source, cot.at[pl.ds(at, share), :], piece_sems.at[c * 4 + d]))
                copies[-1].start()
        for copy in copies:
            copy.wait()
        copy_cot.start()
        low_products(cot, up_ref, low, low_t_ref)
        dots[...] = jnp.zeros_like(dots)

    dn = dot_nn(cot[...], w_ref[...]) + dot_nn(low[...], down_ref[...])
    dn_ref[...] = dn.astype(BF)
    both = dn * g2_ref[...].astype(F32)
    total = dots[...]
    for k in range(both.shape[1] // SUB):
        total = total + both[:, k * SUB : (k + 1) * SUB]
    dots[...] = total

    @pl.when(step == pl.num_programs(0) - 1)
    def _():
        first = lane((8, stats_ref.shape[1]), 0) == 0
        top = jnp.where(first, part_ref[0:8, :], lane_rows(dots[...]))
        stats_ref[...] = jnp.concatenate([top, part_ref[8:, :]], 0).astype(BF)
        copy_cot.wait()


def run_pull_back(me, pieces, weights, up, g2, part, down, tile=384):
    width = pieces[0].shape[2]
    length, inner = g2.shape
    rank = down.shape[0]
    first = (weights.shape[1] - inner) // tile
    return pl.pallas_call(
        pull_back,
        grid_spec=pltpu.PrefetchScalarGridSpec(
            num_scalar_prefetch=1,
            grid=(inner // tile,),
            in_specs=[
                *[pl.BlockSpec(memory_space=pl.ANY)] * len(pieces), one(up),
                pl.BlockSpec((width, tile), lambda j, me: (0, first + j)),
                pl.BlockSpec((length, tile), lambda j, me: (0, j)),
                one(part),
                pl.BlockSpec((rank, tile), lambda j, me: (0, j)),
            ],
            out_specs=[
                pl.BlockSpec((length, tile), lambda j, me: (0, j)), kept(*part.shape),
                pl.BlockSpec(memory_space=pl.ANY), kept(rank, length),
            ],
            scratch_shapes=[
                pltpu.VMEM((length, width), BF),
                pltpu.VMEM((length, rank), BF),
                pltpu.VMEM((length, SUB), F32),
                pltpu.SemaphoreType.DMA,
                pltpu.SemaphoreType.DMA((4 * pieces[0].shape[0],)),
            ],
        ),
        out_shape=[
            jax.ShapeDtypeStruct((length, inner), BF),
            jax.ShapeDtypeStruct(part.shape, BF),
            jax.ShapeDtypeStruct((length, width), BF),
            jax.ShapeDtypeStruct((rank, length), BF),
        ],
        compiler_params=params(),
        cost_estimate=takes(8),
        name="pull_back",
    )(me, *pieces, up, weights, g2, part, down)


def dealt(rows, width, tile, at):
    spec = pl.BlockSpec((rows, tile), lambda j, me: (0, at(j)))
    return [spec] * 4, [jax.ShapeDtypeStruct((rows, width), BF)] * 4


def run_backward(
    me, half, gx, dt, run, run_rows, xc, bc, slope, y, dn, states, stats, marks, taps, par, skip, gain, pick,
    weights, down, up, rank_t, lam, edge, cot=None, g2=None, low_t=None, chosen=None,
):
    length = gx.shape[0] // 2
    inner, chans, width = skip.shape[1], taps.shape[1], weights.shape[0]
    rank = down.shape[0]
    up_block = pl.BlockSpec((rank, 2 * inner), lambda i, me: (0, 0), pipeline_mode=pl.Buffered(1))
    steps = length // SUB
    tile = 512
    assert tile == length
    top = (half + 1) * steps - 1
    sub = lambda i: jnp.maximum(top - i, half * steps)
    col = lambda i: jnp.maximum(i - steps, 0)
    row = lambda cols, at=0: pl.BlockSpec((SUB, cols), lambda i, me, at=at: (sub(i), at))
    lanes = lambda n: pl.BlockSpec((n, SUB), lambda i, me: (0, sub(i)))
    total = inner + chans + SUB
    specs, shapes = dealt(length // 4 + rank, width, tile, col)
    with_grads = cot is not None
    args = [
        gx, gx, dt, run, run_rows, xc, bc, slope, y, dn, states, *stats, marks, taps, par, skip, gain, pick, lam, edge,
        weights, down, up, rank_t,
    ]
    in_specs = [
        row(inner), row(SUB, (inner + chans) // SUB), row(SUB), row(SUB), pl.BlockSpec((16, SUB), lambda i, me: (sub(i), 0)),
        row(inner), row(2 * SUB), row(chans), row(inner), row(inner),
        pl.BlockSpec((1, SUB, inner), lambda i, me: (sub(i), 0, 0)),
        *[lanes(stats[0].shape[0])] * 4,
        row(marks.shape[1]), one(taps), one(par), one(skip), one(gain), one(pick), one(lam), one(edge),
        pl.BlockSpec(memory_space=pl.ANY),
        pl.BlockSpec((rank, tile), lambda i, me: (0, col(i))),
        up_block, lanes(rank),
    ]
    out_specs = [*specs, kept(*lam.shape), kept(*edge.shape), kept(rank, 2 * inner)]
    out_shape = [
        *shapes,
        jax.ShapeDtypeStruct(lam.shape, F32),
        jax.ShapeDtypeStruct(edge.shape, F32),
        jax.ShapeDtypeStruct((rank, 2 * inner), F32),
    ]
    scratch = [
        pltpu.VMEM((length, total), BF),
        pltpu.VMEM((length, rank), BF),
        pltpu.VMEM((rank, length), BF),
        pltpu.VMEM((length, tile), BF),
        pltpu.VMEM((SUB + 8, chans), F32),
        pltpu.VMEM((length, inner), F32),
        pltpu.VMEM((length, inner), F32),
        pltpu.VMEM((steps * 8, inner), F32),
        pltpu.VMEM((length, SUB), F32),
        pltpu.VMEM((width // tile, tile, total), BF),
        pltpu.SemaphoreType.DMA((width // tile,)),
    ]
    if with_grads:
        other = lambda i: sub(i) - steps
        args += [cot, g2, low_t, cot, g2, low_t, *stats, chosen]
        in_specs += [row(width), row(inner), lanes(rank)]
        in_specs += [
            pl.BlockSpec((SUB, width), lambda i, me: (other(i), 0)),
            pl.BlockSpec((SUB, inner), lambda i, me: (other(i), 0)),
            pl.BlockSpec((rank, SUB), lambda i, me: (0, other(i))),
            *[pl.BlockSpec((stats[0].shape[0], SUB), lambda i, me: (0, other(i)))] * 4,
            one(chosen),
        ]
        out_specs.append(kept(rank, inner + width + SUB))
        out_shape.append(jax.ShapeDtypeStruct((rank, inner + width + SUB), BF))
        scratch = [pltpu.VMEM((rank, inner + width), F32), *scratch]
    return pl.pallas_call(
        functools.partial(backward_half, with_grads=with_grads),
        grid_spec=pltpu.PrefetchScalarGridSpec(
            num_scalar_prefetch=1,
            grid=(steps + width // tile,),
            in_specs=in_specs,
            out_specs=out_specs,
            scratch_shapes=scratch,
        ),
        out_shape=out_shape,
        compiler_params=params(),
        cost_estimate=takes(19),
        name="backward_half",
    )(me, *args)


def place(me_ref, pieces, out):
    own, behind, ahead, far_low, far_high = pieces
    share = own.shape[1]
    y, turn = me_ref[0], (me_ref[1] + 4 - pl.program_id(0)) % 4
    for d, part in ((0, own), (1, behind), (3, ahead)):
        out[pl.ds(pl.multiple_of(((y + 4 - d) % 4) * share, share), share), :] = part[0]
    far = pl.ds(pl.multiple_of(((y + 2) % 4) * share, share), share)

    @pl.when(turn < 2)
    def _():
        out[far, :] = far_low[0]

    @pl.when(turn >= 2)
    def _():
        out[far, :] = far_high[0]


def columns_of(stats_refs, cols):
    total = summed(stats_refs)
    rows, length = total.shape
    total = jnp.concatenate([total, jnp.zeros((SUB - rows, length), F32)], 0)
    for k in range(length // SUB):
        cols[k * SUB : (k + 1) * SUB, :] = total[:, k * SUB : (k + 1) * SUB].T
    return total


def finish_branch(me_ref, sum_ref, s0, s1, s2, s3, up_ref, o0, o1, o2, o3, cols):
    columns_of((s0, s1, s2, s3), cols)
    share = o0.shape[0]
    rank = up_ref.shape[0]
    for d, out in enumerate((o0, o1, o2, o3)):
        c = (me_ref[1] + d) % 4
        mine = cols[pl.ds(pl.multiple_of((c * 4 + me_ref[0]) * share, share), share), :]
        rn = lax.rsqrt(mine[:, 0:1] / INNER_CHANNELS + EPS_NORM)
        low = (mine[:, 8 : 8 + rank] * rn).astype(BF)
        total = sum_ref[pl.ds(pl.multiple_of(c * share, share), share), :].astype(F32)
        out[...] = (total * rn + dot_nn(low, up_ref[...])).astype(BF)


def run_to_context(kernel, me, args, share, width, scratch, name):
    return pl.pallas_call(
        kernel,
        grid_spec=pltpu.PrefetchScalarGridSpec(
            num_scalar_prefetch=1,
            grid=(1,),
            in_specs=[one(a) for a in args],
            out_specs=[kept(share, width)] * 4,
            scratch_shapes=[scratch],
        ),
        out_shape=[jax.ShapeDtypeStruct((share, width), BF)] * 4,
        compiler_params=params(),
        cost_estimate=takes(3),
        name=name,
    )(me, *args)


def in_grads(me_ref, adapters_ref, *refs):
    early, late, (up0_ref, up1_ref, normed_ref), outs, (sent_ref, held) = (
        refs[:4], refs[4:8], refs[8:11], refs[11:15], refs[15:]
    )
    half = held.shape[0] // 2
    rank, length = up0_ref.shape[0], normed_ref.shape[0]
    added = lambda refs, *at: sum(r[at].astype(F32) for r in refs[1:]) + refs[0][at].astype(F32)
    for at, parts in ((0, early), (half, late)):
        held[at : at + half, :] = added(parts, slice(0, half)).astype(BF)
    share = outs[0].shape[0]
    for d, out in enumerate(outs):
        c = (me_ref[1] + d) % 4
        out[...] = held[pl.ds(pl.multiple_of(c * share, share), share), :]
    ranks = [added(parts, slice(half, half + rank), slice(0, length // 2)) for parts in (early, late)]
    width, inner2 = normed_ref.shape[1], up0_ref.shape[1]
    sent_ref[:, 0:width] = dot_nn(jnp.concatenate(ranks, 1).astype(BF), normed_ref[...]).astype(BF)
    sent_ref[:, width : width + inner2] = (up0_ref[...] + up1_ref[...]).astype(BF)
    sent_ref[:, width + inner2 :] = (lane((rank, SUB), 1) == adapters_ref[me_ref[1]]).astype(BF)


def run_in_grads(me, adapters, early, late, up0, up1, normed, share):
    rank, inner2 = up0.shape
    width = normed.shape[1]
    columns = width + inner2 + SUB
    args = (*early, *late, up0, up1, normed)
    return pl.pallas_call(
        in_grads,
        grid_spec=pltpu.PrefetchScalarGridSpec(
            num_scalar_prefetch=2,
            grid=(1,),
            in_specs=[one(a) for a in args],
            out_specs=[*[kept(share, width)] * 4, kept(rank, columns)],
            scratch_shapes=[pltpu.VMEM((4 * share, width), BF)],
        ),
        out_shape=[*[jax.ShapeDtypeStruct((share, width), BF)] * 4, jax.ShapeDtypeStruct((rank, columns), BF)],
        compiler_params=params(),
        cost_estimate=takes(3),
        name="in_grads",
    )(me, adapters, *args)


def finish_out(me_ref, p0, p1, p2, p3, p4, tokens_ref, out_ref, held):
    place(me_ref, (p0, p1, p2, p3, p4), held)
    for k in range(held.shape[0] // 16):
        here = slice(k * 16, (k + 1) * 16)
        out_ref[0, here, :] = (tokens_ref[0, here, :].astype(F32) + held[here, :].astype(F32)).astype(BF)


def finish_grad(me_ref, p0, p1, p2, p3, p4, tokens_ref, cot_ref, gain_ref, out_ref, held):
    place(me_ref, (p0, p1, p2, p3, p4), held)
    for k in range(held.shape[0] // 16):
        here = slice(k * 16, (k + 1) * 16)
        t = tokens_ref[0, here, :].astype(F32)
        rms = lax.rsqrt(jnp.mean(t * t, -1, keepdims=True) + EPS_NORM)
        pulled = held[here, :].astype(F32) * gain_ref[...]
        slope = rms * rms * rms * jnp.mean(pulled * t, -1, keepdims=True)
        out_ref[0, here, :] = rms * pulled - t * slope + cot_ref[0, here, :].astype(F32)


def piece_specs(pieces):
    share, width = pieces[0].shape[1:]
    half = pieces[0].shape[0] // 2
    turn = lambda s, me: (me[1] + 4 - s) % 4
    full = pl.BlockSpec((1, share, width), lambda s, me: (turn(s, me), 0, 0))
    return [
        full, full, full,
        pl.BlockSpec((1, share, width), lambda s, me: (jnp.minimum(turn(s, me), half - 1), 0, 0)),
        pl.BlockSpec((1, share, width), lambda s, me: (jnp.maximum(turn(s, me) - half, 0), 0, 0)),
    ]


def run_finish(kernel, me, pieces, extra, dtype, name):
    seqs, block, width = extra[0].shape
    seq = pl.BlockSpec((1, block, width), lambda s, me: (s, 0, 0))
    specs = [seq if a.ndim == 3 else whole(a) for a in extra]
    return pl.pallas_call(
        kernel,
        grid_spec=pltpu.PrefetchScalarGridSpec(
            num_scalar_prefetch=1,
            grid=(seqs,),
            in_specs=[*piece_specs(pieces), *specs],
            out_specs=seq,
            scratch_shapes=[pltpu.VMEM((block, width), BF)],
        ),
        out_shape=jax.ShapeDtypeStruct((seqs, block, width), dtype),
        compiler_params=params(30),
        cost_estimate=takes(5),
        name=name,
    )(me, *[pltpu.with_memory_space_constraint(a, pltpu.HBM) if a.ndim == 3 else a for a in (*pieces, *extra)])


def fill_tables(all_ref, *outs):
    table, rank = outs[0].shape[0], outs[0].shape[1]
    rows, columns = all_ref.shape
    spread = (lane((SUB, table * rank), 0) == lane((SUB, table * rank), 1) // rank).astype(BF)
    place = dot_nn(all_ref[:, columns - SUB :], spread)
    same = lane((rows, table * rank), 0) % rank == lane((rows, table * rank), 1) % rank
    place = jnp.where(same, place, 0.0).T.astype(BF)
    at = 0
    for out in outs:
        slots = out.shape[2:-1] or (1,)
        for slot in range(slots[0]):
            here = dot_nn(place, all_ref[:, at : at + out.shape[-1]])
            for a in range(table):
                if out.ndim == 3:
                    out[a] = here[a * rank : (a + 1) * rank, :]
                else:
                    out[a, :, slot, :] = here[a * rank : (a + 1) * rank, :]
            at += out.shape[-1]


def run_tables(everything, table, rank, widths):
    return pl.pallas_call(
        fill_tables,
        out_shape=[jax.ShapeDtypeStruct((table, rank, *w), F32) for w in widths],
        compiler_params=params(),
        cost_estimate=takes(3),
        name="fill_tables",
    )(everything)


def shifted_by(value, axis, distance):
    size = lax.axis_size(axis)
    return lax.ppermute(value, axis, [(i, (i + distance) % size) for i in range(size)])


def tie(*values):
    return lax.optimization_barrier(values)


def ring_near(own, axis):
    return shifted_by(own, axis, 1), shifted_by(own, axis, -1)


def ring_far(near, axis):
    half = near[0].shape[0] // 2
    return shifted_by(near[0][:half], axis, 1), shifted_by(near[1][half:], axis, -1)


def delivered(pieces, axis):
    return [pieces[0]] + [shifted_by(p, axis, d) for d, p in enumerate(pieces) if d]


def added(parts):
    return sum(p.astype(F32) for p in parts[1:]) + parts[0].astype(F32)


def shared(value, axis):
    return [value] + [shifted_by(value, axis, d) for d in range(1, lax.axis_size(axis))]


def swapped(value, axis):
    return lax.all_to_all(value, axis, 0, 0, tiled=True)


def per_device(
    tokens, output_cotangent, segments, sequence_adapter, input_norm_gain,
    gate_x_projection_weight, bc_projection_weight, step_projection_weight,
    x_convolution_taps, x_convolution_bias, bc_convolution_taps, bc_convolution_bias,
    step_size_bias, log_decay_rate, head_skip_gain, gated_norm_gain, output_projection_weight,
    in_adapter_down, in_adapter_up, out_adapter_down, out_adapter_up,
):
    seqs, block, width = tokens.shape
    inner = gate_x_projection_weight.shape[2]
    heads = step_projection_weight.shape[1]
    rank = in_adapter_down.shape[2]
    ny, nz = lax.axis_size("tensor"), lax.axis_size("context")
    my, mz = lax.axis_index("tensor"), lax.axis_index("context")
    me = jnp.stack([my, mz]).astype(jnp.int32)
    length = block * nz
    share = block // ny

    rows = gate_x_projection_weight.shape[0]
    packed = jnp.concatenate(
        [
            gate_x_projection_weight.reshape(rows, 2 * inner),
            bc_projection_weight,
            step_projection_weight,
            jnp.zeros((rows, SUB - heads), BF),
            output_projection_weight.T,
        ],
        1,
    )
    full = lax.all_gather(packed, ("fsdp", "context"), axis=0, tiled=True)

    quarters = lambda a: [
        lax.dynamic_slice(a, ((mz + d) % nz, my * share, 0), (1, share, width)) for d in range(nz)
    ]
    tokens_s, cot_later, segments = tie(delivered(quarters(tokens), "context"), output_cotangent, segments)
    tokens_near = ring_near(jnp.concatenate(tokens_s, 0), "tensor")
    tokens_s = jnp.concatenate(tokens_s, 0)
    to_lanes = lambda a: jnp.pad(a, (0, SUB - heads))
    vec = jnp.concatenate(
        [
            x_convolution_bias, bc_convolution_bias, gated_norm_gain, input_norm_gain,
            to_lanes(step_size_bias), to_lanes(log_decay_rate), to_lanes(head_skip_gain),
        ]
    )[None]
    marks, taps, conv_bias, par, skip, gain, norm_gain, down_in, up_in, down_out, up_out = run_prepare(
        me, sequence_adapter, swapped(segments, "context").reshape(nz, block), vec, x_convolution_taps, bc_convolution_taps,
        in_adapter_down.transpose(0, 2, 1), in_adapter_up, out_adapter_down.transpose(0, 2, 1), out_adapter_up, width,
    )
    chosen = jnp.full((1, SUB), lax.dynamic_index_in_dim(sequence_adapter, mz, 0, False).astype(F32))
    pick = (jnp.arange(inner)[:, None] // (inner // heads) == jnp.arange(SUB)[None, :]).astype(BF)
    lam, edge = jnp.zeros((SUB, inner), F32), jnp.zeros((8, taps.shape[1]), F32)

    tokens_near, marks, cot_s = tie(tokens_near, marks, delivered(quarters(cot_later), "context"))
    normed, low_rank = run_rows(near_rows, me, (tokens_s, *tokens_near), down_in, norm_gain, (), "near_rows")
    tokens_far, cot_s, normed = tie(ring_far(tokens_near, "tensor"), jnp.concatenate(cot_s, 0), normed)
    cot_parts = shared(cot_s, "tensor")
    normed, low_rank = run_rows(far_rows, me, tokens_far, down_in, norm_gain, (normed, low_rank), "far_rows")
    gx, rank_t, part, dt, run, run_turned, y, xc, bc, slope, g2, states, out_all = run_forward(
        normed, low_rank, up_in, full, down_out, marks, taps, conv_bias, par, skip, gain
    )
    g2, cot_parts = tie(g2, cot_parts)
    dn, stats, cot, d_low_t = run_pull_back(me, cot_parts, full, up_out, g2, part, down_out)
    out_all, stats = tie(out_all, stats)
    out_sum = lax.psum_scatter(out_all.reshape(length, width), "tensor", scatter_dimension=0, tiled=True)
    stats_all = shared(stats, "tensor")

    backward = lambda half, *carried, **more: run_backward(
        me, half, gx, dt, run, run_turned, xc, bc, slope, y, dn, states, stats_all, marks, taps, par, skip, gain, pick,
        full, down_in, up_in, rank_t, *carried, **more,
    )
    *late, lam, edge, late_up, sent = backward(1, lam, edge, cot=cot, g2=g2, low_t=d_low_t, chosen=chosen)
    sent_out = lax.all_gather(sent, ("fsdp", "context"), axis=0, tiled=True)
    lam, late = tie(lam, late)
    late_parts = delivered(late, "tensor")
    *early, _, _, early_up = backward(0, lam, edge)
    early, late_parts, out_sum = tie(early, late_parts, out_sum)
    early_parts = delivered(early, "tensor")
    scratch = pltpu.VMEM((length, SUB), F32)
    branch = run_to_context(finish_branch, me, (out_sum, *stats_all, up_out), share, width, scratch, "finish_branch")
    branch_parts = delivered(branch, "context")
    early_parts, branch_parts = tie(early_parts, branch_parts)
    branch_q = jnp.stack(branch_parts)
    out_near = ring_near(branch_q, "tensor")
    *d_in, sent = run_in_grads(
        me, sequence_adapter, early_parts, late_parts, early_up, late_up, normed, share
    )
    sent_all = lax.all_gather(sent, ("fsdp", "context"), axis=0, tiled=True)
    d_in_parts = delivered(d_in, "context")
    d_in_parts, out_near, sent = tie(d_in_parts, out_near, sent)
    d_in_q = jnp.stack(d_in_parts)
    d_in_near = ring_near(d_in_q, "tensor")
    out_far = ring_far(out_near, "tensor")
    table = in_adapter_down.shape[0]
    out_tables = run_tables(sent_out, table, rank, ((inner,), (width,)))
    d_in_near, out_far, out_tables = tie(d_in_near, out_far, out_tables)
    d_in_far = ring_far(d_in_near, "tensor")
    layer_out = run_finish(finish_out, me, (branch_q, *out_near, *out_far), (tokens,), BF, "finish_out")
    layer_out, d_in_far = tie(layer_out, d_in_far)
    grad_tokens = run_finish(
        finish_grad, me, (d_in_q, *d_in_near, *d_in_far), (tokens, output_cotangent, norm_gain), F32, "finish_grad"
    )
    in_tables = run_tables(sent_all, table, rank, ((width,), (2, inner)))
    return (
        layer_out,
        grad_tokens,
        in_tables[0].transpose(0, 2, 1),
        in_tables[1],
        out_tables[0].transpose(0, 2, 1),
        out_tables[1],
    )


def solution(mesh):
    placed = (
        P("fsdp", "context", None),
        P("fsdp", "context", None),
        P("fsdp", "context"),
        P("fsdp"),
        P(),
        P(("fsdp", "context"), None, "tensor"),
        P(("fsdp", "context"), None),
        P(("fsdp", "context"), "tensor"),
        P(None, "tensor"),
        P("tensor"),
        P(),
        P(),
        P("tensor"),
        P("tensor"),
        P("tensor"),
        P("tensor"),
        P("tensor", ("fsdp", "context")),
        P(),
        P(None, None, None, "tensor"),
        P(None, "tensor", None),
        P(),
    )
    return jax.shard_map(
        per_device,
        mesh=mesh,
        in_specs=placed,
        out_specs=(
            P("fsdp", "context", None),
            P("fsdp", "context", None),
            P(),
            P(None, None, None, "tensor"),
            P(None, "tensor", None),
            P(),
        ),
        check_vma=False,
    )
```
